32 devices in a mesh: dp: 8 (over z, x), seq: 4 (over y, core).
Axes of the slice: x: 2, y: 2, z: 4, core: 2. Of those that a mesh axis runs over, the one named last changes fastest.
Arguments:
- captions: bfloat16 [96, 128, 768], P(('dp', 'seq')), may hold values from -6 to 6
- images: bfloat16 [96, 196, 768], P('dp'), may hold values from -6 to 6
- tissue_mask: int32 [96, 196], P('dp'), may hold values from 0 to 1, as said below
- gain_self: bfloat16 [768], P(('dp', 'seq')), may hold values from 0.5 to 1.5
- gain_cross: bfloat16 [768], P(('dp', 'seq')), may hold values from 0.5 to 1.5
- gain_mlp: bfloat16 [768], P(('dp', 'seq')), may hold values from 0.5 to 1.5
- w_qkv: bfloat16 [768, 2304], P(('dp', 'seq')), may hold values from -0.21875 to 0.21875
- w_self_out: bfloat16 [768, 768], P(('dp', 'seq')), may hold values from -0.625 to 0.625
- w_cross_q: bfloat16 [768, 768], P(('dp', 'seq')), may hold values from -0.21875 to 0.21875
- w_cross_kv: bfloat16 [768, 1536], P(('dp', 'seq')), may hold values from -0.21875 to 0.21875
- w_cross_out: bfloat16 [768, 768], P(('dp', 'seq')), may hold values from -0.625 to 0.625
- w_up: bfloat16 [768, 3072], P(('dp', 'seq')), may hold values from -0.21875 to 0.21875
- w_down: bfloat16 [3072, 768], P(('dp', 'seq')), may hold values from -0.109375 to 0.109375
- cotangent: bfloat16 [96, 128, 768], P(('dp', 'seq')), may hold values from -6 to 6
Outputs:
- block_out: bfloat16 [96, 128, 768], P(('dp', 'seq'))
- grad_captions: float32 [96, 128, 768], P(('dp', 'seq'))
- grad_images: float32 [96, 196, 768], P('dp', None, 'seq')
- grad_gain_self: float32 [768], P(('dp', 'seq'))
- grad_gain_cross: float32 [768], P(('dp', 'seq'))
- grad_gain_mlp: float32 [768], P(('dp', 'seq'))
- grad_w_qkv: float32 [768, 2304], P(('dp', 'seq'))
- grad_w_self_out: float32 [768, 768], P(('dp', 'seq'))
- grad_w_cross_q: float32 [768, 768], P(('dp', 'seq'))
- grad_w_cross_kv: float32 [768, 1536], P(('dp', 'seq'))
- grad_w_cross_out: float32 [768, 768], P(('dp', 'seq'))
- grad_w_up: float32 [768, 3072], P(('dp', 'seq'))
- grad_w_down: float32 [3072, 768], P(('dp', 'seq'))
The draws below stay inside these ranges and needn't reach their ends.
Inputs may be any that keep to these rules, and one draw needn't show every extreme that they name: `tissue_mask`: at least 65 of every image's patches are valid; the valid ones lie anywhere among its 196 slots and their number differs from image to image.
All inputs are finite; a program needn't handle non-finite values.
Results may differ from the reference program's by a relative error of at most 0.019.
Values may be sent and summed in bfloat16 or wider, within the bound.
A program may use at most 192 MiB of HBM per device.

```python
import jax
import jax.numpy as jnp
from jax import lax

D = 768
HEADS = 12
HEAD = 64
FF = 3072
LEN = 128
PATCHES = 196
CAPS_DEV = 12
CAPTIONS = 96
N_DP = 8


def draw_tissue_mask(key, part):
    count_key = jax.random.fold_in(key, 11)
    order_key = jax.random.fold_in(key, 12)
    valid_counts = jax.random.randint(count_key, (CAPTIONS, 1), PATCHES // 3, PATCHES + 1)
    order_scores = jax.random.randint(order_key, (CAPTIONS, PATCHES), 0, 1 << 20) * PATCHES + jnp.arange(PATCHES)[None, :]
    rank_table = jnp.argsort(jnp.argsort(order_scores, axis=-1, stable=True), axis=-1, stable=True)
    return (rank_table < valid_counts).astype(jnp.int32)


def block_levels(key, extent, cuts, low, high):
    loudness, own = 1.0, jax.random.fold_in(key, 6)
    for dim, blocks in cuts:
        heights = jnp.exp(jax.random.uniform(jax.random.fold_in(own, dim), (blocks,), jnp.float32, low / len(cuts), high / len(cuts)))
        loudness = loudness * jnp.repeat(heights, extent[dim] // blocks).reshape([-1 if axis == dim else 1 for axis in range(len(extent))])
    return loudness


def centred(rng, dims, deviation, limit, pieces=(), kind=jnp.bfloat16):
    entries = deviation * jax.random.normal(rng, dims, jnp.float32)
    if pieces:
        entries = entries * block_levels(rng, dims, pieces, -0.22, 0.18)
    return jnp.clip(entries, -limit, limit).astype(kind)


def setup_inputs(seed: int = 0) -> dict:
    splits = jax.random.split(jax.random.key(seed), 15)
    captions = centred(splits[0], (CAPTIONS, LEN, D), 1.0, 6.0, ((0, 32),))
    images = centred(splits[1], (CAPTIONS, PATCHES, D), 1.0, 6.0, ((0, 8),))
    tissue_mask = draw_tissue_mask(jax.random.fold_in(splits[14], 71), 0)
    gain_self = jnp.clip(1.0 + 0.1 * jax.random.normal(splits[3], (D,), jnp.float32), 0.5, 1.5).astype(jnp.bfloat16)
    gain_cross = jnp.clip(1.0 + 0.1 * jax.random.normal(splits[4], (D,), jnp.float32), 0.5, 1.5).astype(jnp.bfloat16)
    gain_mlp = jnp.clip(1.0 + 0.1 * jax.random.normal(splits[5], (D,), jnp.float32), 0.5, 1.5).astype(jnp.bfloat16)
    w_qkv = centred(splits[6], (D, 3 * D), D ** -0.5, 0.21875, ((0, 32),))
    w_self_out = centred(splits[7], (D, D), (D // 8) ** -0.5, 0.625, ((0, 32),))
    w_cross_q = centred(splits[8], (D, D), D ** -0.5, 0.21875, ((0, 32),))
    w_cross_kv = centred(splits[9], (D, 2 * D), D ** -0.5, 0.21875, ((0, 32),))
    w_cross_out = centred(splits[10], (D, D), (D // 8) ** -0.5, 0.625, ((0, 32),))
    w_up = centred(splits[11], (D, FF), D ** -0.5, 0.21875, ((0, 32),))
    w_down = centred(splits[12], (FF, D), FF ** -0.5, 0.109375, ((0, 32),))
    cotangent = centred(splits[13], (CAPTIONS, LEN, D), 1.0, 6.0, ((0, 32),))
    return dict(captions=captions, images=images, tissue_mask=tissue_mask, gain_self=gain_self, gain_cross=gain_cross, gain_mlp=gain_mlp, w_qkv=w_qkv, w_self_out=w_self_out, w_cross_q=w_cross_q, w_cross_kv=w_cross_kv, w_cross_out=w_cross_out, w_up=w_up, w_down=w_down, cotangent=cotangent)


@jax.custom_vjp
def low(v):
    return lax.optimization_barrier(v.astype(jnp.bfloat16)).astype(jnp.float32)

@jax.custom_vjp
def low_back(v):
    return v

def low_keep(v):
    return (low(v), None)

def low_pass(kept, grad):
    return (grad,)

def back_keep(v):
    return (v, None)

def back_low(kept, grad):
    return (low(grad),)
low.defvjp(low_keep, low_pass)
low_back.defvjp(back_keep, back_low)
epsilon = 1e-05
highest = lax.Precision.HIGHEST

def layer_norm(inputs, gain_vector):
    centered = inputs - lax.optimization_barrier(jnp.mean(inputs, axis=-1, keepdims=True))
    spread = lax.optimization_barrier(jnp.mean(centered * centered, axis=-1, keepdims=True))
    return centered * lax.rsqrt(spread + epsilon) * gain_vector

def project(inputs, matrix):
    return jnp.einsum('btd,de->bte', inputs, matrix, precision=highest)

def attend(query_heads, key_heads, value_heads, allowed):
    factor = HEAD ** (-0.5)
    scores = low_back(jnp.einsum('bqhe,bkhe->bhqk', query_heads, key_heads, precision=highest)) * factor
    scores = jnp.where(allowed, scores, -1e+30)
    shifted = scores - lax.optimization_barrier(jnp.max(scores, axis=-1, keepdims=True))
    exponent = jnp.exp(shifted)
    probabilities = exponent / lax.optimization_barrier(jnp.sum(exponent, axis=-1, keepdims=True))
    return jnp.einsum('bhqk,bkhe->bqhe', low(probabilities), value_heads, precision=highest)

def decoder_block(tokens, image_rows, allowed_keys, params):
    gain_one, gain_two, gain_three, m_qkv, m_self_out, m_cross_q, m_cross_kv, m_cross_out, m_up, m_down = params
    count_rows, length, model_width = tokens.shape
    normed = low(layer_norm(tokens, gain_one))
    packed = low_back(low(project(normed, m_qkv)))
    query_heads = packed[..., :model_width].reshape(count_rows, length, HEADS, HEAD)
    key_heads = packed[..., model_width:2 * model_width].reshape(count_rows, length, HEADS, HEAD)
    value_heads = packed[..., 2 * model_width:].reshape(count_rows, length, HEADS, HEAD)
    position = jnp.arange(length)
    causal = (position[:, None] >= position[None, :])[None, None]
    attended = low_back(low(attend(query_heads, key_heads, value_heads, causal))).reshape(count_rows, length, model_width)
    after_self = tokens + low_back(project(attended, m_self_out))
    normed_two = low(layer_norm(after_self, gain_two))
    cross_queries = low_back(low(project(normed_two, m_cross_q))).reshape(count_rows, length, HEADS, HEAD)
    image_pairs = low_back(low(project(image_rows, m_cross_kv)))
    cross_keys = image_pairs[..., :model_width].reshape(count_rows, PATCHES, HEADS, HEAD)
    cross_values = image_pairs[..., model_width:].reshape(count_rows, PATCHES, HEADS, HEAD)
    cross_mixed = low_back(low(attend(cross_queries, cross_keys, cross_values, allowed_keys[:, None, None, :])))
    cross_mixed = cross_mixed.reshape(count_rows, length, model_width)
    after_cross = after_self + low_back(project(cross_mixed, m_cross_out))
    normed_three = low(layer_norm(after_cross, gain_three))
    hidden = low_back(project(normed_three, m_up))
    active = low(jax.nn.gelu(hidden, approximate=False))
    return after_cross + low_back(project(active, m_down))

def reference(captions, images, tissue_mask, gain_self, gain_cross, gain_mlp, w_qkv, w_self_out, w_cross_q, w_cross_kv, w_cross_out, w_up, w_down, cotangent):
    params = tuple((weight_arg.astype(jnp.float32) for weight_arg in (gain_self, gain_cross, gain_mlp, w_qkv, w_self_out, w_cross_q, w_cross_kv, w_cross_out, w_up, w_down)))
    allowed = tissue_mask > 0
    allowed_grouped = allowed.reshape(N_DP, CAPS_DEV, PATCHES)

    def forward(tokens, image_rows, weight_set):
        tokens_grouped = tokens.reshape(N_DP, CAPS_DEV, LEN, D)
        images_grouped = image_rows.reshape(N_DP, CAPS_DEV, PATCHES, D)
        checked = jax.checkpoint(decoder_block)

        def one_group(triple):
            return checked(triple[0], triple[1], triple[2], weight_set)
        outputs = lax.map(one_group, (tokens_grouped, images_grouped, allowed_grouped))
        return outputs.reshape(CAPTIONS, LEN, D)
    result, pullback = jax.vjp(forward, captions.astype(jnp.float32), images.astype(jnp.float32), params)
    grad_tokens, grad_image_rows, weight_grads = pullback(cotangent.astype(jnp.float32))
    return (result.astype(jnp.bfloat16), grad_tokens, grad_image_rows, weight_grads[0], weight_grads[1], weight_grads[2], weight_grads[3], weight_grads[4], weight_grads[5], weight_grads[6], weight_grads[7], weight_grads[8], weight_grads[9])
```

```python
import jax
import jax.numpy as jnp
from jax import lax
from jax.sharding import PartitionSpec as P

HEADS = 12
HEAD = 64
EPS = 1e-05
BOTH = ("dp", "seq")
f32 = jnp.float32
bf16 = jnp.bfloat16


def norm_stats(v):
    mean = jnp.mean(v, axis=-1, keepdims=True)
    centered = v - mean
    r = lax.rsqrt(jnp.mean(centered * centered, axis=-1, keepdims=True) + EPS)
    return centered * r, r


def norm_back(xhat, r, gain, e):
    u = e * gain
    mu = jnp.mean(u, axis=-1, keepdims=True)
    mx = jnp.mean(u * xhat, axis=-1, keepdims=True)
    return r * (u - mu - xhat * mx), jnp.sum(e * xhat, axis=(0, 1))


def mm(a, b):
    return jnp.einsum("btd,de->bte", a, b, preferred_element_type=f32)


def mm_t(a, b):
    return jnp.einsum("bte,de->btd", a, b, preferred_element_type=f32)


def wgrad(a, b):
    return jnp.einsum("btd,bte->de", a, b, preferred_element_type=f32)


def split_heads(a):
    b, t, _ = a.shape
    return a.reshape(b, t, -1, HEAD)


def attend(q, k, v, allowed):
    s = jnp.einsum("bqhe,bkhe->bhqk", q, k, preferred_element_type=f32) * HEAD ** (-0.5)
    s = jnp.where(allowed, s, -1e30)
    ex = jnp.exp(s - jnp.max(s, axis=-1, keepdims=True))
    p = ex / jnp.sum(ex, axis=-1, keepdims=True)
    o = jnp.einsum("bhqk,bkhe->bqhe", p.astype(bf16), v, preferred_element_type=f32)
    return p, o.astype(bf16)


def attend_back(q, k, v, p, g):
    dp = jnp.einsum("bqhe,bkhe->bhqk", g, v, preferred_element_type=f32)
    ds = (p * (dp - jnp.sum(dp * p, axis=-1, keepdims=True)) * HEAD ** (-0.5)).astype(bf16)
    dq = jnp.einsum("bhqk,bkhe->bqhe", ds, k, preferred_element_type=f32).astype(bf16)
    dk = jnp.einsum("bhqk,bqhe->bkhe", ds, q, preferred_element_type=f32).astype(bf16)
    dv = jnp.einsum("bhqk,bqhe->bkhe", p.astype(bf16), g, preferred_element_type=f32).astype(bf16)
    return dq, dk, dv


def layer(x0, img, mask, gains, weights, cot):
    g1, g2, g3 = (g.astype(f32) for g in gains)
    w_qkv, w_so, w_cq, w_ckv, w_co, w_up, w_down = weights
    b, t, d = x0.shape
    x = x0.astype(f32)
    pos = jnp.arange(t)
    causal = (pos[:, None] >= pos[None, :])[None, None]
    allowed = (mask > 0)[:, None, None, :]
    h1, r1 = norm_stats(x)
    n1 = (h1 * g1).astype(bf16)
    qkv = mm(n1, w_qkv).astype(bf16)
    q1, k1, v1 = (split_heads(qkv[..., i * d : (i + 1) * d]) for i in range(3))
    p1, o1 = attend(q1, k1, v1, causal)
    o1 = o1.reshape(b, t, d)
    x1 = x + mm(o1, w_so)
    h2, r2 = norm_stats(x1)
    n2 = (h2 * g2).astype(bf16)
    q2 = split_heads(mm(n2, w_cq).astype(bf16))
    kv = mm(img, w_ckv).astype(bf16)
    k2, v2 = split_heads(kv[..., :d]), split_heads(kv[..., d:])
    p2, o2 = attend(q2, k2, v2, allowed)
    o2 = o2.reshape(b, t, d)
    x2 = x1 + mm(o2, w_co)
    h3, r3 = norm_stats(x2)
    n3 = (h3 * g3).astype(bf16)
    hpre = mm(n3, w_up)
    cdf = 0.5 * (1.0 + lax.erf(hpre * (0.5**0.5)))
    act = (hpre * cdf).astype(bf16)
    out = (x2 + mm(act, w_down)).astype(bf16)

    gw_down = wgrad(act, cot)
    pdf = jnp.exp(-0.5 * hpre * hpre) * (0.5 / jnp.pi) ** 0.5
    gh = (mm_t(cot, w_down) * (cdf + hpre * pdf)).astype(bf16)
    gw_up = wgrad(n3, gh)
    dx2, gg3 = norm_back(h3, r3, g3, mm_t(gh, w_up))
    gx2 = cot.astype(f32) + dx2
    gx2b = gx2.astype(bf16)
    gw_co = wgrad(o2, gx2b)
    go2 = split_heads(mm_t(gx2b, w_co).astype(bf16))
    dq2, dk2, dv2 = attend_back(q2, k2, v2, p2, go2)
    dq2 = dq2.reshape(b, t, d)
    dkv = jnp.concatenate([dk2.reshape(b, -1, d), dv2.reshape(b, -1, d)], axis=-1)
    gw_ckv = wgrad(img, dkv)
    gimg = mm_t(dkv, w_ckv).astype(bf16)
    gw_cq = wgrad(n2, dq2)
    dx1, gg2 = norm_back(h2, r2, g2, mm_t(dq2, w_cq))
    gx1 = gx2 + dx1
    gx1b = gx1.astype(bf16)
    gw_so = wgrad(o1, gx1b)
    go1 = split_heads(mm_t(gx1b, w_so).astype(bf16))
    dq1, dk1, dv1 = attend_back(q1, k1, v1, p1, go1)
    dqkv = jnp.concatenate([a.reshape(b, t, d) for a in (dq1, dk1, dv1)], axis=-1)
    gw_qkv = wgrad(n1, dqkv)
    dx0, gg1 = norm_back(h1, r1, g1, mm_t(dqkv, w_qkv))
    gx0 = gx1 + dx0
    return out, gx0, gimg, (gg1, gg2, gg3), (gw_qkv, gw_so, gw_cq, gw_ckv, gw_co, gw_up, gw_down)


def on_device(captions, images, tissue_mask, gain_self, gain_cross, gain_mlp, *rest):
    weights, cotangent = rest[:-1], rest[-1]
    count = captions.shape[0]
    start = lax.axis_index("seq") * count
    img = lax.dynamic_slice_in_dim(images, start, count, 0)
    mask = lax.dynamic_slice_in_dim(tissue_mask, start, count, 0)
    gains = jnp.stack([gain_self, gain_cross, gain_mlp], axis=1)
    gains = lax.all_gather(gains, BOTH, axis=0, tiled=True)
    gains = tuple(gains[:, i] for i in range(3))
    full = [lax.all_gather(w, BOTH, axis=0, tiled=True) for w in weights]
    out, gx0, gimg, gg, gw = layer(captions, img, mask, gains, full, cotangent)
    gimg = lax.all_to_all(gimg, "seq", split_axis=2, concat_axis=0, tiled=True).astype(f32)
    gg = lax.psum_scatter(jnp.stack(gg, axis=1), BOTH, scatter_dimension=0, tiled=True)
    shards = [
        lax.psum_scatter(g.astype(bf16), BOTH, scatter_dimension=0, tiled=True).astype(f32)
        for g in gw
    ]
    return (out, gx0, gimg, gg[:, 0], gg[:, 1], gg[:, 2], *shards)


def solution(mesh):
    tok = P(BOTH, None, None)
    vec = P(BOTH)
    mat = P(BOTH, None)
    return jax.shard_map(
        on_device,
        mesh=mesh,
        in_specs=(tok, P("dp", None, None), P("dp", None), vec, vec, vec, *([mat] * 7), tok),
        out_specs=(tok, tok, P("dp", None, "seq"), vec, vec, vec, *([mat] * 7)),
        check_vma=False,
    )
```

```python
import functools

import jax
import jax.numpy as jnp
from jax import lax
from jax.experimental import pallas as pl
from jax.experimental.pallas import tpu as pltpu
from jax.sharding import PartitionSpec as P

HEADS = 12
HEAD = 64
EPS = 1e-05
BOTH = ("dp", "seq")
f32 = jnp.float32
bf16 = jnp.bfloat16
MESH = pl.DeviceIdType.MESH
HBM = pltpu.MemorySpace.HBM
VMEM = pltpu.MemorySpace.VMEM
LANES = 128


class Place:
    def __init__(self, nz):
        dp, seq = lax.axis_index("dp"), lax.axis_index("seq")
        self.nz = nz
        self.z, self.x = dp // 2, lax.rem(dp, 2)
        self.y, self.c = seq // 2, lax.rem(seq, 2)
        c, x, y = self.c, self.x, self.y
        self.p = x + c * (y - x)
        self.s = y + c * (x - y)
        self.sib = (dp, 2 * y + (1 - c))
        self.p_xy = (x + (1 - c) * (1 - 2 * x), y + c * (1 - 2 * y))
        self.s_xy = (x + c * (1 - 2 * x), y + (1 - c) * (1 - 2 * y))
        self.ps_xy = (1 - x, 1 - y)
        self.p_dev = self.dev(self.z, self.p_xy)
        self.s_dev = self.dev(self.z, self.s_xy)
        self.z_of = [lax.rem(self.z + k, nz) for k in range(nz)]
        self.z_devs = [self.dev(self.z_of[k], (x, y)) for k in range(nz)]

    def dev(self, z, xy):
        return (2 * z + xy[0], 2 * xy[1] + self.c)

    def column(self, p, s):
        return p + self.c * (s - p), s + self.c * (p - s)

    def partners(self):
        return [*self.z_devs[1:], self.p_dev, self.s_dev, self.sib]


def enter(partners):
    barrier = pltpu.get_barrier_semaphore()
    for d in partners:
        pl.semaphore_signal(barrier, inc=1, device_id=d, device_id_type=MESH)
    pl.semaphore_wait(barrier, len(partners))


def remote(src, dst, sems, i, dev):
    return pltpu.make_async_remote_copy(
        src_ref=src, dst_ref=dst, send_sem=sems[0].at[i], recv_sem=sems[1].at[i],
        device_id=dev, device_id_type=MESH,
    )


class Gather:
    def __init__(self, here, shard, full, sems, local):
        h = here
        x, y, c = h.x, h.y, h.c
        mine = full.at[h.z, x, y, c]

        def col(xy):
            return full.at[:, xy[0], xy[1], c]

        self.own = pltpu.make_async_copy(shard, mine, local)
        nz = h.nz
        self.zs = [remote(shard, mine, sems, k - 1, h.z_devs[k]) for k in range(1, nz)]
        own, px, sx, psx = (x, y), h.p_xy, h.s_xy, h.ps_xy
        n = nz - 1
        self.p_own = remote(col(own), col(own), sems, n, h.p_dev)
        self.s_own = remote(col(own), col(own), sems, n + 1, h.s_dev)
        self.s_p = remote(col(px), col(px), sems, n + 2, h.s_dev)
        self.sibs = [
            remote(col(xy), col(xy), sems, n + 3 + i, h.sib)
            for i, xy in enumerate((own, px, sx, psx))
        ]

    @staticmethod
    def count(nz):
        return nz + 6

    def step(self, i):
        if i == 0:
            self.own.start()
            for t in self.zs:
                t.start()
        elif i == 1:
            self.own.wait()
            for t in self.zs:
                t.wait_recv()
            self.p_own.start()
            self.s_own.start()
            self.sibs[0].start()
        elif i == 2:
            self.p_own.wait_recv()
            self.s_p.start()
            self.sibs[1].start()
        elif i == 3:
            self.s_own.wait_recv()
            self.sibs[2].start()
            self.s_p.wait_recv()
            self.sibs[3].start()
        elif i == 4:
            for t in self.sibs:
                t.wait_recv()
        elif i == 5:
            for t in (*self.zs, self.p_own, self.s_own, self.s_p, *self.sibs):
                t.wait_send()


def gather_kernel(nz, n_w, *refs):
    shards, fulls = refs[:n_w], refs[n_w : 2 * n_w]
    local, ssem, rsem = refs[2 * n_w :]
    here = Place(nz)
    enter(here.partners())
    gs = [
        Gather(here, shards[i], fulls[i], (ssem.at[i], rsem.at[i]), local.at[i]) for i in range(n_w)
    ]
    for g in gs:
        g.step(0)
    for t in range(n_w + 3):
        for step in (4, 3, 2, 1):
            i = t - (step - 1)
            if 0 <= i < n_w:
                gs[i].step(step)
    for g in gs:
        g.step(5)


def gather_all(nz, shards):
    n_w = len(shards)
    count = Gather.count(nz)
    outs = [jax.ShapeDtypeStruct((nz, 2, 2, 2, *w.shape), w.dtype) for w in shards]
    return pl.pallas_call(
        functools.partial(gather_kernel, nz, n_w),
        out_shape=outs,
        in_specs=[pl.BlockSpec(memory_space=HBM)] * n_w,
        out_specs=[pl.BlockSpec(memory_space=HBM)] * n_w,
        scratch_shapes=[
            pltpu.SemaphoreType.DMA((n_w,)),
            pltpu.SemaphoreType.DMA((n_w, count)),
            pltpu.SemaphoreType.DMA((n_w, count)),
        ],
        compiler_params=pltpu.CompilerParams(collective_id=0, has_side_effects=True),
    )(*shards)


class Scatter:
    def __init__(self, here, part, bufs, out, sems, local):
        self.h, self.part, self.out = here, part, out
        self.own, self.rc, self.rs, self.rp, self.rz = bufs
        h = here
        nz = h.nz
        c = h.c
        self.load = pltpu.make_async_copy(part.at[:, :, :, c], self.own, local)
        self.core = remote(part.at[:, :, :, 1 - c], self.rc, sems, 0, h.sib)
        self.s = [
            remote(self.rc.at[:, *h.column(p, 1 - h.s)], self.rs.at[p], sems, 1 + i, h.s_dev)
            for i, p in enumerate((1 - h.p, h.p))
        ]
        self.pp = remote(self.rs.at[1 - h.p], self.rp, sems, 3, h.p_dev)
        self.zs = [
            remote(self.rp.at[h.z_of[k]], self.rz.at[k - 1], sems, 3 + k, h.z_devs[k])
            for k in range(1, nz)
        ]

    @staticmethod
    def count(nz):
        return nz + 3

    def add(self, dst, a, b):
        def body(z, _):
            dst[z] = (a[z].astype(f32) + b[z].astype(f32)).astype(bf16)
            return 0

        lax.fori_loop(0, self.h.nz, body, 0)

    def step(self, i):
        h = self.h
        if i == 0:
            self.load.start()
            self.core.start()
        elif i == 1:
            self.load.wait()
            self.core.wait_recv()
            for j, p in enumerate((1 - h.p, h.p)):
                xy = h.column(p, 1 - h.s)
                self.add(self.rc.at[:, *xy], self.rc.at[:, *xy], self.own.at[:, *xy])
                self.s[j].start()
            for p in (1 - h.p, h.p):
                xy = h.column(p, h.s)
                self.add(self.rc.at[:, *xy], self.rc.at[:, *xy], self.own.at[:, *xy])
        elif i == 2:
            xy = h.column(1 - h.p, h.s)
            self.s[0].wait_recv()
            self.add(self.rs.at[1 - h.p], self.rs.at[1 - h.p], self.rc.at[:, *xy])
            self.pp.start()
            xy = h.column(h.p, h.s)
            self.s[1].wait_recv()
            self.add(self.rs.at[h.p], self.rs.at[h.p], self.rc.at[:, *xy])
        elif i == 3:
            self.pp.wait_recv()
            self.add(self.rp, self.rp, self.rs.at[h.p])
            for t in self.zs:
                t.start()
        elif i == 4:
            for t in self.zs:
                t.wait_recv()
            total = self.rp[h.z].astype(f32)
            for k in range(h.nz - 1):
                total = total + self.rz[k].astype(f32)
            self.out[...] = total
        elif i == 5:
            for t in (self.core, *self.s, self.pp, *self.zs):
                t.wait_send()


def scatter_kernel(nz, n_w, *refs):
    parts, img = refs[:n_w], refs[n_w]
    outs, img_out = refs[n_w + 1 : 2 * n_w + 1], refs[2 * n_w + 1]
    rest = refs[2 * n_w + 2 :]
    bufs = [rest[5 * i : 5 * i + 5] for i in range(n_w)]
    local, ssem, rsem, isem, jsem = rest[5 * n_w :]
    here = Place(nz)
    dp, seq = lax.axis_index("dp"), lax.axis_index("seq")
    peers = [(dp, lax.rem(seq + k, 4)) for k in range(1, 4)]
    enter([*here.partners(), *peers])
    keep = pltpu.make_async_copy(img.at[seq], img_out.at[seq], local.at[n_w])
    keep.start()
    moves = [
        remote(img.at[lax.rem(seq + k, 4)], img_out.at[seq], (isem, jsem), k - 1, peers[k - 1])
        for k in range(1, 4)
    ]
    ss = [
        Scatter(here, parts[i], bufs[i], outs[i], (ssem.at[i], rsem.at[i]), local.at[i])
        for i in range(n_w)
    ]
    for s in ss:
        s.step(0)
    for m in moves:
        m.start()
    for t in range(n_w + 3):
        for step in (4, 3, 2, 1):
            i = t - (step - 1)
            if 0 <= i < n_w:
                ss[i].step(step)
    for s in ss:
        s.step(5)
    keep.wait()
    for m in moves:
        m.wait()


def scatter_all(nz, parts, img):
    n_w = len(parts)
    count = Scatter.count(nz)
    scratch = []
    for w in parts:
        blk = w.shape[4:]
        scratch += [
            pltpu.VMEM((nz, 2, 2, *blk), bf16),
            pltpu.VMEM((nz, 2, 2, *blk), bf16),
            pltpu.VMEM((2, nz, *blk), bf16),
            pltpu.VMEM((nz, *blk), bf16),
            pltpu.VMEM((nz - 1, *blk), bf16),
        ]
    return pl.pallas_call(
        functools.partial(scatter_kernel, nz, n_w),
        out_shape=[
            *(jax.ShapeDtypeStruct(w.shape[4:], f32) for w in parts),
            jax.ShapeDtypeStruct(img.shape, img.dtype),
        ],
        in_specs=[pl.BlockSpec(memory_space=HBM)] * (n_w + 1),
        out_specs=[*([pl.BlockSpec(memory_space=VMEM)] * n_w), pl.BlockSpec(memory_space=HBM)],
        scratch_shapes=[
            *scratch,
            pltpu.SemaphoreType.DMA((n_w + 1,)),
            pltpu.SemaphoreType.DMA((n_w, count)),
            pltpu.SemaphoreType.DMA((n_w, count)),
            pltpu.SemaphoreType.DMA((3,)),
            pltpu.SemaphoreType.DMA((3,)),
        ],
        compiler_params=pltpu.CompilerParams(
            collective_id=1, has_side_effects=True, vmem_limit_bytes=56 << 20
        ),
    )(*parts, img)


def norm_stats(v):
    mean = jnp.mean(v, axis=-1, keepdims=True)
    centered = v - mean
    r = lax.rsqrt(jnp.mean(centered * centered, axis=-1, keepdims=True) + EPS)
    return centered * r, r


def norm_back(xhat, r, gain, e):
    u = e * gain
    mu = jnp.mean(u, axis=-1, keepdims=True)
    mx = jnp.mean(u * xhat, axis=-1, keepdims=True)
    return r * (u - mu - xhat * mx), jnp.sum(e * xhat, axis=(0, 1))


def mm(a, b):
    return jnp.einsum("btd,de->bte", a, b, preferred_element_type=f32)


def mm_t(a, b):
    return jnp.einsum("bte,de->btd", a, b, preferred_element_type=f32)


def wgrad(a, b):
    return jnp.einsum("btd,bte->de", a, b, preferred_element_type=f32)


def split_heads(a):
    b, t, _ = a.shape
    return a.reshape(b, t, -1, HEAD)


def attend(q, k, v, allowed):
    s = jnp.einsum("bqhe,bkhe->bhqk", q, k, preferred_element_type=f32) * HEAD ** (-0.5)
    s = jnp.where(allowed, s, -1e30)
    ex = jnp.exp(s - jnp.max(s, axis=-1, keepdims=True))
    p = ex / jnp.sum(ex, axis=-1, keepdims=True)
    o = jnp.einsum("bhqk,bkhe->bqhe", p.astype(bf16), v, preferred_element_type=f32)
    return p, o.astype(bf16)


def attend_back(q, k, v, p, g):
    dp = jnp.einsum("bqhe,bkhe->bhqk", g, v, preferred_element_type=f32)
    ds = (p * (dp - jnp.sum(dp * p, axis=-1, keepdims=True)) * HEAD ** (-0.5)).astype(bf16)
    dq = jnp.einsum("bhqk,bkhe->bqhe", ds, k, preferred_element_type=f32).astype(bf16)
    dk = jnp.einsum("bhqk,bqhe->bkhe", ds, q, preferred_element_type=f32).astype(bf16)
    dv = jnp.einsum("bhqk,bqhe->bkhe", p.astype(bf16), g, preferred_element_type=f32).astype(bf16)
    return dq, dk, dv


def layer(x0, img, mask, gains, weights, cot):
    g1, g2, g3 = (g.astype(f32) for g in gains)
    w_qkv, w_so, w_cq, w_ckv, w_co, w_up, w_down = weights
    b, t, d = x0.shape
    x = x0.astype(f32)
    pos = jnp.arange(t)
    causal = (pos[:, None] >= pos[None, :])[None, None]
    allowed = (mask > 0)[:, None, None, :]
    h1, r1 = norm_stats(x)
    n1 = (h1 * g1).astype(bf16)
    qkv = mm(n1, w_qkv).astype(bf16)
    q1, k1, v1 = (split_heads(qkv[..., i * d : (i + 1) * d]) for i in range(3))
    p1, o1 = attend(q1, k1, v1, causal)
    o1 = o1.reshape(b, t, d)
    x1 = x + mm(o1, w_so)
    h2, r2 = norm_stats(x1)
    n2 = (h2 * g2).astype(bf16)
    q2 = split_heads(mm(n2, w_cq).astype(bf16))
    kv = mm(img, w_ckv).astype(bf16)
    k2, v2 = split_heads(kv[..., :d]), split_heads(kv[..., d:])
    p2, o2 = attend(q2, k2, v2, allowed)
    o2 = o2.reshape(b, t, d)
    x2 = x1 + mm(o2, w_co)
    h3, r3 = norm_stats(x2)
    n3 = (h3 * g3).astype(bf16)
    hpre = mm(n3, w_up)
    cdf = 0.5 * (1.0 + lax.erf(hpre * (0.5**0.5)))
    act = (hpre * cdf).astype(bf16)
    out = (x2 + mm(act, w_down)).astype(bf16)

    gw_down = wgrad(act, cot)
    pdf = jnp.exp(-0.5 * hpre * hpre) * (0.5 / jnp.pi) ** 0.5
    gh = (mm_t(cot, w_down) * (cdf + hpre * pdf)).astype(bf16)
    gw_up = wgrad(n3, gh)
    dx2, gg3 = norm_back(h3, r3, g3, mm_t(gh, w_up))
    gx2 = cot.astype(f32) + dx2
    gx2b = gx2.astype(bf16)
    gw_co = wgrad(o2, gx2b)
    go2 = split_heads(mm_t(gx2b, w_co).astype(bf16))
    dq2, dk2, dv2 = attend_back(q2, k2, v2, p2, go2)
    dq2 = dq2.reshape(b, t, d)
    dkv = jnp.concatenate([dk2.reshape(b, -1, d), dv2.reshape(b, -1, d)], axis=-1)
    gw_ckv = wgrad(img, dkv)
    gimg = mm_t(dkv, w_ckv).astype(bf16)
    gw_cq = wgrad(n2, dq2)
    dx1, gg2 = norm_back(h2, r2, g2, mm_t(dq2, w_cq))
    gx1 = gx2 + dx1
    gx1b = gx1.astype(bf16)
    gw_so = wgrad(o1, gx1b)
    go1 = split_heads(mm_t(gx1b, w_so).astype(bf16))
    dq1, dk1, dv1 = attend_back(q1, k1, v1, p1, go1)
    dqkv = jnp.concatenate([a.reshape(b, t, d) for a in (dq1, dk1, dv1)], axis=-1)
    gw_qkv = wgrad(n1, dqkv)
    dx0, gg1 = norm_back(h1, r1, g1, mm_t(dqkv, w_qkv))
    gx0 = gx1 + dx0
    return out, gx0, gimg, (gg1, gg2, gg3), (gw_qkv, gw_so, gw_cq, gw_ckv, gw_co, gw_up, gw_down)


def on_device(captions, images, tissue_mask, gain_self, gain_cross, gain_mlp, *rest):
    weights, cotangent = rest[:-1], rest[-1]
    n_dp, n_seq = lax.axis_size("dp"), lax.axis_size("seq")
    count = captions.shape[0]
    start = lax.axis_index("seq") * count
    img = lax.dynamic_slice_in_dim(images, start, count, 0)
    mask = lax.dynamic_slice_in_dim(tissue_mask, start, count, 0)
    gains = jnp.stack([gain_self, gain_cross, gain_mlp], axis=1)
    own_kernels = n_seq == 4 and n_dp % 2 == 0 and all(w.shape[0] % 8 == 0 for w in weights)
    d = captions.shape[-1]
    if own_kernels:
        nz = n_dp // 2
        pad = jnp.pad(gains, ((0, 0), (0, LANES - 3)))
        *full, gains = gather_all(nz, [*weights, pad])
        full = [w.reshape(-1, w.shape[-1]) for w in full]
        gains = gains.reshape(-1, LANES)
    else:
        full = [lax.all_gather(w, BOTH, axis=0, tiled=True) for w in weights]
        gains = lax.all_gather(gains, BOTH, axis=0, tiled=True)
    gains = tuple(gains[:, i] for i in range(3))
    out, gx0, gimg, gg, gw = layer(captions, img, mask, gains, full, cotangent)
    gg = jnp.stack(gg, axis=1)
    gw = [g.astype(bf16) for g in gw]
    if own_kernels:
        pad = jnp.pad(gg, ((0, 0), (0, LANES - 3))).astype(bf16)
        parts = [g.reshape(nz, 2, 2, 2, -1, g.shape[-1]) for g in (*gw[::-1], pad)]
        img_parts = gimg.reshape(-1, n_seq, d // n_seq).swapaxes(0, 1)
        *shards, gg, gimg = scatter_all(nz, parts, img_parts)
        shards = shards[::-1]
        gimg = gimg.reshape(images.shape[0], images.shape[1], -1)
    else:
        shards = [
            lax.psum_scatter(g, BOTH, scatter_dimension=0, tiled=True).astype(f32) for g in gw
        ]
        gg = lax.psum_scatter(gg, BOTH, scatter_dimension=0, tiled=True)
        gimg = lax.all_to_all(gimg, "seq", split_axis=2, concat_axis=0, tiled=True)
    return (out, gx0, gimg.astype(f32), gg[:, 0], gg[:, 1], gg[:, 2], *shards)


def solution(mesh):
    tok = P(BOTH, None, None)
    vec = P(BOTH)
    mat = P(BOTH, None)
    return jax.shard_map(
        on_device,
        mesh=mesh,
        in_specs=(tok, P("dp", None, None), P("dp", None), vec, vec, vec, *([mat] * 7), tok),
        out_specs=(tok, tok, P("dp", None, "seq"), vec, vec, vec, *([mat] * 7)),
        check_vma=False,
    )
```

```python
import functools

import jax
import jax.numpy as jnp
from jax import lax
from jax.experimental import pallas as pl
from jax.experimental.pallas import tpu as pltpu
from jax.sharding import PartitionSpec as P

HEADS = 12
HEAD = 64
EPS = 1e-05
BOTH = ("dp", "seq")
f32 = jnp.float32
bf16 = jnp.bfloat16
MESH = pl.DeviceIdType.MESH
HBM = pltpu.MemorySpace.HBM
VMEM = pltpu.MemorySpace.VMEM
LANES = 128


class Place:
    def __init__(self, nz):
        dp, seq = lax.axis_index("dp"), lax.axis_index("seq")
        self.nz = nz
        self.z, self.x = dp // 2, lax.rem(dp, 2)
        self.y, self.c = seq // 2, lax.rem(seq, 2)
        c, x, y = self.c, self.x, self.y
        self.p = x + c * (y - x)
        self.s = y + c * (x - y)
        self.sib = (dp, 2 * y + (1 - c))
        self.p_xy = (x + (1 - c) * (1 - 2 * x), y + c * (1 - 2 * y))
        self.s_xy = (x + c * (1 - 2 * x), y + (1 - c) * (1 - 2 * y))
        self.ps_xy = (1 - x, 1 - y)
        self.p_dev = self.dev(self.z, self.p_xy)
        self.s_dev = self.dev(self.z, self.s_xy)
        self.z_of = [lax.rem(self.z + k, nz) for k in range(nz)]
        self.z_devs = [self.dev(self.z_of[k], (x, y)) for k in range(nz)]

    def dev(self, z, xy):
        return (2 * z + xy[0], 2 * xy[1] + self.c)

    def column(self, p, s):
        return p + self.c * (s - p), s + self.c * (p - s)

    def partners(self):
        return [*self.z_devs[1:], self.p_dev, self.s_dev, self.sib]


def enter(partners):
    barrier = pltpu.get_barrier_semaphore()
    for d in partners:
        pl.semaphore_signal(barrier, inc=1, device_id=d, device_id_type=MESH)
    pl.semaphore_wait(barrier, len(partners))


def remote(src, dst, sems, i, dev):
    return pltpu.make_async_remote_copy(
        src_ref=src, dst_ref=dst, send_sem=sems[0].at[i], recv_sem=sems[1].at[i],
        device_id=dev, device_id_type=MESH,
    )


class Gather:
    def __init__(self, here, shard, full, sems, local):
        h = here
        x, y, c = h.x, h.y, h.c
        mine = full.at[h.z, x, y, c]

        def col(xy):
            return full.at[:, xy[0], xy[1], c]

        self.own = pltpu.make_async_copy(shard, mine, local)
        nz = h.nz
        self.zs = [remote(shard, mine, sems, k - 1, h.z_devs[k]) for k in range(1, nz)]
        own, px, sx, psx = (x, y), h.p_xy, h.s_xy, h.ps_xy
        n = nz - 1
        self.p_own = remote(col(own), col(own), sems, n, h.p_dev)
        self.s_own = remote(col(own), col(own), sems, n + 1, h.s_dev)
        self.s_p = remote(col(px), col(px), sems, n + 2, h.s_dev)
        self.sibs = [
            remote(col(xy), col(xy), sems, n + 3 + i, h.sib)
            for i, xy in enumerate((own, px, sx, psx))
        ]

    @staticmethod
    def count(nz):
        return nz + 6

    def step(self, i):
        if i == 0:
            self.own.start()
            for t in self.zs:
                t.start()
        elif i == 1:
            self.own.wait()
            for t in self.zs:
                t.wait_recv()
            self.p_own.start()
            self.s_own.start()
            self.sibs[0].start()
        elif i == 2:
            self.p_own.wait_recv()
            self.s_p.start()
            self.sibs[1].start()
        elif i == 3:
            self.s_own.wait_recv()
            self.sibs[2].start()
            self.s_p.wait_recv()
            self.sibs[3].start()
        elif i == 4:
            for t in self.sibs:
                t.wait_recv()
        elif i == 5:
            for t in (*self.zs, self.p_own, self.s_own, self.s_p, *self.sibs):
                t.wait_send()


class Clock:
    def __init__(self, budget):
        self.budget, self.queue = budget, []

    def add(self, cost, work):
        self.queue.append((cost, work))

    def spend(self, budget=None):
        left = self.budget if budget is None else budget
        while self.queue and left > 0:
            cost, work = self.queue.pop(0)
            work()
            left -= cost


def stats(v):
    mean = jnp.mean(v, axis=-1, keepdims=True)
    cen = v - mean
    r = lax.rsqrt(jnp.mean(cen * cen, axis=-1, keepdims=True) + EPS)
    return cen * r, r


def dot(a, b):
    return jnp.dot(a, b, preferred_element_type=f32)


def dot_nt(a, b):
    return lax.dot_general(a, b, (((1,), (1,)), ((), ())), preferred_element_type=f32)


def dot_tn(a, b):
    return lax.dot_general(a, b, (((0,), (0,)), ((), ())), preferred_element_type=f32)


def matrix(ref, lo=None, hi=None):
    v = ref[..., lo:hi]
    return v.reshape(-1, v.shape[-1])


def head_lanes():
    lane = lax.broadcasted_iota(jnp.int32, (1, 2 * HEAD), 1)
    low = jnp.where(lane < HEAD, 1.0, 0.0)
    return low.astype(bf16), (1.0 - low).astype(bf16)


def softmax(s):
    e = jnp.exp(s - jnp.max(s, axis=-1, keepdims=True))
    return (e * (1.0 / jnp.sum(e, axis=-1, keepdims=True))).astype(bf16)


def pair(ref, rows, base, j):
    return ref.at[rows, pl.ds(pl.multiple_of(base + j * 2 * HEAD, 2 * HEAD), 2 * HEAD)]


SCALE = HEAD ** (-0.5)


def chunk_cols(weights, d):
    out = []
    for i, w in enumerate(weights):
        wide = d if w.shape[1] % d == 0 and i < 6 else d // 3
        out += [(i, s, wide) for s in range(0, w.shape[1], wide)]
    return out


def forward_kernel(nz, dims, chunks, *refs):
    b, t, d, kp, ff = dims
    n = len(chunks) + 1
    xs, img, mb, gsh = refs[:4]
    shards = refs[4:11]
    out = refs[11]
    res = refs[12 : 12 + N_RES]
    fulls = refs[12 + N_RES : 12 + N_RES + n]
    rest = refs[12 + N_RES + n :]
    (n1, qkv, p1, o1, x1, n2, q2, kv2, p2, o2, x2, n3, act, dg, grow) = keep = rest[:N_RES]
    g = rest[N_RES : N_RES + n]
    local, ssem, rsem, csem = rest[N_RES + n :]
    here = Place(nz)
    enter(here.partners())
    srcs = [gsh] + [shards[i].at[:, s : s + w] for i, s, w in chunks]
    gs = [
        Gather(here, srcs[i], g[i], (ssem.at[i], rsem.at[i]), local.at[i]) for i in range(n)
    ]
    for q in gs:
        q.step(0)
    copies = []

    def flush(src, dst):
        cp = pltpu.make_async_copy(src, dst, csem.at[len(copies)])
        cp.start()
        copies.append(cp)

    def save(*which):
        for k in which:
            flush(keep[k], res[k])

    names = {}
    for k, (i, s, wide) in enumerate(chunks):
        names.setdefault(i, []).append(k + 1)
    lanes = head_lanes()
    heads = d // HEAD
    pairs = heads // 2
    tok = [slice(i * t, (i + 1) * t) for i in range(b)]
    pat = [slice(i * kp, (i + 1) * kp) for i in range(b)]

    def first():
        grow[...] = jnp.transpose(matrix(g[0]).astype(f32))[:8]
        for r in tok:
            h, _ = stats(xs[r].astype(f32))
            n1[r] = (h * grow[0:1]).astype(bf16)
        save(0, 14)

    def project(src, k, dst, at, step=256):
        def work():
            wide = g[k].shape[-1]
            for s in range(0, wide, min(step, wide)):
                e = min(s + step, wide)
                dst[:, at + s : at + e] = dot(src[...], matrix(g[k], s, e)).astype(bf16)

        return work

    def self_pairs(lo, hi):
        def body(j, _):
            causal = lax.broadcasted_iota(jnp.int32, (t, t), 0) >= lax.broadcasted_iota(
                jnp.int32, (t, t), 1
            )
            for i, r in enumerate(tok):
                q, k, v = (pair(qkv, r, m * d, j)[...] for m in range(3))
                o = jnp.zeros((t, 2 * HEAD), f32)
                for a in range(2):
                    s = dot_nt(q, k * lanes[a]) * SCALE
                    p = softmax(jnp.where(causal, s, -1e30))
                    p1[i * heads + 2 * j + a] = p
                    o = o + dot(p, v * lanes[a])
                pair(o1, r, 0, j)[...] = o.astype(bf16)
            return 0

        return lambda: lax.fori_loop(lo, hi, body, 0)

    def cross_pairs(lo, hi):
        def body(j, _):
            for i, r in enumerate(tok):
                q = pair(q2, r, 0, j)[...]
                k, v = (pair(kv2, pat[i], m * d, j)[...] for m in range(2))
                bias = mb[i : i + 1]
                o = jnp.zeros((t, 2 * HEAD), f32)
                for a in range(2):
                    p = softmax(dot_nt(q, k * lanes[a]) * SCALE + bias)
                    p2[i * heads + 2 * j + a] = p
                    o = o + dot(p, v * lanes[a])
                pair(o2, r, 0, j)[...] = o.astype(bf16)
            return 0

        return lambda: lax.fori_loop(lo, hi, body, 0)

    def residual(base, o, k, dst, row, normed):
        def work():
            for r in tok:
                v = base[r].astype(f32) + dot(o[r], matrix(g[k]))
                dst[r] = v
                h, _ = stats(v)
                normed[r] = (h * grow[row : row + 1]).astype(bf16)

        return work

    def mlp_up(k, at):
        def work():
            for s in range(0, g[k].shape[-1], 256):
                h = dot(n3[...], matrix(g[k], s, s + 256))
                cdf = 0.5 * (1.0 + lax.erf(h * (0.5**0.5)))
                act[:, at + s : at + s + 256] = (h * cdf).astype(bf16)
                pdf = jnp.exp(-0.5 * h * h) * (0.5 / jnp.pi) ** 0.5
                dg[:, at + s : at + s + 256] = (cdf + h * pdf).astype(bf16)

        return work

    def mlp_down(k, at):
        def work():
            wide = g[k].shape[-1]
            y = x2[:, at : at + wide] + dot(act[...], matrix(g[k]))
            out[:, at : at + wide] = y.astype(bf16)

        return work

    clock = Clock(BUDGET)
    third = [(i * pairs // 3, (i + 1) * pairs // 3) for i in range(3)]

    def arrived(k):
        if k == 0:
            clock.add(2.0, first)
            return
        i, s, wide = chunks[k - 1]
        last = k == names[i][-1]
        if i == 0:
            clock.add(1.7, project(n1, k, qkv, s))
            if last:
                clock.add(0.0, lambda: save(1))
                for lo, hi in third:
                    clock.add(2.5, self_pairs(lo, hi))
                clock.add(0.0, lambda: save(2, 3))
        elif i == 1:
            clock.add(2.5, residual(xs, o1, k, x1, 1, n2))
            clock.add(0.0, lambda: save(4, 5))
        elif i == 2:
            clock.add(1.7, project(n2, k, q2, 0))
            clock.add(0.0, lambda: save(6))
        elif i == 3:
            clock.add(2.5, project(img, k, kv2, s))
            if last:
                clock.add(0.0, lambda: save(7))
                for lo, hi in third:
                    clock.add(3.0, cross_pairs(lo, hi))
                clock.add(0.0, lambda: save(8, 9))
        elif i == 4:
            clock.add(2.5, residual(x1, o2, k, x2, 2, n3))
            clock.add(0.0, lambda: save(10, 11))
        elif i == 5:
            clock.add(3.5, mlp_up(k, s))
            if last:
                clock.add(0.0, lambda: save(12, 13))
        else:
            clock.add(2.0, mlp_down(k, s))

    for tick in range(n + LAG[-1]):
        for step in (4, 3, 2, 1):
            i = tick - LAG[step - 1]
            if 0 <= i < n:
                gs[i].step(step)
                if step == 4:
                    flush(g[i], fulls[i])
                    arrived(i)
        clock.spend()
    clock.spend(1e9)
    for q in gs:
        q.step(5)
    for cp in copies:
        cp.wait()


N_RES = 15
LAG = (0, 2, 4, 6)
BUDGET = 4.0


def residual_shapes(b, t, d, kp, ff):
    m, heads = b * t, d // HEAD
    S = jax.ShapeDtypeStruct
    tok, tokf = S((m, d), bf16), S((m, d), f32)
    return [
        tok, S((m, 3 * d), bf16), S((b * heads, t, t), bf16), tok, tokf, tok, tok,
        S((b * kp, 2 * d), bf16), S((b * heads, t, kp), bf16), tok, tokf, tok,
        S((m, ff), bf16), S((m, ff), bf16), S((8, d), f32),
    ]


def forward(nz, xs, img, mb, gains, weights):
    b, t, d = xs.shape
    kp, ff = img.shape[1], weights[5].shape[1]
    chunks = chunk_cols(weights, d)
    n = len(chunks) + 1
    res = residual_shapes(b, t, d, kp, ff)
    blocks = [gains.shape] + [(weights[i].shape[0], w) for i, _, w in chunks]
    fulls = [jax.ShapeDtypeStruct((nz, 2, 2, 2, *s), bf16) for s in blocks]
    count = Gather.count(nz)
    outs = pl.pallas_call(
        functools.partial(forward_kernel, nz, (b, t, d, kp, ff), chunks),
        out_shape=[jax.ShapeDtypeStruct((b * t, d), bf16), *res, *fulls],
        in_specs=[*([pl.BlockSpec(memory_space=VMEM)] * 3), *([pl.BlockSpec(memory_space=HBM)] * 8)],
        out_specs=[
            pl.BlockSpec(memory_space=VMEM), *([pl.BlockSpec(memory_space=HBM)] * (N_RES + n))
        ],
        scratch_shapes=[
            *(pltpu.VMEM(s.shape, s.dtype) for s in (*res, *fulls)),
            pltpu.SemaphoreType.DMA((n,)),
            pltpu.SemaphoreType.DMA((n, count)),
            pltpu.SemaphoreType.DMA((n, count)),
            pltpu.SemaphoreType.DMA((N_RES + n,)),
        ],
        compiler_params=pltpu.CompilerParams(
            collective_id=0, has_side_effects=True, vmem_limit_bytes=60 << 20
        ),
    )(xs.reshape(b * t, d), img.reshape(b * kp, d), mb, gains, *weights)
    return outs[0].reshape(b, t, d), outs[1 : 1 + N_RES], outs[1 + N_RES :]


class Scatter:
    def __init__(self, here, part, bufs, out, sems):
        self.h, self.out = here, out
        self.rc, self.rs, self.rp, self.rz = bufs
        h, nz = here, here.nz
        self.own = part.at[:, :, :, h.c]
        self.core = remote(part.at[:, :, :, 1 - h.c], self.rc, sems, 0, h.sib)
        self.s = [
            remote(self.rc.at[:, *h.column(p, 1 - h.s)], self.rs.at[p], sems, 1 + i, h.s_dev)
            for i, p in enumerate((1 - h.p, h.p))
        ]
        self.pp = remote(self.rs.at[1 - h.p], self.rp, sems, 3, h.p_dev)
        self.zs = [
            remote(self.rp.at[h.z_of[k]], self.rz.at[k - 1], sems, 3 + k, h.z_devs[k])
            for k in range(1, nz)
        ]

    @staticmethod
    def count(nz):
        return nz + 3

    def add(self, dst, a, b):
        def body(z, _):
            dst[z] = (a[z].astype(f32) + b[z].astype(f32)).astype(bf16)
            return 0

        lax.fori_loop(0, self.h.nz, body, 0)

    def step(self, i):
        h = self.h
        if i == 0:
            self.core.start()
        elif i == 1:
            self.core.wait_recv()
            for j, p in enumerate((1 - h.p, h.p)):
                xy = h.column(p, 1 - h.s)
                self.add(self.rc.at[:, *xy], self.rc.at[:, *xy], self.own.at[:, *xy])
                self.s[j].start()
            for p in (1 - h.p, h.p):
                xy = h.column(p, h.s)
                self.add(self.rc.at[:, *xy], self.rc.at[:, *xy], self.own.at[:, *xy])
            self.core.wait_send()
        elif i == 2:
            xy = h.column(1 - h.p, h.s)
            self.s[0].wait_recv()
            self.add(self.rs.at[1 - h.p], self.rs.at[1 - h.p], self.rc.at[:, *xy])
            self.pp.start()
            xy = h.column(h.p, h.s)
            self.s[1].wait_recv()
            self.add(self.rs.at[h.p], self.rs.at[h.p], self.rc.at[:, *xy])
        elif i == 3:
            self.pp.wait_recv()
            self.add(self.rp, self.rp, self.rs.at[h.p])
            for t in self.zs:
                t.start()
        elif i == 4:
            for t in self.zs:
                t.wait_recv()
            total = self.rp[h.z].astype(f32)
            for k in range(h.nz - 1):
                total = total + self.rz[k].astype(f32)
            self.out[...] = total
        elif i == 5:
            for t in (*self.s, self.pp, *self.zs):
                t.wait_send()


class Planner:
    ADDS = (0.3, 1.0, 0.6, 0.4, 0.3)

    def __init__(self, scatters, sizes, slots):
        self.sc, self.sizes, self.slots = scatters, sizes, slots
        self.now, self.xy, self.zl, self.core = 0.0, 0.0, 0.0, 0.0
        self.ready = {}

    def start(self, i):
        self.sc[i].step(0)
        self.core = max(self.core, self.now) + self.sizes[i] * 1.5 + 0.5
        self.ready[i] = (1, self.core + 1.0)

    def emit(self, i):
        step, when = self.ready[i]
        self.now = max(self.now, when) + self.ADDS[step] * self.sizes[i]
        self.sc[i].step(step)
        size = self.sizes[i]
        if step == 1:
            self.xy = max(self.xy, self.now) + 3.8 * size
            self.ready[i] = (2, self.xy + 1.5)
        elif step == 2:
            self.xy = max(self.xy, self.now) + 1.9 * size
            self.ready[i] = (3, self.xy + 1.5)
        elif step == 3:
            self.zl = max(self.zl, self.now) + 3.8 * size
            self.ready[i] = (4, self.zl + 1.5)
        else:
            del self.ready[i]

    def due(self, slack=0.0):
        best = None
        for i, (step, when) in self.ready.items():
            if when <= self.now + slack and (best is None or (step, -i) > best[0]):
                best = ((step, -i), i)
        return None if best is None else best[1]

    def settle(self):
        while (i := self.due()) is not None:
            self.emit(i)

    def free_slot(self, i):
        while i in self.ready and self.ready[i][0] == 1:
            self.emit(i)

    def compute(self, cost, work):
        self.settle()
        work()
        self.now += cost

    def finish(self):
        while self.ready:
            i = min(self.ready, key=lambda k: (self.ready[k][1], k))
            self.emit(i)
        for s in self.sc:
            s.step(5)


def backward_kernel(nz, dims, chunks, *refs):
    b, t, d, kp, ff = dims
    heads = d // HEAD
    pairs = heads // 2
    m = b * t
    n_c = len(chunks)
    order = [*range(n_c - 3, n_c), *range(n_c - 7, n_c - 3), 7, 5, 6, 4, 3, None, 0, 1, 2]
    n = len(order)
    h_in = refs[: 3 + N_RES + n_c]
    h_cot, h_img, h_xs = h_in[:3]
    res = dict(zip(RES_NAMES, h_in[3 : 3 + N_RES]))
    full = h_in[3 + N_RES :]
    at = len(h_in)
    gx_out, img_out = refs[at : at + 2]
    outs = refs[at + 2 : at + 9]
    gg_out = refs[at + 9]
    rest = list(refs[at + 10 :])
    take = lambda k: [rest.pop(0) for _ in range(k)]
    cot, act, dg, n3, xf, o2, p2, q2, kv2, img, n2, o1, p1, n1, xs, grow = take(16)
    gx, gxb, go, gi, ggr = take(5)
    wd, ws = take(3), take(6)
    pd, ps, pg = take(3), take(4), take(1)[0]
    bufs = [take(4) for _ in range(n)]
    lsem, ssem, rsem, isem, jsem, osem = rest
    here = Place(nz)
    dp, seq = lax.axis_index("dp"), lax.axis_index("seq")
    peers = [(dp, lax.rem(seq + k, 4)) for k in range(1, 4)]

    loads, waits = {}, {}

    def load(name, src, dst):
        cp = pltpu.make_async_copy(src, dst, lsem.at[len(loads)])
        loads[name] = cp
        cp.start()

    def need(*names):
        for k in names:
            if k in loads and k not in waits:
                loads[k].wait()
                waits[k] = True

    q_at = act.at[:, : 3 * d]
    load("act", res["act"], act)
    load("cot", h_cot, cot)
    for j in range(3):
        load("wd%d" % j, full[n_c - 3 + j], wd[j])
    load("dg", res["dg"], dg)
    load("n3", res["n3"], n3)
    for j in range(4):
        load("up%d" % j, full[n_c - 7 + j], ws[j])
    load("x2", res["x2"], xf)
    load("grow", res["grow"], grow)
    for name, dst in (("o2", o2), ("p2", p2), ("q2", q2), ("kv2", kv2)):
        load(name, res[name], dst)
    load("co", full[7], ws[4])
    load("ckv0", full[5], ws[5])
    load("img", h_img, img)
    for name, dst in (("n2", n2), ("o1", o1), ("p1", p1), ("n1", n1)):
        load(name, res[name], dst)
    load("xs", h_xs, xs)
    enter([*here.partners(), *peers])
    ggr[...] = jnp.zeros_like(ggr)

    parts, small = [], 0
    for k in order:
        if k is None:
            parts.append(pg)
        elif k >= n_c - 3:
            parts.append(pd[k - (n_c - 3)])
        else:
            parts.append(ps[small % 4])
            small += 1
    place = {k: i for i, k in enumerate(order)}
    dst = [
        gg_out if k is None else outs[chunks[k][0]].at[:, chunks[k][1] : chunks[k][1] + chunks[k][2]]
        for k in order
    ]
    sc = [
        Scatter(here, parts[i], bufs[i], dst[i], (ssem.at[i], rsem.at[i])) for i in range(n)
    ]
    sizes = [0.2 if k is None else 1.35 if k >= n_c - 3 else 1.0 for k in order]
    plan = Planner(sc, sizes, None)
    smalls = [i for i, k in enumerate(order) if k is not None and k < n_c - 3]

    def slot_ready(i):
        if i in smalls and smalls.index(i) >= 4:
            plan.free_slot(smalls[smalls.index(i) - 4])

    lanes = head_lanes()
    tok = [slice(i * t, (i + 1) * t) for i in range(b)]
    pat = [slice(i * kp, (i + 1) * kp) for i in range(b)]

    def grad_small(k, x, dy, first, cost):
        i = place[k]
        slot_ready(i)

        def work():
            for s in range(0, d, 256):
                r = dot_tn(x[...], dy[:, first + s : first + s + 256])
                parts[i][:, :, :, :, :, s : s + 256] = r.reshape(nz, 2, 2, 2, -1, 256).astype(bf16)

        plan.compute(cost, work)
        plan.start(i)

    def grad_down(j):
        k = n_c - 3 + j
        i = place[k]
        wide = d // 3

        def work():
            rows = ff // nz
            for z in range(nz):
                r = dot_tn(act[:, z * rows : (z + 1) * rows], cot[:, j * wide : (j + 1) * wide])
                parts[i][z] = r.reshape(2, 2, 2, -1, wide).astype(bf16)

        plan.compute(1.8, work)
        plan.start(i)

    def hidden(z):
        rows = ff // nz
        cols = slice(z * rows, (z + 1) * rows)
        wide = d // 3

        def work():
            half = rows // 2
            for x in range(2):
                g = None
                for j in range(3):
                    w = wd[j][z, x].reshape(half, wide)
                    term = dot_nt(cot[:, j * wide : (j + 1) * wide], w)
                    g = term if g is None else g + term
                at = slice(z * rows + x * half, z * rows + (x + 1) * half)
                dg[:, at] = (g * dg[:, at].astype(f32)).astype(bf16)

        plan.compute(1.3, work)

    def norm_grad(src, ups, base, row, first):
        def work():
            gain = grow[row : row + 1]
            acc = jnp.zeros((1, d), f32)
            for r in tok:
                e = None
                for j, w in enumerate(ups):
                    term = dot_nt(src[r, j * d : (j + 1) * d], matrix(w))
                    e = term if e is None else e + term
                h, rs = stats_r(base[r].astype(f32))
                u = e * gain
                mu = jnp.mean(u, axis=-1, keepdims=True)
                mx = jnp.mean(u * h, axis=-1, keepdims=True)
                prev = cot[r].astype(f32) if first else gx[r]
                v = prev + rs * (u - mu - h * mx)
                gx[r] = v
                gxb[r] = v.astype(bf16)
                acc = acc + jnp.sum(e * h, axis=0, keepdims=True)
            ggr[row : row + 1] = acc

        plan.compute(1.5 + 1.2 * len(ups), work)

    def back_project(w):
        def work():
            half = d // 2
            for s in range(2):
                rows = w[s * (nz // 2) : (s + 1) * (nz // 2)].reshape(half, d)
                go[:, s * half : (s + 1) * half] = dot_nt(gxb[...], rows).astype(bf16)

        plan.compute(1.4, work)

    def pairs_back(lo, hi, p_ref, q_ref, q_base, kv_ref, kv_base, rows):
        def body(j, _):
            for i, r in enumerate(tok):
                rk = rows[i]
                q, g = pair(q_ref, r, q_base, j)[...], pair(go, r, 0, j)[...]
                k, v = (pair(kv_ref, rk, kv_base + x * d, j)[...] for x in range(2))
                dq = dk = dv = None
                for a in range(2):
                    lane = lanes[a]
                    pb = p_ref[i * heads + 2 * j + a]
                    p = pb.astype(f32)
                    dpr = dot_nt(g, v * lane)
                    pd = dpr * p
                    ds = ((pd - p * jnp.sum(pd, axis=-1, keepdims=True)) * SCALE).astype(bf16)
                    terms = (dot(ds, k * lane), dot_tn(ds, q * lane), dot_tn(pb, g * lane))
                    if a == 0:
                        dq, dk, dv = terms
                    else:
                        dq, dk, dv = dq + terms[0], dk + terms[1], dv + terms[2]
                pair(q_ref, r, q_base, j)[...] = dq.astype(bf16)
                pair(kv_ref, rk, kv_base, j)[...] = dk.astype(bf16)
                pair(kv_ref, rk, kv_base + d, j)[...] = dv.astype(bf16)
            return 0

        return lambda: lax.fori_loop(lo, hi, body, 0)

    thirds = [(i * pairs // 3, (i + 1) * pairs // 3) for i in range(3)]

    need("act", "cot")
    for j in range(3):
        grad_down(j)
    load("qkv", res["qkv"], q_at)
    need("wd0", "wd1", "wd2", "dg")
    for z in range(nz):
        hidden(z)
    need("n3")
    for j in range(4):
        grad_small(n_c - 7 + j, n3, dg, j * d, 1.4)
    need("up0", "up1", "up2", "up3", "x2", "grow")
    norm_grad(dg, ws[:4], xf, 2, True)
    load("x1", res["x1"], xf)
    load("ckv1", full[6], ws[0])
    load("cq", full[4], ws[1])
    load("so", full[3], ws[2])
    load("qkv0", full[0], ws[3])
    need("co")
    back_project(ws[4])
    load("qkv1", full[1], ws[4])
    need("o2")
    grad_small(7, o2, gxb, 0, 1.4)
    need("p2", "q2", "kv2")
    for lo, hi in thirds:
        plan.compute(4.0, pairs_back(lo, hi, p2, q2, 0, kv2, 0, pat))
    need("img")
    grad_small(5, img, kv2, 0, 2.0)
    grad_small(6, img, kv2, d, 2.0)
    need("ckv0", "ckv1")
    wide = d // 4

    def image_grad():
        for i, r in enumerate(pat):
            y = dot_nt(kv2[r, :d], matrix(ws[5])) + dot_nt(kv2[r, d:], matrix(ws[0]))
            y = y.astype(bf16)
            for s in range(4):
                gi[s, r] = y[:, s * wide : (s + 1) * wide]

    plan.compute(4.0, image_grad)
    keep = pltpu.make_async_copy(gi.at[seq], img_out.at[seq], osem.at[0])
    keep.start()
    moves = [
        remote(gi.at[lax.rem(seq + k, 4)], img_out.at[seq], (isem, jsem), k - 1, peers[k - 1])
        for k in range(1, 4)
    ]
    for mv in moves:
        mv.start()
    load("qkv2", full[2], ws[5])
    need("n2", "cq", "x1")
    norm_grad(q2, [ws[1]], xf, 1, False)
    need("so")
    back_project(ws[2])
    grad_small(4, n2, q2, 0, 1.4)
    need("o1")
    grad_small(3, o1, gxb, 0, 1.4)
    need("p1", "qkv")
    for lo, hi in thirds:
        plan.compute(3.0, pairs_back(lo, hi, p1, act, 0, act, d, tok))
    need("xs", "qkv0", "qkv1", "qkv2", "n1")
    norm_grad(act, [ws[3], ws[4], ws[5]], xs, 0, False)
    gx_copy = pltpu.make_async_copy(gx, gx_out, osem.at[1])
    gx_copy.start()

    def gain_terms():
        r = jnp.transpose(ggr[...])
        pg[...] = r.reshape(nz, 2, 2, 2, -1, LANES).astype(bf16)

    plan.compute(0.7, gain_terms)
    plan.start(place[None])
    for j in range(3):
        grad_small(j, n1, act, j * d, 1.4)
    plan.finish()
    keep.wait()
    gx_copy.wait()
    for mv in moves:
        mv.wait()


def stats_r(v):
    mean = jnp.mean(v, axis=-1, keepdims=True)
    cen = v - mean
    r = lax.rsqrt(jnp.mean(cen * cen, axis=-1, keepdims=True) + EPS)
    return cen * r, r


RES_NAMES = (
    "n1", "qkv", "p1", "o1", "x1", "n2", "q2", "kv2",
    "p2", "o2", "x2", "n3", "act", "dg", "grow",
)


def backward(nz, cot, img, xs, weights, res, fulls):
    b, t, d = xs.shape
    kp, ff = img.shape[1], weights[5].shape[1]
    m, heads = b * t, d // HEAD
    chunks = chunk_cols(weights, d)
    n_c = len(chunks)
    n = n_c + 1
    rows = weights[0].shape[0]
    down = (weights[6].shape[0], d // 3)
    tok, tokf = pltpu.VMEM((m, d), bf16), pltpu.VMEM((m, d), f32)
    part = lambda blk: pltpu.VMEM((nz, 2, 2, 2, *blk), bf16)
    blocks = [down] * 3 + [(rows, d)] * 9 + [(rows, LANES)] + [(rows, d)] * 3
    bufs = []
    for blk in blocks:
        bufs += [
            pltpu.VMEM((nz, 2, 2, *blk), bf16),
            pltpu.VMEM((2, nz, *blk), bf16),
            pltpu.VMEM((nz, *blk), bf16),
            pltpu.VMEM((nz - 1, *blk), bf16),
        ]
    count = Scatter.count(nz)
    hbm, vm = pl.BlockSpec(memory_space=HBM), pl.BlockSpec(memory_space=VMEM)
    hid = pltpu.VMEM((m, ff), bf16)
    S = jax.ShapeDtypeStruct
    outs = pl.pallas_call(
        functools.partial(backward_kernel, nz, (b, t, d, kp, ff), chunks),
        out_shape=[
            S((m, d), f32), S((4, b * kp, d // 4), bf16),
            *(S(w.shape, f32) for w in weights), S((rows, LANES), f32),
        ],
        in_specs=[hbm] * (3 + N_RES + n_c),
        out_specs=[hbm, hbm, *([vm] * 8)],
        scratch_shapes=[
            tok, hid, hid, tok, tokf, tok, pltpu.VMEM((b * heads, t, kp), bf16), tok,
            pltpu.VMEM((b * kp, 2 * d), bf16), pltpu.VMEM((b * kp, d), bf16), tok, tok,
            pltpu.VMEM((b * heads, t, t), bf16), tok, tok, pltpu.VMEM((8, d), f32),
            tokf, tok, tok, pltpu.VMEM((4, b * kp, d // 4), bf16), pltpu.VMEM((LANES, d), f32),
            *([part(down)] * 3), *([part((rows, d))] * 6),
            *([part(down)] * 3), *([part((rows, d))] * 4), part((rows, LANES)),
            *bufs,
            pltpu.SemaphoreType.DMA((3 + N_RES + n_c,)),
            pltpu.SemaphoreType.DMA((n, count)),
            pltpu.SemaphoreType.DMA((n, count)),
            pltpu.SemaphoreType.DMA((3,)),
            pltpu.SemaphoreType.DMA((3,)),
            pltpu.SemaphoreType.DMA((2,)),
        ],
        compiler_params=pltpu.CompilerParams(
            collective_id=1, has_side_effects=True, vmem_limit_bytes=63 << 20
        ),
    )(cot.reshape(m, d), img.reshape(b * kp, d), xs.reshape(m, d), *res, *fulls)
    return outs


def norm_stats(v):
    mean = jnp.mean(v, axis=-1, keepdims=True)
    centered = v - mean
    r = lax.rsqrt(jnp.mean(centered * centered, axis=-1, keepdims=True) + EPS)
    return centered * r, r


def norm_back(xhat, r, gain, e):
    u = e * gain
    mu = jnp.mean(u, axis=-1, keepdims=True)
    mx = jnp.mean(u * xhat, axis=-1, keepdims=True)
    return r * (u - mu - xhat * mx), jnp.sum(e * xhat, axis=(0, 1))


def mm(a, b):
    return jnp.einsum("btd,de->bte", a, b, preferred_element_type=f32)


def mm_t(a, b):
    return jnp.einsum("bte,de->btd", a, b, preferred_element_type=f32)


def wgrad(a, b):
    return jnp.einsum("btd,bte->de", a, b, preferred_element_type=f32)


def split_heads(a):
    b, t, _ = a.shape
    return a.reshape(b, t, -1, HEAD)


def attend(q, k, v, allowed):
    s = jnp.einsum("bqhe,bkhe->bhqk", q, k, preferred_element_type=f32) * HEAD ** (-0.5)
    s = jnp.where(allowed, s, -1e30)
    ex = jnp.exp(s - jnp.max(s, axis=-1, keepdims=True))
    p = ex / jnp.sum(ex, axis=-1, keepdims=True)
    o = jnp.einsum("bhqk,bkhe->bqhe", p.astype(bf16), v, preferred_element_type=f32)
    return p, o.astype(bf16)


def attend_back(q, k, v, p, g):
    dp = jnp.einsum("bqhe,bkhe->bhqk", g, v, preferred_element_type=f32)
    ds = (p * (dp - jnp.sum(dp * p, axis=-1, keepdims=True)) * HEAD ** (-0.5)).astype(bf16)
    dq = jnp.einsum("bhqk,bkhe->bqhe", ds, k, preferred_element_type=f32).astype(bf16)
    dk = jnp.einsum("bhqk,bqhe->bkhe", ds, q, preferred_element_type=f32).astype(bf16)
    dv = jnp.einsum("bhqk,bqhe->bkhe", p.astype(bf16), g, preferred_element_type=f32).astype(bf16)
    return dq, dk, dv


def layer(x0, img, mask, gains, weights, cot):
    g1, g2, g3 = (g.astype(f32) for g in gains)
    w_qkv, w_so, w_cq, w_ckv, w_co, w_up, w_down = weights
    b, t, d = x0.shape
    x = x0.astype(f32)
    pos = jnp.arange(t)
    causal = (pos[:, None] >= pos[None, :])[None, None]
    allowed = (mask > 0)[:, None, None, :]
    h1, r1 = norm_stats(x)
    n1 = (h1 * g1).astype(bf16)
    qkv = mm(n1, w_qkv).astype(bf16)
    q1, k1, v1 = (split_heads(qkv[..., i * d : (i + 1) * d]) for i in range(3))
    p1, o1 = attend(q1, k1, v1, causal)
    o1 = o1.reshape(b, t, d)
    x1 = x + mm(o1, w_so)
    h2, r2 = norm_stats(x1)
    n2 = (h2 * g2).astype(bf16)
    q2 = split_heads(mm(n2, w_cq).astype(bf16))
    kv = mm(img, w_ckv).astype(bf16)
    k2, v2 = split_heads(kv[..., :d]), split_heads(kv[..., d:])
    p2, o2 = attend(q2, k2, v2, allowed)
    o2 = o2.reshape(b, t, d)
    x2 = x1 + mm(o2, w_co)
    h3, r3 = norm_stats(x2)
    n3 = (h3 * g3).astype(bf16)
    hpre = mm(n3, w_up)
    cdf = 0.5 * (1.0 + lax.erf(hpre * (0.5**0.5)))
    act = (hpre * cdf).astype(bf16)
    out = (x2 + mm(act, w_down)).astype(bf16)

    gw_down = wgrad(act, cot)
    pdf = jnp.exp(-0.5 * hpre * hpre) * (0.5 / jnp.pi) ** 0.5
    gh = (mm_t(cot, w_down) * (cdf + hpre * pdf)).astype(bf16)
    gw_up = wgrad(n3, gh)
    dx2, gg3 = norm_back(h3, r3, g3, mm_t(gh, w_up))
    gx2 = cot.astype(f32) + dx2
    gx2b = gx2.astype(bf16)
    gw_co = wgrad(o2, gx2b)
    go2 = split_heads(mm_t(gx2b, w_co).astype(bf16))
    dq2, dk2, dv2 = attend_back(q2, k2, v2, p2, go2)
    dq2 = dq2.reshape(b, t, d)
    dkv = jnp.concatenate([dk2.reshape(b, -1, d), dv2.reshape(b, -1, d)], axis=-1)
    gw_ckv = wgrad(img, dkv)
    gimg = mm_t(dkv, w_ckv).astype(bf16)
    gw_cq = wgrad(n2, dq2)
    dx1, gg2 = norm_back(h2, r2, g2, mm_t(dq2, w_cq))
    gx1 = gx2 + dx1
    gx1b = gx1.astype(bf16)
    gw_so = wgrad(o1, gx1b)
    go1 = split_heads(mm_t(gx1b, w_so).astype(bf16))
    dq1, dk1, dv1 = attend_back(q1, k1, v1, p1, go1)
    dqkv = jnp.concatenate([a.reshape(b, t, d) for a in (dq1, dk1, dv1)], axis=-1)
    gw_qkv = wgrad(n1, dqkv)
    dx0, gg1 = norm_back(h1, r1, g1, mm_t(dqkv, w_qkv))
    gx0 = gx1 + dx0
    return out, gx0, gimg, (gg1, gg2, gg3), (gw_qkv, gw_so, gw_cq, gw_ckv, gw_co, gw_up, gw_down)


def native(captions, img, mask, gains, weights, cotangent):
    full = [lax.all_gather(w, BOTH, axis=0, tiled=True) for w in weights]
    gains = lax.all_gather(gains, BOTH, axis=0, tiled=True)
    gains = tuple(gains[:, i] for i in range(3))
    out, gx0, gimg, gg, gw = layer(captions, img, mask, gains, full, cotangent)
    gg = lax.psum_scatter(jnp.stack(gg, axis=1), BOTH, scatter_dimension=0, tiled=True)
    shards = [
        lax.psum_scatter(g.astype(bf16), BOTH, scatter_dimension=0, tiled=True).astype(f32)
        for g in gw
    ]
    gimg = lax.all_to_all(gimg, "seq", split_axis=2, concat_axis=0, tiled=True)
    return (out, gx0, gimg.astype(f32), gg[:, 0], gg[:, 1], gg[:, 2], *shards)


def on_device(captions, images, tissue_mask, gain_self, gain_cross, gain_mlp, *rest):
    weights, cotangent = rest[:-1], rest[-1]
    n_dp, n_seq = lax.axis_size("dp"), lax.axis_size("seq")
    b, t, d = captions.shape
    patches = images.shape[1]
    start = lax.axis_index("seq") * b
    img = lax.dynamic_slice_in_dim(images, start, b, 0)
    mask = lax.dynamic_slice_in_dim(tissue_mask, start, b, 0)
    gains = jnp.stack([gain_self, gain_cross, gain_mlp], axis=1)
    if n_seq != 4 or n_dp % 2 or any(w.shape[0] % 8 for w in weights):
        return native(captions, img, mask, gains, weights, cotangent)
    nz = n_dp // 2
    more = -patches % 16
    img = jnp.pad(img, ((0, 0), (0, more), (0, 0)))
    bias = jnp.where(mask > 0, 0.0, -1e30).astype(f32)
    bias = jnp.pad(bias, ((0, -b % 8), (0, more)), constant_values=-1e30)
    gains = jnp.pad(gains, ((0, 0), (0, LANES - 3)))
    out, res, fulls = forward(nz, captions, img, bias, gains, weights)
    gx, gimg, *gw, gg = backward(nz, cotangent, img, captions, weights, res, fulls[1:])
    gimg = gimg.reshape(4 * b, patches + more, -1)[:, :patches].astype(f32)
    return (out, gx.reshape(b, t, d), gimg, gg[:, 0], gg[:, 1], gg[:, 2], *gw)


def solution(mesh):
    tok = P(BOTH, None, None)
    vec = P(BOTH)
    mat = P(BOTH, None)
    return jax.shard_map(
        on_device,
        mesh=mesh,
        in_specs=(tok, P("dp", None, None), P("dp", None), vec, vec, vec, *([mat] * 7), tok),
        out_specs=(tok, tok, P("dp", None, "seq"), vec, vec, vec, *([mat] * 7)),
        check_vma=False,
    )
```

```python
import functools

import jax
import jax.numpy as jnp
from jax import lax
from jax.experimental import pallas as pl
from jax.experimental.pallas import tpu as pltpu
from jax.sharding import PartitionSpec as P

HEADS = 12
HEAD = 64
EPS = 1e-05
BOTH = ("dp", "seq")
f32 = jnp.float32
bf16 = jnp.bfloat16
MESH = pl.DeviceIdType.MESH
HBM = pltpu.MemorySpace.HBM
VMEM = pltpu.MemorySpace.VMEM
LANES = 128


class Place:
    def __init__(self, nz, wide=False):
        dp, seq = lax.axis_index("dp"), lax.axis_index("seq")
        self.nz = nz
        self.z, self.x = dp // 2, lax.rem(dp, 2)
        self.y, self.c = seq // 2, lax.rem(seq, 2)
        x, y = self.x, self.y
        self.role = role = 1 if wide else self.c
        self.p = x + role * (y - x)
        self.s = y + role * (x - y)
        self.sib = (dp, 2 * y + (1 - self.c))
        self.p_xy = (x + (1 - role) * (1 - 2 * x), y + role * (1 - 2 * y))
        self.s_xy = (x + role * (1 - 2 * x), y + (1 - role) * (1 - 2 * y))
        self.ps_xy = (1 - x, 1 - y)
        self.p_dev = self.dev(self.z, self.p_xy)
        self.s_dev = self.dev(self.z, self.s_xy)
        self.z_of = [lax.rem(self.z + k, nz) for k in range(nz)]
        self.z_devs = [self.dev(self.z_of[k], (x, y)) for k in range(nz)]

    def dev(self, z, xy):
        return (2 * z + xy[0], 2 * xy[1] + self.c)

    def column(self, p, s):
        return p + self.role * (s - p), s + self.role * (p - s)

    def partners(self):
        return [*self.z_devs[1:], self.p_dev, self.s_dev, self.sib]


def enter(partners):
    barrier = pltpu.get_barrier_semaphore()
    for d in partners:
        pl.semaphore_signal(barrier, inc=1, device_id=d, device_id_type=MESH)
    pl.semaphore_wait(barrier, len(partners))


def remote(src, dst, sems, i, dev):
    return pltpu.make_async_remote_copy(
        src_ref=src, dst_ref=dst, send_sem=sems[0].at[i], recv_sem=sems[1].at[i],
        device_id=dev, device_id_type=MESH,
    )


class Gather:
    LOADS = (("z", 8), ("xy", 8), ("xy", 4), ("core", 8), None)
    WORK = (0.3, 0.3, 0.2, 0.2, 0.1)

    def __init__(self, here, shard, full, sems, local):
        h = here
        x, y, c = h.x, h.y, h.c
        mine = full.at[h.z, x, y, c]

        def col(xy):
            return full.at[:, xy[0], xy[1], c]

        self.own = pltpu.make_async_copy(shard, mine, local)
        nz = h.nz
        self.zs = [remote(shard, mine, sems, k - 1, h.z_devs[k]) for k in range(1, nz)]
        own, px, sx, psx = (x, y), h.p_xy, h.s_xy, h.ps_xy
        n = nz - 1
        self.p_own = remote(col(own), col(own), sems, n, h.p_dev)
        self.s_own = remote(col(own), col(own), sems, n + 1, h.s_dev)
        self.s_p = remote(col(px), col(px), sems, n + 2, h.s_dev)
        self.sibs = [
            remote(col(xy), col(xy), sems, n + 3 + i, h.sib)
            for i, xy in enumerate((own, px, sx, psx))
        ]

    @staticmethod
    def count(nz):
        return nz + 6

    def step(self, i):
        if i == 0:
            self.own.start()
            for t in self.zs:
                t.start()
        elif i == 1:
            self.own.wait()
            for t in self.zs:
                t.wait_recv()
            self.p_own.start()
            self.s_own.start()
            self.sibs[0].start()
        elif i == 2:
            self.p_own.wait_recv()
            self.s_p.start()
            self.sibs[1].start()
        elif i == 3:
            self.s_own.wait_recv()
            self.sibs[2].start()
            self.s_p.wait_recv()
            self.sibs[3].start()
        elif i == 4:
            for t in self.sibs:
                t.wait_recv()
        elif i == 5:
            for t in (*self.zs, self.p_own, self.s_own, self.s_p, *self.sibs):
                t.wait_send()


class GatherPlane(Gather):
    LOADS = (("xy", 2), ("xy", 1), ("z", 32), ("core", 12), None)

    def __init__(self, here, shard, full, sems, local):
        h = here
        x, y, c, z = h.x, h.y, h.c, h.z
        mine = full.at[z, x, y, c]
        pb = full.at[z, h.p_xy[0], h.p_xy[1], c]

        def plane(i):
            return full.at[i, :, :, c]

        self.own = pltpu.make_async_copy(shard, mine, local)
        nz = h.nz
        self.p_own = remote(shard, mine, sems, 0, h.p_dev)
        self.s_own = remote(shard, mine, sems, 1, h.s_dev)
        self.s_p = remote(pb, pb, sems, 2, h.s_dev)
        self.zs = [remote(plane(z), plane(z), sems, 2 + k, h.z_devs[k]) for k in range(1, nz)]
        self.sibs = [
            remote(plane(h.z_of[-k]), plane(h.z_of[-k]), sems, 2 + nz + k, h.sib)
            for k in range(nz)
        ]

    def step(self, i):
        if i == 0:
            self.own.start()
            self.p_own.start()
            self.s_own.start()
        elif i == 1:
            self.p_own.wait_recv()
            self.s_p.start()
        elif i == 2:
            self.own.wait()
            self.s_own.wait_recv()
            self.s_p.wait_recv()
            for t in self.zs:
                t.start()
            self.sibs[0].start()
        elif i == 3:
            for k, t in enumerate(self.zs):
                t.wait_recv()
                self.sibs[k + 1].start()
        else:
            super().step(i)


def add_blocks(count, dst, a, b):
    def body(i, _):
        dst(i)[...] = (a(i)[...].astype(f32) + b(i)[...].astype(f32)).astype(bf16)
        return 0

    lax.fori_loop(0, count, body, 0)


class Scatter:
    LOADS = (("core", 16), ("xy", 8), ("xy", 4), ("z", 8), None)
    WORK = (0.3, 1.2, 0.7, 0.4, 0.3)

    @staticmethod
    def shapes(nz, blk):
        return (nz, 2, 2, *blk), (2, nz, *blk), (nz, *blk), (nz - 1, *blk)

    @staticmethod
    def count(nz):
        return nz + 3

    def __init__(self, here, part, bufs, out, sems):
        self.h, self.out = here, out
        self.rc, self.rs, self.rp, self.rz = bufs
        h, nz = here, here.nz
        self.own = part.at[:, :, :, h.c]
        self.core = remote(part.at[:, :, :, 1 - h.c], self.rc, sems, 0, h.sib)
        self.s = [
            remote(self.rc.at[:, *h.column(p, 1 - h.s)], self.rs.at[p], sems, 1 + i, h.s_dev)
            for i, p in enumerate((1 - h.p, h.p))
        ]
        self.pp = remote(self.rs.at[1 - h.p], self.rp, sems, 3, h.p_dev)
        self.zs = [
            remote(self.rp.at[h.z_of[k]], self.rz.at[k - 1], sems, 3 + k, h.z_devs[k])
            for k in range(1, nz)
        ]

    def sum_core(self):
        at = lambda r: lambda i: r.at[lax.div(i, 4), lax.rem(lax.div(i, 2), 2), lax.rem(i, 2)]
        add_blocks(4 * self.h.nz, at(self.rc), at(self.rc), at(self.own))

    def step(self, i):
        h, nz = self.h, self.h.nz
        if i == 0:
            self.core.start()
        elif i == 1:
            self.core.wait_recv()
            self.sum_core()
            for t in self.s:
                t.start()
            self.core.wait_send()
        elif i == 2:
            for t in self.s:
                t.wait_recv()

            def kept(i):
                return self.rc.at[lax.rem(i, nz), *h.column(lax.div(i, nz), h.s)]

            mine = lambda i: self.rs.at[lax.div(i, nz), lax.rem(i, nz)]
            add_blocks(2 * nz, mine, mine, kept)
            self.pp.start()
        elif i == 3:
            self.pp.wait_recv()
            mine = lambda i: self.rp.at[i]
            add_blocks(nz, mine, mine, lambda i: self.rs.at[h.p, i])
            for t in self.zs:
                t.start()
        elif i == 4:
            for t in self.zs:
                t.wait_recv()
            total = self.rp[h.z].astype(f32)
            for k in range(nz - 1):
                total = total + self.rz[k].astype(f32)
            self.out[...] = total
        elif i == 5:
            for t in (*self.s, self.pp, *self.zs):
                t.wait_send()


class ScatterPlane(Scatter):
    LOADS = (("core", 16), ("z", 32), ("xy", 2), ("xy", 1), None)

    @staticmethod
    def shapes(nz, blk):
        return (nz, 2, 2, *blk), (nz - 1, 2, 2, *blk), (2, *blk), blk

    def __init__(self, here, part, bufs, out, sems):
        self.h, self.out = here, out
        self.rc, self.rz, self.rs, self.rp = bufs
        h, nz = here, here.nz
        self.own = part.at[:, :, :, h.c]
        self.core = remote(part.at[:, :, :, 1 - h.c], self.rc, sems, 0, h.sib)
        self.zs = [
            remote(self.rc.at[h.z_of[k]], self.rz.at[k - 1], sems, k, h.z_devs[k])
            for k in range(1, nz)
        ]
        self.s = [
            remote(self.rc.at[h.z, *h.column(p, 1 - h.s)], self.rs.at[p], sems, nz + p, h.s_dev)
            for p in range(2)
        ]
        self.pp = remote(self.rs.at[1 - h.p], self.rp, sems, nz + 2, h.p_dev)

    def step(self, i):
        h, nz = self.h, self.h.nz
        if i == 1:
            self.core.wait_recv()
            self.sum_core()
            for t in self.zs:
                t.start()
            self.core.wait_send()
        elif i == 2:
            for t in self.zs:
                t.wait_recv()

            def body(i, _):
                mine = self.rc.at[h.z, lax.div(i, 2), lax.rem(i, 2)]
                total = mine[...].astype(f32)
                for k in range(nz - 1):
                    total = total + self.rz[k, lax.div(i, 2), lax.rem(i, 2)].astype(f32)
                mine[...] = total.astype(bf16)
                return 0

            lax.fori_loop(0, 4, body, 0)
            for t in self.s:
                t.start()
        elif i == 3:
            for t in self.s:
                t.wait_recv()
            mine = lambda i: self.rs.at[i]
            add_blocks(2, mine, mine, lambda i: self.rc.at[h.z, *h.column(i, h.s)])
            self.pp.start()
        elif i == 4:
            self.pp.wait_recv()
            self.out[...] = self.rs[h.p].astype(f32) + self.rp[...].astype(f32)
        else:
            super().step(i)


class Planner:
    UNIT = {"xy": 0.8, "z": 0.8, "core": 0.1}
    HOP = 3.0

    def __init__(self, chunks, sizes):
        self.chunks, self.sizes = chunks, sizes
        self.now, self.free = 0.0, dict.fromkeys(self.UNIT, 0.0)
        self.ready, self.queue, self.arrived = {}, [], None
        self.held, self.ahead = [], 0

    def emit(self, i):
        step, when = self.ready.get(i, (0, 0.0))
        chunk, size = self.chunks[i], self.sizes[i]
        self.now = max(self.now, when) + chunk.WORK[step] * size
        chunk.step(step)
        load = chunk.LOADS[step]
        if load is None:
            del self.ready[i]
            if self.arrived:
                self.arrived(i)
            return
        if step == 1 and i + self.ahead in self.held:
            self.held.remove(i + self.ahead)
            self.emit(i + self.ahead)
        link, amount = load
        self.free[link] = max(self.free[link], self.now) + self.UNIT[link] * amount * size
        self.ready[i] = (step + 1, self.free[link] + self.HOP)

    def settle(self):
        while True:
            due = [(-s, i) for i, (s, when) in self.ready.items() if when <= self.now]
            if not due:
                return
            self.emit(min(due)[1])

    def free_slot(self, i):
        while i in self.ready and self.ready[i][0] == 1:
            self.emit(i)

    def compute(self, cost, work):
        self.settle()
        work()
        self.now += cost

    def later(self, cost, work):
        self.queue.append((cost, work))

    def finish(self):
        while self.ready or self.queue:
            self.settle()
            if self.queue:
                self.compute(*self.queue.pop(0))
            elif self.ready:
                self.emit(min(self.ready, key=lambda k: (self.ready[k][1], k)))
        for c in self.chunks:
            c.step(5)


def stats(v):
    mean = jnp.mean(v, axis=-1, keepdims=True)
    cen = v - mean
    r = lax.rsqrt(jnp.mean(cen * cen, axis=-1, keepdims=True) + EPS)
    return cen * r, r


def dot(a, b):
    return jnp.dot(a, b, preferred_element_type=f32)


def dot_nt(a, b):
    return lax.dot_general(a, b, (((1,), (1,)), ((), ())), preferred_element_type=f32)


def dot_tn(a, b):
    return lax.dot_general(a, b, (((0,), (0,)), ((), ())), preferred_element_type=f32)


def matrix(ref, lo=None, size=None):
    v = ref[...] if lo is None else ref[..., pl.ds(lo, size)]
    return v.reshape(-1, v.shape[-1])


def tiles(total, size, work):
    def body(i, _):
        work(pl.multiple_of(i * size, size))
        return 0

    lax.fori_loop(0, total // size, body, 0)


def span(start, size, unit=2 * HEAD):
    return pl.ds(pl.multiple_of(start, unit), size)


def head_lanes():
    lane = lax.broadcasted_iota(jnp.int32, (1, 2 * HEAD), 1)
    low = jnp.where(lane < HEAD, 1.0, 0.0)
    return low.astype(bf16), (1.0 - low).astype(bf16)


def softmax(s):
    e = jnp.exp(s - jnp.max(s, axis=-1, keepdims=True))
    return (e * (1.0 / jnp.sum(e, axis=-1, keepdims=True))).astype(bf16)


def pair(ref, rows, base, j):
    return ref.at[rows, pl.ds(pl.multiple_of(base + j * 2 * HEAD, 2 * HEAD), 2 * HEAD)]


SCALE = HEAD ** (-0.5)


def chunk_cols(weights, d):
    out = []
    for i, w in enumerate(weights):
        wide = d if w.shape[1] % d == 0 and i < 6 else d // 3
        out += [(i, s, wide) for s in range(0, w.shape[1], wide)]
    return out


def forward_kernel(nz, dims, chunks, *refs):
    b, t, d, kp, ff = dims
    n = len(chunks) + 1
    xs, mask, images, gsh = refs[:4]
    shards = refs[4:11]
    out = refs[11]
    res = refs[12 : 12 + N_RES]
    fulls = refs[12 + N_RES : 12 + N_RES + n]
    rest = refs[12 + N_RES + n :]
    (n1, qkv, p1, o1, x1, n2, q2, kv2, p2, o2, x2, n3, act, dg, grow, img) = keep = rest[:N_RES]
    g = rest[N_RES : N_RES + n]
    raw, mb, local, ssem, rsem, csem, isem = rest[N_RES + n :]
    here = Place(nz)
    seq = lax.axis_index("seq")
    patches = mask.shape[1]
    enter(here.partners())
    srcs = [gsh] + [shards[i].at[:, s : s + w] for i, s, w in chunks]
    gs = []
    for i in range(n):
        kind = GatherPlane if i in (11, 12) else Gather
        gs.append(kind(here, srcs[i], g[i], (ssem.at[i], rsem.at[i]), local.at[i]))
    sizes = [gsh.shape[-1] / d] + [r.shape[-1] * r.shape[-2] / (d * gsh.shape[0]) for r in g[1:]]
    plan = Planner(gs, sizes)
    plan.ahead = AHEAD
    plan.held = [i for i in range(AHEAD, n) if i not in (11, 12)]
    for i in range(n):
        if i not in plan.held:
            plan.emit(i)
    pictures = pltpu.make_async_copy(images.at[pl.ds(seq * b, b)], raw, isem.at[0])
    pictures.start()
    mb[...] = jnp.full(mb.shape, -1e30, f32)
    for i in range(b):
        row = mask[pl.ds(seq * b + i, 1), :]
        mb[i : i + 1, :patches] = jnp.where(row > 0, 0.0, -1e30)
    copies = []

    def flush(src, dst):
        cp = pltpu.make_async_copy(src, dst, csem.at[len(copies)])
        cp.start()
        copies.append(cp)

    def save(*which):
        for k in which:
            flush(keep[k], res[k])

    names = {}
    for k, (i, s, wide) in enumerate(chunks):
        names.setdefault(i, []).append(k + 1)
    lanes = head_lanes()
    heads = d // HEAD
    pairs = heads // 2
    tok = [slice(i * t, (i + 1) * t) for i in range(b)]
    pat = [slice(i * kp, (i + 1) * kp) for i in range(b)]

    def first():
        grow[...] = jnp.transpose(matrix(g[0]).astype(f32))[:8]

        def rows(r):
            h, _ = stats(xs[pl.ds(r, t)].astype(f32))
            n1[pl.ds(r, t)] = (h * grow[0:1]).astype(bf16)

        tiles(b * t, t, rows)
        save(0, 14)

    def project(src, k, dst, at):
        def tile(s):
            v = src()
            dst[:, span(at + s, 256)] = dot(v, matrix(g[k], s, 256)).astype(bf16)

        return lambda: tiles(g[k].shape[-1], 256, tile)

    def self_pairs(lo, hi):
        def body(j, _):
            causal = lax.broadcasted_iota(jnp.int32, (t, t), 0) >= lax.broadcasted_iota(
                jnp.int32, (t, t), 1
            )
            for i, r in enumerate(tok):
                q, k, v = (pair(qkv, r, m * d, j)[...] for m in range(3))
                o = jnp.zeros((t, 2 * HEAD), f32)
                for a in range(2):
                    s = dot_nt(q, k * lanes[a]) * SCALE
                    p = softmax(jnp.where(causal, s, -1e30))
                    p1[i * heads + 2 * j + a] = p
                    o = o + dot(p, v * lanes[a])
                pair(o1, r, 0, j)[...] = o.astype(bf16)
            return 0

        return lambda: lax.fori_loop(lo, hi, body, 0)

    def cross_pairs(lo, hi):
        def body(j, _):
            for i, r in enumerate(tok):
                q = pair(q2, r, 0, j)[...]
                k, v = (pair(kv2, pat[i], m * d, j)[...] for m in range(2))
                bias = mb[i : i + 1]
                o = jnp.zeros((t, 2 * HEAD), f32)
                for a in range(2):
                    p = softmax(dot_nt(q, k * lanes[a]) * SCALE + bias)
                    p2[i * heads + 2 * j + a] = p
                    o = o + dot(p, v * lanes[a])
                pair(o2, r, 0, j)[...] = o.astype(bf16)
            return 0

        return lambda: lax.fori_loop(lo, hi, body, 0)

    def residual(base, o, k, dst, row, normed):
        def rows(s):
            r = pl.ds(s, t)
            v = base[r].astype(f32) + dot(o[r], matrix(g[k]))
            dst[r] = v
            h, _ = stats(v)
            normed[r] = (h * grow[row : row + 1]).astype(bf16)

        return lambda: tiles(b * t, t, rows)

    def mlp_up(k, at):
        def tile(s):
            h = dot(n3[...], matrix(g[k], s, 256))
            cols = span(at + s, 256)
            cdf = 0.5 * (1.0 + lax.erf(h * (0.5**0.5)))
            act[:, cols] = (h * cdf).astype(bf16)
            pdf = jnp.exp(-0.5 * h * h) * (0.5 / jnp.pi) ** 0.5
            dg[:, cols] = (cdf + h * pdf).astype(bf16)

        return lambda: tiles(g[k].shape[-1], 256, tile)

    def mlp_down(k, at):
        wide = g[k].shape[-1]

        def rows(s):
            r = pl.ds(s, t)
            y = x2[r, at : at + wide] + dot(act[r], matrix(g[k]))
            out[r, at : at + wide] = y.astype(bf16)

        return lambda: tiles(b * t, t, rows)

    def images_here():
        pictures.wait()
        whole = patches // 16 * 16
        for i in range(b):
            img[i * kp : i * kp + whole] = raw[i, :whole]
            if whole < patches:
                img[i * kp + whole : (i + 1) * kp] = jnp.zeros((kp - whole, d), bf16)
                img[i * kp + whole : i * kp + patches] = raw[i, whole:]
        save(15)

    third = [(i * pairs // 3, (i + 1) * pairs // 3) for i in range(3)]

    landed = set()

    def arrived(c):
        flush(g[c], fulls[c])
        landed.add(c)
        while queued[0] in landed:
            use(queued[0])
            queued[0] += 1

    queued = [0]

    def use(c):
        add = plan.later
        if c == 0:
            add(2.0, first)
            add(0.0, images_here)
            return
        i, s, wide = chunks[c - 1]
        last = c == names[i][-1]
        if i == 0:
            add(1.7, project(lambda: n1[...], c, qkv, s))
            if last:
                add(0.0, lambda: save(1))
                for lo, hi in third:
                    add(2.5, self_pairs(lo, hi))
                add(0.0, lambda: save(2, 3))
        elif i == 1:
            add(2.5, residual(xs, o1, c, x1, 1, n2))
            add(0.0, lambda: save(4, 5))
        elif i == 2:
            add(1.7, project(lambda: n2[...], c, q2, 0))
            add(0.0, lambda: save(6))
        elif i == 3:
            add(2.5, project(lambda: img[...], c, kv2, s))
            if last:
                add(0.0, lambda: save(7))
                for lo, hi in third:
                    add(3.0, cross_pairs(lo, hi))
                add(0.0, lambda: save(8, 9))
        elif i == 4:
            add(2.5, residual(x1, o2, c, x2, 2, n3))
            add(0.0, lambda: save(10, 11))
        elif i == 5:
            add(3.5, mlp_up(c, s))
            if last:
                add(0.0, lambda: save(12, 13))
        else:
            add(2.0, mlp_down(c, s))

    plan.arrived = arrived
    plan.finish()
    for cp in copies:
        cp.wait()


N_RES = 16
AHEAD = 99


def residual_shapes(b, t, d, kp, ff):
    m, heads = b * t, d // HEAD
    S = jax.ShapeDtypeStruct
    tok, tokf = S((m, d), bf16), S((m, d), f32)
    return [
        tok, S((m, 3 * d), bf16), S((b * heads, t, t), bf16), tok, tokf, tok, tok,
        S((b * kp, 2 * d), bf16), S((b * heads, t, kp), bf16), tok, tokf, tok,
        S((m, ff), bf16), S((m, ff), bf16), S((8, d), f32), S((b * kp, d), bf16),
    ]


def forward(nz, xs, images, mask, gains, weights):
    b, t, d = xs.shape
    kp, ff = padded(images.shape[1]), weights[5].shape[1]
    chunks = chunk_cols(weights, d)
    n = len(chunks) + 1
    res = residual_shapes(b, t, d, kp, ff)
    blocks = [gains.shape] + [(weights[i].shape[0], w) for i, _, w in chunks]
    fulls = [jax.ShapeDtypeStruct((nz, 2, 2, 2, *s), bf16) for s in blocks]
    count = Gather.count(nz)
    hbm, vm = pl.BlockSpec(memory_space=HBM), pl.BlockSpec(memory_space=VMEM)
    outs = pl.pallas_call(
        functools.partial(forward_kernel, nz, (b, t, d, kp, ff), chunks),
        out_shape=[jax.ShapeDtypeStruct((b * t, d), bf16), *res, *fulls],
        in_specs=[vm, vm, *([hbm] * 9)],
        out_specs=[vm, *([hbm] * (N_RES + n))],
        scratch_shapes=[
            *(pltpu.VMEM(s.shape, s.dtype) for s in (*res, *fulls)),
            pltpu.VMEM((b, *images.shape[1:]), bf16),
            pltpu.VMEM((b + -b % 8, kp), f32),
            pltpu.SemaphoreType.DMA((n,)),
            pltpu.SemaphoreType.DMA((n, count)),
            pltpu.SemaphoreType.DMA((n, count)),
            pltpu.SemaphoreType.DMA((N_RES + n,)),
            pltpu.SemaphoreType.DMA((1,)),
        ],
        compiler_params=pltpu.CompilerParams(
            collective_id=0, has_side_effects=True, vmem_limit_bytes=60 << 20
        ),
    )(xs.reshape(b * t, d), mask, images, gains, *weights)
    return outs[0], outs[1 : 1 + N_RES], outs[1 + N_RES :]


def padded(patches):
    return patches + -patches % 16


def backward_kernel(nz, dims, chunks, *refs):
    b, t, d, kp, ff = dims
    heads = d // HEAD
    pairs = heads // 2
    m = b * t
    n_c = len(chunks)
    order = [*range(n_c - 3, n_c), *range(n_c - 7, n_c - 3), 7, 5, 6, 4, 3, None, 0, 1, 2]
    n = len(order)
    h_in = refs[: 2 + N_RES + n_c]
    h_cot, h_xs = h_in[:2]
    res = dict(zip(RES_NAMES, h_in[2 : 2 + N_RES]))
    full = h_in[2 + N_RES :]
    at = len(h_in)
    gx_out, img_out = refs[at : at + 2]
    outs = refs[at + 2 : at + 9]
    gg_out = refs[at + 9]
    rest = list(refs[at + 10 :])
    take = lambda k: [rest.pop(0) for _ in range(k)]
    cot, act, dg, n3, xf, o2, p2, q2, kv2, img, n2, o1, p1, n1, xs, grow = take(16)
    gx, gxb, go, gi, ggr = take(5)
    wd, ws = take(3), take(6)
    pd, ps, pg = take(3), take(4), take(1)[0]
    bufs = [take(4) for _ in range(n)]
    lsem, ssem, rsem, isem, jsem, osem = rest
    here, broad = Place(nz), Place(nz, wide=True)
    dp, seq = lax.axis_index("dp"), lax.axis_index("seq")
    peers = [(dp, lax.rem(seq + k, 4)) for k in range(1, 4)]

    loads, waits = {}, {}

    def load(name, src, dst):
        cp = pltpu.make_async_copy(src, dst, lsem.at[len(loads)])
        loads[name] = cp
        cp.start()

    def need(*names):
        for k in names:
            if k in loads and k not in waits:
                loads[k].wait()
                waits[k] = True

    q_at = act.at[:, : 3 * d]
    load("act", res["act"], act)
    load("cot", h_cot, cot)
    for j in range(3):
        load("wd%d" % j, full[n_c - 3 + j], wd[j])
    load("dg", res["dg"], dg)
    load("n3", res["n3"], n3)
    for j in range(4):
        load("up%d" % j, full[n_c - 7 + j], ws[j])
    load("x2", res["x2"], xf)
    load("grow", res["grow"], grow)
    for name, dst in (("o2", o2), ("p2", p2), ("q2", q2), ("kv2", kv2)):
        load(name, res[name], dst)
    load("img", res["img"], img)
    load("co", full[7], ws[4])
    load("ckv0", full[5], ws[5])
    for name, dst in (("n2", n2), ("o1", o1), ("p1", p1), ("n1", n1)):
        load(name, res[name], dst)
    load("xs", h_xs, xs)
    enter([*here.partners(), *peers])
    ggr[...] = jnp.zeros_like(ggr)

    parts, small = [], 0
    for k in order:
        if k is None:
            parts.append(pg)
        elif k >= n_c - 3:
            parts.append(pd[k - (n_c - 3)])
        else:
            parts.append(ps[small % 4])
            small += 1
    place = {k: i for i, k in enumerate(order)}
    dst = [
        gg_out if k is None else outs[chunks[k][0]].at[:, chunks[k][1] : chunks[k][1] + chunks[k][2]]
        for k in order
    ]
    sc = []
    for i in range(n):
        kind = ScatterPlane if i in PLANES else Scatter
        at = broad if i in BROAD else here
        sc.append(kind(at, parts[i], bufs[i], dst[i], (ssem.at[i], rsem.at[i])))
    sizes = [0.2 if k is None else 1.35 if k >= n_c - 3 else 1.0 for k in order]
    plan = Planner(sc, sizes)
    smalls = [i for i, k in enumerate(order) if k is not None and k < n_c - 3]

    def slot_ready(i):
        if i in smalls and smalls.index(i) >= 4:
            plan.free_slot(smalls[smalls.index(i) - 4])

    lanes = head_lanes()
    tok = [slice(i * t, (i + 1) * t) for i in range(b)]
    pat = [slice(i * kp, (i + 1) * kp) for i in range(b)]

    def grad_small(k, x, dy, first, cost):
        i = place[k]
        slot_ready(i)

        def work():
            rows = x()
            for s in range(0, d, 256):
                r = dot_tn(rows, dy[:, first + s : first + s + 256])
                parts[i][:, :, :, :, :, s : s + 256] = r.reshape(nz, 2, 2, 2, -1, 256).astype(bf16)

        plan.compute(cost, work)
        plan.emit(i)

    def grad_down(j):
        k = n_c - 3 + j
        i = place[k]
        wide = d // 3

        rows = ff // nz

        def work(z, _):
            r = dot_tn(act[:, span(z * rows, rows)], cot[:, j * wide : (j + 1) * wide])
            parts[i][z] = r.reshape(2, 2, 2, -1, wide).astype(bf16)
            return 0

        plan.compute(1.8, lambda: lax.fori_loop(0, nz, work, 0))
        plan.emit(i)

    def hidden(z):
        half, wide = ff // nz // 2, d // 3

        def work(x, _):
            g = None
            for j in range(3):
                w = wd[j][z, x].reshape(half, wide)
                term = dot_nt(cot[:, j * wide : (j + 1) * wide], w)
                g = term if g is None else g + term
            at = span((2 * z + x) * half, half)
            dg[:, at] = (g * dg[:, at].astype(f32)).astype(bf16)
            return 0

        plan.compute(1.3, lambda: lax.fori_loop(0, 2, work, 0))

    def norm_grad(src, ups, base, row, first):
        ggr[row : row + 1] = jnp.zeros((1, d), f32)

        def work(s):
            r = pl.ds(s, t)
            e = None
            for j, w in enumerate(ups):
                term = dot_nt(src[r, j * d : (j + 1) * d], matrix(w))
                e = term if e is None else e + term
            h, rs = stats(base[r].astype(f32))
            u = e * grow[row : row + 1]
            mu = jnp.mean(u, axis=-1, keepdims=True)
            mx = jnp.mean(u * h, axis=-1, keepdims=True)
            prev = cot[r].astype(f32) if first else gx[r]
            v = prev + rs * (u - mu - h * mx)
            gx[r] = v
            gxb[r] = v.astype(bf16)
            ggr[row : row + 1] += jnp.sum(e * h, axis=0, keepdims=True)

        plan.compute(1.5 + 1.2 * len(ups), lambda: tiles(m, t, work))

    def back_project(w):
        half = d // 2

        def work(s, _):
            rows = w[pl.ds(s * (nz // 2), nz // 2)].reshape(half, d)
            go[:, span(s * half, half)] = dot_nt(gxb[...], rows).astype(bf16)
            return 0

        plan.compute(1.4, lambda: lax.fori_loop(0, 2, work, 0))

    def pairs_back(lo, hi, p_ref, q_ref, q_base, kv_ref, kv_base, rows):
        def body(j, _):
            for i, r in enumerate(tok):
                rk = rows[i]
                q, g = pair(q_ref, r, q_base, j)[...], pair(go, r, 0, j)[...]
                k, v = (pair(kv_ref, rk, kv_base + x * d, j)[...] for x in range(2))
                dq = dk = dv = None
                for a in range(2):
                    lane = lanes[a]
                    pb = p_ref[i * heads + 2 * j + a]
                    p = pb.astype(f32)
                    dpr = dot_nt(g, v * lane)
                    pd = dpr * p
                    ds = ((pd - p * jnp.sum(pd, axis=-1, keepdims=True)) * SCALE).astype(bf16)
                    terms = (dot(ds, k * lane), dot_tn(ds, q * lane), dot_tn(pb, g * lane))
                    if a == 0:
                        dq, dk, dv = terms
                    else:
                        dq, dk, dv = dq + terms[0], dk + terms[1], dv + terms[2]
                pair(q_ref, r, q_base, j)[...] = dq.astype(bf16)
                pair(kv_ref, rk, kv_base, j)[...] = dk.astype(bf16)
                pair(kv_ref, rk, kv_base + d, j)[...] = dv.astype(bf16)
            return 0

        return lambda: lax.fori_loop(lo, hi, body, 0)

    thirds = [(i * pairs // 3, (i + 1) * pairs // 3) for i in range(3)]

    need("act", "cot")
    for j in range(3):
        grad_down(j)
    load("qkv", res["qkv"], q_at)
    need("wd0", "wd1", "wd2", "dg")
    for z in range(nz):
        hidden(z)
    need("n3")
    for j in range(4):
        grad_small(n_c - 7 + j, lambda: n3[...], dg, j * d, 1.4)
    need("up0", "up1", "up2", "up3", "x2", "grow")
    norm_grad(dg, ws[:4], xf, 2, True)
    load("x1", res["x1"], xf)
    load("ckv1", full[6], ws[0])
    load("cq", full[4], ws[1])
    load("so", full[3], ws[2])
    load("qkv0", full[0], ws[3])
    need("co")
    back_project(ws[4])
    load("qkv1", full[1], ws[4])
    need("o2")
    grad_small(7, lambda: o2[...], gxb, 0, 1.4)
    need("p2", "q2", "kv2")
    for lo, hi in thirds:
        plan.compute(4.0, pairs_back(lo, hi, p2, q2, 0, kv2, 0, pat))
    need("img")
    grad_small(5, lambda: img[...], kv2, 0, 2.0)
    grad_small(6, lambda: img[...], kv2, d, 2.0)
    need("ckv0", "ckv1")
    wide = d // 4

    def image_grad(i, _):
        r = span(i * kp, kp, 16)
        y = dot_nt(matrix(ws[5]), kv2[r, :d]) + dot_nt(matrix(ws[0]), kv2[r, d:])
        y = y.astype(bf16)
        for s in range(4):
            gi[s, i] = y[s * wide : (s + 1) * wide]
        return 0

    plan.compute(4.0, lambda: lax.fori_loop(0, b, image_grad, 0))
    keep = pltpu.make_async_copy(gi.at[seq], img_out.at[seq], osem.at[0])
    keep.start()
    moves = [
        remote(gi.at[lax.rem(seq + k, 4)], img_out.at[seq], (isem, jsem), k - 1, peers[k - 1])
        for k in range(1, 4)
    ]
    for mv in moves:
        mv.start()
    load("qkv2", full[2], ws[5])
    need("n2", "cq", "x1")
    norm_grad(q2, [ws[1]], xf, 1, False)
    need("so")
    back_project(ws[2])
    grad_small(4, lambda: n2[...], q2, 0, 1.4)
    need("o1")
    grad_small(3, lambda: o1[...], gxb, 0, 1.4)
    need("p1", "qkv")
    for lo, hi in thirds:
        plan.compute(3.0, pairs_back(lo, hi, p1, act, 0, act, d, tok))
    need("xs", "qkv0", "qkv1", "qkv2", "n1")
    norm_grad(act, [ws[3], ws[4], ws[5]], xs, 0, False)
    gx_copy = pltpu.make_async_copy(gx, gx_out, osem.at[1])
    gx_copy.start()

    def gain_terms():
        r = jnp.transpose(ggr[...])
        pg[...] = r.reshape(nz, 2, 2, 2, -1, LANES).astype(bf16)

    plan.compute(0.7, gain_terms)
    plan.emit(place[None])
    for j in range(3):
        grad_small(j, lambda: n1[...], act, j * d, 1.4)
    plan.finish()
    keep.wait()
    gx_copy.wait()
    for mv in moves:
        mv.wait()


PLANES = (0, 3)
BROAD = ()

RES_NAMES = (
    "n1", "qkv", "p1", "o1", "x1", "n2", "q2", "kv2",
    "p2", "o2", "x2", "n3", "act", "dg", "grow", "img",
)


def backward(nz, cot, patches, xs, weights, res, fulls):
    b, t, d = xs.shape
    kp, ff = padded(patches), weights[5].shape[1]
    m, heads = b * t, d // HEAD
    chunks = chunk_cols(weights, d)
    n_c = len(chunks)
    n = n_c + 1
    rows = weights[0].shape[0]
    down = (weights[6].shape[0], d // 3)
    tok, tokf = pltpu.VMEM((m, d), bf16), pltpu.VMEM((m, d), f32)
    part = lambda blk: pltpu.VMEM((nz, 2, 2, 2, *blk), bf16)
    blocks = [down] * 3 + [(rows, d)] * 9 + [(rows, LANES)] + [(rows, d)] * 3
    bufs = []
    for i, blk in enumerate(blocks):
        kind = ScatterPlane if i in PLANES else Scatter
        bufs += [pltpu.VMEM(s, bf16) for s in kind.shapes(nz, blk)]
    count = Scatter.count(nz)
    hbm, vm = pl.BlockSpec(memory_space=HBM), pl.BlockSpec(memory_space=VMEM)
    hid = pltpu.VMEM((m, ff), bf16)
    S = jax.ShapeDtypeStruct
    outs = pl.pallas_call(
        functools.partial(backward_kernel, nz, (b, t, d, kp, ff), chunks),
        out_shape=[
            S((m, d), f32), S((4, b, d // 4, kp), bf16),
            *(S(w.shape, f32) for w in weights), S((rows, LANES), f32),
        ],
        in_specs=[hbm] * (2 + N_RES + n_c),
        out_specs=[hbm, hbm, *([vm] * 8)],
        scratch_shapes=[
            tok, hid, hid, tok, tokf, tok, pltpu.VMEM((b * heads, t, kp), bf16), tok,
            pltpu.VMEM((b * kp, 2 * d), bf16), pltpu.VMEM((b * kp, d), bf16), tok, tok,
            pltpu.VMEM((b * heads, t, t), bf16), tok, tok, pltpu.VMEM((8, d), f32),
            tokf, tok, tok, pltpu.VMEM((4, b, d // 4, kp), bf16), pltpu.VMEM((LANES, d), f32),
            *([part(down)] * 3), *([part((rows, d))] * 6),
            *([part(down)] * 3), *([part((rows, d))] * 4), part((rows, LANES)),
            *bufs,
            pltpu.SemaphoreType.DMA((2 + N_RES + n_c,)),
            pltpu.SemaphoreType.DMA((n, count)),
            pltpu.SemaphoreType.DMA((n, count)),
            pltpu.SemaphoreType.DMA((3,)),
            pltpu.SemaphoreType.DMA((3,)),
            pltpu.SemaphoreType.DMA((2,)),
        ],
        compiler_params=pltpu.CompilerParams(
            collective_id=1, has_side_effects=True, vmem_limit_bytes=63 << 20
        ),
    )(cot.reshape(m, d), xs.reshape(m, d), *res, *fulls)
    return outs


def finish_kernel(n, *refs):
    ins, gi, gg = refs[:n], refs[n], refs[n + 1]
    outs, go, gains = refs[n + 2 : 2 * n + 2], refs[2 * n + 2], refs[2 * n + 3 : 2 * n + 6]
    held, pics, wide = refs[2 * n + 6 : 3 * n + 6], refs[3 * n + 6], refs[3 * n + 7]
    isem, osem = refs[3 * n + 8 :]
    arrive = [pltpu.make_async_copy(ins[i], held[i], isem.at[i]) for i in range(n)]
    leave = [pltpu.make_async_copy(held[i], outs[i], osem.at[i]) for i in range(n)]
    half = gi.shape[0] // 2
    parts = [pl.ds(k * half, half) for k in range(2)]
    p_in = [pltpu.make_async_copy(gi.at[r], pics.at[r], isem.at[n + k]) for k, r in enumerate(parts)]
    p_out = [pltpu.make_async_copy(wide.at[r], go.at[r], osem.at[n + k]) for k, r in enumerate(parts)]
    for cp in (*p_in, *arrive):
        cp.start()

    def widen(i, _):
        wide[i] = pics[i].astype(f32)[:, : wide.shape[2]]
        return 0

    for k in range(2):
        p_in[k].wait()
        lax.fori_loop(k * half, (k + 1) * half, widen, 0)
        p_out[k].start()
    for i in range(n):
        arrive[i].wait()
        leave[i].start()
    row = jnp.transpose(gg[...])
    for k, r in enumerate(gains):
        r[...] = row[k, : r.shape[0]]
    for cp in (*p_out, *leave):
        cp.wait()


def finish(arrays, gi, gg, patches):
    n = len(arrays)
    hbm, vm = pl.BlockSpec(memory_space=HBM), pl.BlockSpec(memory_space=VMEM)
    S = jax.ShapeDtypeStruct
    vec = S((gg.shape[0],), f32)
    return pl.pallas_call(
        functools.partial(finish_kernel, n),
        out_shape=[
            *(S(a.shape, a.dtype) for a in arrays), S((*gi.shape[:2], patches), f32), vec, vec, vec
        ],
        in_specs=[*([hbm] * (n + 1)), vm],
        out_specs=[*([hbm] * (n + 1)), vm, vm, vm],
        scratch_shapes=[
            *(pltpu.VMEM(a.shape, a.dtype) for a in arrays),
            pltpu.VMEM(gi.shape, bf16), pltpu.VMEM((*gi.shape[:2], patches), f32),
            pltpu.SemaphoreType.DMA((n + 2,)), pltpu.SemaphoreType.DMA((n + 2,)),
        ],
        compiler_params=pltpu.CompilerParams(vmem_limit_bytes=62 << 20),
    )(*arrays, gi, gg)


def norm_stats(v):
    mean = jnp.mean(v, axis=-1, keepdims=True)
    centered = v - mean
    r = lax.rsqrt(jnp.mean(centered * centered, axis=-1, keepdims=True) + EPS)
    return centered * r, r


def norm_back(xhat, r, gain, e):
    u = e * gain
    mu = jnp.mean(u, axis=-1, keepdims=True)
    mx = jnp.mean(u * xhat, axis=-1, keepdims=True)
    return r * (u - mu - xhat * mx), jnp.sum(e * xhat, axis=(0, 1))


def mm(a, b):
    return jnp.einsum("btd,de->bte", a, b, preferred_element_type=f32)


def mm_t(a, b):
    return jnp.einsum("bte,de->btd", a, b, preferred_element_type=f32)


def wgrad(a, b):
    return jnp.einsum("btd,bte->de", a, b, preferred_element_type=f32)


def split_heads(a):
    b, t, _ = a.shape
    return a.reshape(b, t, -1, HEAD)


def attend(q, k, v, allowed):
    s = jnp.einsum("bqhe,bkhe->bhqk", q, k, preferred_element_type=f32) * HEAD ** (-0.5)
    s = jnp.where(allowed, s, -1e30)
    ex = jnp.exp(s - jnp.max(s, axis=-1, keepdims=True))
    p = ex / jnp.sum(ex, axis=-1, keepdims=True)
    o = jnp.einsum("bhqk,bkhe->bqhe", p.astype(bf16), v, preferred_element_type=f32)
    return p, o.astype(bf16)


def attend_back(q, k, v, p, g):
    dp = jnp.einsum("bqhe,bkhe->bhqk", g, v, preferred_element_type=f32)
    ds = (p * (dp - jnp.sum(dp * p, axis=-1, keepdims=True)) * HEAD ** (-0.5)).astype(bf16)
    dq = jnp.einsum("bhqk,bkhe->bqhe", ds, k, preferred_element_type=f32).astype(bf16)
    dk = jnp.einsum("bhqk,bqhe->bkhe", ds, q, preferred_element_type=f32).astype(bf16)
    dv = jnp.einsum("bhqk,bqhe->bkhe", p.astype(bf16), g, preferred_element_type=f32).astype(bf16)
    return dq, dk, dv


def layer(x0, img, mask, gains, weights, cot):
    g1, g2, g3 = (g.astype(f32) for g in gains)
    w_qkv, w_so, w_cq, w_ckv, w_co, w_up, w_down = weights
    b, t, d = x0.shape
    x = x0.astype(f32)
    pos = jnp.arange(t)
    causal = (pos[:, None] >= pos[None, :])[None, None]
    allowed = (mask > 0)[:, None, None, :]
    h1, r1 = norm_stats(x)
    n1 = (h1 * g1).astype(bf16)
    qkv = mm(n1, w_qkv).astype(bf16)
    q1, k1, v1 = (split_heads(qkv[..., i * d : (i + 1) * d]) for i in range(3))
    p1, o1 = attend(q1, k1, v1, causal)
    o1 = o1.reshape(b, t, d)
    x1 = x + mm(o1, w_so)
    h2, r2 = norm_stats(x1)
    n2 = (h2 * g2).astype(bf16)
    q2 = split_heads(mm(n2, w_cq).astype(bf16))
    kv = mm(img, w_ckv).astype(bf16)
    k2, v2 = split_heads(kv[..., :d]), split_heads(kv[..., d:])
    p2, o2 = attend(q2, k2, v2, allowed)
    o2 = o2.reshape(b, t, d)
    x2 = x1 + mm(o2, w_co)
    h3, r3 = norm_stats(x2)
    n3 = (h3 * g3).astype(bf16)
    hpre = mm(n3, w_up)
    cdf = 0.5 * (1.0 + lax.erf(hpre * (0.5**0.5)))
    act = (hpre * cdf).astype(bf16)
    out = (x2 + mm(act, w_down)).astype(bf16)

    gw_down = wgrad(act, cot)
    pdf = jnp.exp(-0.5 * hpre * hpre) * (0.5 / jnp.pi) ** 0.5
    gh = (mm_t(cot, w_down) * (cdf + hpre * pdf)).astype(bf16)
    gw_up = wgrad(n3, gh)
    dx2, gg3 = norm_back(h3, r3, g3, mm_t(gh, w_up))
    gx2 = cot.astype(f32) + dx2
    gx2b = gx2.astype(bf16)
    gw_co = wgrad(o2, gx2b)
    go2 = split_heads(mm_t(gx2b, w_co).astype(bf16))
    dq2, dk2, dv2 = attend_back(q2, k2, v2, p2, go2)
    dq2 = dq2.reshape(b, t, d)
    dkv = jnp.concatenate([dk2.reshape(b, -1, d), dv2.reshape(b, -1, d)], axis=-1)
    gw_ckv = wgrad(img, dkv)
    gimg = mm_t(dkv, w_ckv).astype(bf16)
    gw_cq = wgrad(n2, dq2)
    dx1, gg2 = norm_back(h2, r2, g2, mm_t(dq2, w_cq))
    gx1 = gx2 + dx1
    gx1b = gx1.astype(bf16)
    gw_so = wgrad(o1, gx1b)
    go1 = split_heads(mm_t(gx1b, w_so).astype(bf16))
    dq1, dk1, dv1 = attend_back(q1, k1, v1, p1, go1)
    dqkv = jnp.concatenate([a.reshape(b, t, d) for a in (dq1, dk1, dv1)], axis=-1)
    gw_qkv = wgrad(n1, dqkv)
    dx0, gg1 = norm_back(h1, r1, g1, mm_t(dqkv, w_qkv))
    gx0 = gx1 + dx0
    return out, gx0, gimg, (gg1, gg2, gg3), (gw_qkv, gw_so, gw_cq, gw_ckv, gw_co, gw_up, gw_down)


def native(captions, img, mask, gains, weights, cotangent):
    full = [lax.all_gather(w, BOTH, axis=0, tiled=True) for w in weights]
    gains = lax.all_gather(gains, BOTH, axis=0, tiled=True)
    gains = tuple(gains[:, i] for i in range(3))
    out, gx0, gimg, gg, gw = layer(captions, img, mask, gains, full, cotangent)
    gg = lax.psum_scatter(jnp.stack(gg, axis=1), BOTH, scatter_dimension=0, tiled=True)
    shards = [
        lax.psum_scatter(g.astype(bf16), BOTH, scatter_dimension=0, tiled=True).astype(f32)
        for g in gw
    ]
    gimg = lax.all_to_all(gimg, "seq", split_axis=2, concat_axis=0, tiled=True)
    return (out, gx0, gimg.astype(f32), gg[:, 0], gg[:, 1], gg[:, 2], *shards)


def on_device(captions, images, tissue_mask, gain_self, gain_cross, gain_mlp, *rest):
    weights, cotangent = rest[:-1], rest[-1]
    n_dp, n_seq = lax.axis_size("dp"), lax.axis_size("seq")
    b, t, d = captions.shape
    patches = images.shape[1]
    if n_seq != 4 or n_dp % 4 or any(w.shape[0] % 8 for w in weights):
        start = lax.axis_index("seq") * b
        img = lax.dynamic_slice_in_dim(images, start, b, 0)
        mask = lax.dynamic_slice_in_dim(tissue_mask, start, b, 0)
        gains = jnp.stack([gain_self, gain_cross, gain_mlp], axis=1)
        return native(captions, img, mask, gains, weights, cotangent)
    nz = n_dp // 2
    lane = lax.broadcasted_iota(jnp.int32, (gain_self.shape[0], LANES), 1)
    gains = jnp.zeros(lane.shape, bf16)
    for i, gain in enumerate((gain_self, gain_cross, gain_mlp)):
        gains = jnp.where(lane == i, gain[:, None], gains)
    out, res, fulls = forward(nz, captions, images, tissue_mask, gains, weights)
    gx, gimg, *gw, gg = backward(nz, cotangent, patches, captions, weights, res, fulls[1:])
    gimg = gimg.reshape(4 * b, *gimg.shape[2:])
    out, gx, *gw, gimg, gs, gc, gm = finish([out, gx, *gw], gimg, gg, patches)
    out, gx = out.reshape(b, t, d), gx.reshape(b, t, d)
    return (out, gx, gimg.swapaxes(1, 2), gs, gc, gm, *gw)


def solution(mesh):
    tok = P(BOTH, None, None)
    vec = P(BOTH)
    mat = P(BOTH, None)
    return jax.shard_map(
        on_device,
        mesh=mesh,
        in_specs=(tok, P("dp", None, None), P("dp", None), vec, vec, vec, *([mat] * 7), tok),
        out_specs=(tok, tok, P("dp", None, "seq"), vec, vec, vec, *([mat] * 7)),
        check_vma=False,
    )
```

```python
import functools

import jax
import jax.numpy as jnp
from jax import lax
from jax.experimental import pallas as pl
from jax.experimental.pallas import tpu as pltpu
from jax.sharding import PartitionSpec as P

HEADS = 12
HEAD = 64
EPS = 1e-05
BOTH = ("dp", "seq")
f32 = jnp.float32
bf16 = jnp.bfloat16
MESH = pl.DeviceIdType.MESH
HBM = pltpu.MemorySpace.HBM
VMEM = pltpu.MemorySpace.VMEM
LANES = 128


class Place:
    def __init__(self, nz, wide=False):
        dp, seq = lax.axis_index("dp"), lax.axis_index("seq")
        self.nz = nz
        self.z, self.x = dp // 2, lax.rem(dp, 2)
        self.y, self.c = seq // 2, lax.rem(seq, 2)
        x, y = self.x, self.y
        self.role = role = 1 if wide else self.c
        self.p = x + role * (y - x)
        self.s = y + role * (x - y)
        self.sib = (dp, 2 * y + (1 - self.c))
        self.p_xy = (x + (1 - role) * (1 - 2 * x), y + role * (1 - 2 * y))
        self.s_xy = (x + role * (1 - 2 * x), y + (1 - role) * (1 - 2 * y))
        self.ps_xy = (1 - x, 1 - y)
        self.p_dev = self.dev(self.z, self.p_xy)
        self.s_dev = self.dev(self.z, self.s_xy)
        self.z_of = [lax.rem(self.z + k, nz) for k in range(nz)]
        self.z_devs = [self.dev(self.z_of[k], (x, y)) for k in range(nz)]

    def dev(self, z, xy):
        return (2 * z + xy[0], 2 * xy[1] + self.c)

    def column(self, p, s):
        return p + self.role * (s - p), s + self.role * (p - s)

    def partners(self):
        return [*self.z_devs[1:], self.p_dev, self.s_dev, self.sib]


def enter(partners):
    barrier = pltpu.get_barrier_semaphore()
    for d in partners:
        pl.semaphore_signal(barrier, inc=1, device_id=d, device_id_type=MESH)
    pl.semaphore_wait(barrier, len(partners))


def remote(src, dst, sems, i, dev):
    return pltpu.make_async_remote_copy(
        src_ref=src, dst_ref=dst, send_sem=sems[0].at[i], recv_sem=sems[1].at[i],
        device_id=dev, device_id_type=MESH,
    )


class Gather:
    LOADS = (("z", 8), ("xy", 8), ("xy", 4), ("core", 8), None)
    WORK = (0.3, 0.3, 0.2, 0.2, 0.1)

    def __init__(self, here, shard, full, sems, local):
        h = here
        x, y, c = h.x, h.y, h.c
        mine = full.at[h.z, x, y, c]

        def col(xy):
            return full.at[:, xy[0], xy[1], c]

        self.own = pltpu.make_async_copy(shard, mine, local)
        nz = h.nz
        self.zs = [remote(shard, mine, sems, k - 1, h.z_devs[k]) for k in range(1, nz)]
        own, px, sx, psx = (x, y), h.p_xy, h.s_xy, h.ps_xy
        n = nz - 1
        self.p_own = remote(col(own), col(own), sems, n, h.p_dev)
        self.s_own = remote(col(own), col(own), sems, n + 1, h.s_dev)
        self.s_p = remote(col(px), col(px), sems, n + 2, h.s_dev)
        self.sibs = [
            remote(col(xy), col(xy), sems, n + 3 + i, h.sib)
            for i, xy in enumerate((own, px, sx, psx))
        ]

    @staticmethod
    def count(nz):
        return nz + 6

    def step(self, i):
        if i == 0:
            self.own.start()
            for t in self.zs:
                t.start()
        elif i == 1:
            self.own.wait()
            for t in self.zs:
                t.wait_recv()
            self.p_own.start()
            self.s_own.start()
            self.sibs[0].start()
        elif i == 2:
            self.p_own.wait_recv()
            self.s_p.start()
            self.sibs[1].start()
        elif i == 3:
            self.s_own.wait_recv()
            self.sibs[2].start()
            self.s_p.wait_recv()
            self.sibs[3].start()
        elif i == 4:
            for t in self.sibs:
                t.wait_recv()
        elif i == 5:
            for t in (*self.zs, self.p_own, self.s_own, self.s_p, *self.sibs):
                t.wait_send()


class GatherPlane(Gather):
    LOADS = (("xy", 2), ("xy", 1), ("z", 32), ("core", 12), None)

    def __init__(self, here, shard, full, sems, local):
        h = here
        x, y, c, z = h.x, h.y, h.c, h.z
        mine = full.at[z, x, y, c]
        pb = full.at[z, h.p_xy[0], h.p_xy[1], c]

        def plane(i):
            return full.at[i, :, :, c]

        self.own = pltpu.make_async_copy(shard, mine, local)
        nz = h.nz
        self.p_own = remote(shard, mine, sems, 0, h.p_dev)
        self.s_own = remote(shard, mine, sems, 1, h.s_dev)
        self.s_p = remote(pb, pb, sems, 2, h.s_dev)
        self.zs = [remote(plane(z), plane(z), sems, 2 + k, h.z_devs[k]) for k in range(1, nz)]
        self.sibs = [
            remote(plane(h.z_of[-k]), plane(h.z_of[-k]), sems, 2 + nz + k, h.sib)
            for k in range(nz)
        ]

    def step(self, i):
        if i == 0:
            self.own.start()
            self.p_own.start()
            self.s_own.start()
        elif i == 1:
            self.p_own.wait_recv()
            self.s_p.start()
        elif i == 2:
            self.own.wait()
            self.s_own.wait_recv()
            self.s_p.wait_recv()
            for t in self.zs:
                t.start()
            self.sibs[0].start()
        elif i == 3:
            for k, t in enumerate(self.zs):
                t.wait_recv()
                self.sibs[k + 1].start()
        else:
            super().step(i)


def add_blocks(count, dst, a, b):
    def body(i, _):
        dst(i)[...] = (a(i)[...].astype(f32) + b(i)[...].astype(f32)).astype(bf16)
        return 0

    lax.fori_loop(0, count, body, 0)


class Scatter:
    LOADS = (("core", 16), ("xy", 8), ("xy", 4), ("z", 8), None)
    WORK = (0.3, 1.2, 0.7, 0.4, 0.3)

    @staticmethod
    def shapes(nz, blk):
        return (nz, 2, 2, *blk), (2, nz, *blk), (nz, *blk), (nz - 1, *blk)

    @staticmethod
    def count(nz):
        return nz + 3

    def __init__(self, here, part, bufs, out, sems):
        self.h, self.out = here, out
        self.rc, self.rs, self.rp, self.rz = bufs
        h, nz = here, here.nz
        self.own = part.at[:, :, :, h.c]
        self.core = remote(part.at[:, :, :, 1 - h.c], self.rc, sems, 0, h.sib)
        self.s = [
            remote(self.rc.at[:, *h.column(p, 1 - h.s)], self.rs.at[p], sems, 1 + i, h.s_dev)
            for i, p in enumerate((1 - h.p, h.p))
        ]
        self.pp = remote(self.rs.at[1 - h.p], self.rp, sems, 3, h.p_dev)
        self.zs = [
            remote(self.rp.at[h.z_of[k]], self.rz.at[k - 1], sems, 3 + k, h.z_devs[k])
            for k in range(1, nz)
        ]

    def sum_core(self):
        at = lambda r: lambda i: r.at[lax.div(i, 4), lax.rem(lax.div(i, 2), 2), lax.rem(i, 2)]
        add_blocks(4 * self.h.nz, at(self.rc), at(self.rc), at(self.own))

    def step(self, i):
        h, nz = self.h, self.h.nz
        if i == 0:
            self.core.start()
        elif i == 1:
            self.core.wait_recv()
            self.sum_core()
            for t in self.s:
                t.start()
            self.core.wait_send()
        elif i == 2:
            for t in self.s:
                t.wait_recv()

            def kept(i):
                return self.rc.at[lax.rem(i, nz), *h.column(lax.div(i, nz), h.s)]

            mine = lambda i: self.rs.at[lax.div(i, nz), lax.rem(i, nz)]
            add_blocks(2 * nz, mine, mine, kept)
            self.pp.start()
        elif i == 3:
            self.pp.wait_recv()
            mine = lambda i: self.rp.at[i]
            add_blocks(nz, mine, mine, lambda i: self.rs.at[h.p, i])
            for t in self.zs:
                t.start()
        elif i == 4:
            for t in self.zs:
                t.wait_recv()
            total = self.rp[h.z].astype(f32)
            for k in range(nz - 1):
                total = total + self.rz[k].astype(f32)
            self.out[...] = total
        elif i == 5:
            for t in (*self.s, self.pp, *self.zs):
                t.wait_send()


class ScatterPlane(Scatter):
    LOADS = (("core", 16), ("z", 32), ("xy", 2), ("xy", 1), None)

    @staticmethod
    def shapes(nz, blk):
        return (nz, 2, 2, *blk), (nz - 1, 2, 2, *blk), (2, *blk), blk

    def __init__(self, here, part, bufs, out, sems):
        self.h, self.out = here, out
        self.rc, self.rz, self.rs, self.rp = bufs
        h, nz = here, here.nz
        self.own = part.at[:, :, :, h.c]
        self.core = remote(part.at[:, :, :, 1 - h.c], self.rc, sems, 0, h.sib)
        self.zs = [
            remote(self.rc.at[h.z_of[k]], self.rz.at[k - 1], sems, k, h.z_devs[k])
            for k in range(1, nz)
        ]
        self.s = [
            remote(self.rc.at[h.z, *h.column(p, 1 - h.s)], self.rs.at[p], sems, nz + p, h.s_dev)
            for p in range(2)
        ]
        self.pp = remote(self.rs.at[1 - h.p], self.rp, sems, nz + 2, h.p_dev)

    def step(self, i):
        h, nz = self.h, self.h.nz
        if i == 1:
            self.core.wait_recv()
            self.sum_core()
            for t in self.zs:
                t.start()
            self.core.wait_send()
        elif i == 2:
            for t in self.zs:
                t.wait_recv()

            def body(i, _):
                mine = self.rc.at[h.z, lax.div(i, 2), lax.rem(i, 2)]
                total = mine[...].astype(f32)
                for k in range(nz - 1):
                    total = total + self.rz[k, lax.div(i, 2), lax.rem(i, 2)].astype(f32)
                mine[...] = total.astype(bf16)
                return 0

            lax.fori_loop(0, 4, body, 0)
            for t in self.s:
                t.start()
        elif i == 3:
            for t in self.s:
                t.wait_recv()
            mine = lambda i: self.rs.at[i]
            add_blocks(2, mine, mine, lambda i: self.rc.at[h.z, *h.column(i, h.s)])
            self.pp.start()
        elif i == 4:
            self.pp.wait_recv()
            self.out[...] = self.rs[h.p].astype(f32) + self.rp[...].astype(f32)
        else:
            super().step(i)


class Planner:
    UNIT = {"xy": 0.8, "z": 0.8, "core": 0.1}
    HOP = 3.0

    def __init__(self, chunks, sizes):
        self.chunks, self.sizes = chunks, sizes
        self.now, self.free = 0.0, dict.fromkeys(self.UNIT, 0.0)
        self.ready, self.queue, self.arrived = {}, [], None
        self.held, self.ahead = [], 0

    def emit(self, i):
        step, when = self.ready.get(i, (0, 0.0))
        chunk, size = self.chunks[i], self.sizes[i]
        self.now = max(self.now, when) + chunk.WORK[step] * size
        chunk.step(step)
        load = chunk.LOADS[step]
        if load is None:
            del self.ready[i]
            if self.arrived:
                self.arrived(i)
            return
        if step == 1 and i + self.ahead in self.held:
            self.held.remove(i + self.ahead)
            self.emit(i + self.ahead)
        link, amount = load
        self.free[link] = max(self.free[link], self.now) + self.UNIT[link] * amount * size
        self.ready[i] = (step + 1, self.free[link] + self.HOP)

    def settle(self):
        while True:
            due = [(-s, i) for i, (s, when) in self.ready.items() if when <= self.now]
            if not due:
                return
            self.emit(min(due)[1])

    def free_slot(self, i):
        while i in self.ready and self.ready[i][0] == 1:
            self.emit(i)

    def compute(self, cost, work):
        self.settle()
        work()
        self.now += cost

    def later(self, cost, work):
        self.queue.append((cost, work))

    def finish(self):
        while self.ready or self.queue:
            self.settle()
            if self.queue:
                self.compute(*self.queue.pop(0))
            elif self.ready:
                self.emit(min(self.ready, key=lambda k: (self.ready[k][1], k)))
        for c in self.chunks:
            c.step(5)


def stats(v):
    mean = jnp.mean(v, axis=-1, keepdims=True)
    cen = v - mean
    r = lax.rsqrt(jnp.mean(cen * cen, axis=-1, keepdims=True) + EPS)
    return cen * r, r


def dot(a, b):
    return jnp.dot(a, b, preferred_element_type=f32)


def dot_nt(a, b):
    return lax.dot_general(a, b, (((1,), (1,)), ((), ())), preferred_element_type=f32)


def dot_tn(a, b):
    return lax.dot_general(a, b, (((0,), (0,)), ((), ())), preferred_element_type=f32)


def matrix(ref, lo=None, size=None):
    v = ref[...] if lo is None else ref[..., pl.ds(lo, size)]
    return v.reshape(-1, v.shape[-1])


def tiles(total, size, work):
    def body(i, _):
        work(pl.multiple_of(i * size, size))
        return 0

    lax.fori_loop(0, total // size, body, 0)


def span(start, size, unit=2 * HEAD):
    return pl.ds(pl.multiple_of(start, unit), size)


def head_lanes():
    lane = lax.broadcasted_iota(jnp.int32, (1, 2 * HEAD), 1)
    low = jnp.where(lane < HEAD, 1.0, 0.0)
    return low.astype(bf16), (1.0 - low).astype(bf16)


def softmax(s):
    e = jnp.exp(s - jnp.max(s, axis=-1, keepdims=True))
    return (e * (1.0 / jnp.sum(e, axis=-1, keepdims=True))).astype(bf16)


def pair(ref, rows, base, j):
    return ref.at[rows, pl.ds(pl.multiple_of(base + j * 2 * HEAD, 2 * HEAD), 2 * HEAD)]


SCALE = HEAD ** (-0.5)


def chunk_cols(weights, d):
    out = []
    for i, w in enumerate(weights):
        wide = d if w.shape[1] % d == 0 and i < 6 else d // 3
        out += [(i, s, wide) for s in range(0, w.shape[1], wide)]
    return out


def forward_kernel(nz, dims, chunks, *refs):
    b, t, d, kp, ff = dims
    n = len(chunks) + 1
    xs, mask = refs[:2]
    gains = refs[2:5]
    images = refs[5]
    shards = refs[6:13]
    out = refs[13]
    res = refs[14 : 14 + N_RES]
    fulls = refs[14 + N_RES : 14 + N_RES + n]
    rest = refs[14 + N_RES + n :]
    (n1, qkv, p1, o1, x1, n2, q2, kv2, p2, o2, x2, n3, act, dg, grow, img) = keep = rest[:N_RES]
    g = rest[N_RES : N_RES + n]
    raw, mb, gsh, turn, local, ssem, rsem, csem, isem = rest[N_RES + n :]
    here = Place(nz)
    seq = lax.axis_index("seq")
    patches = mask.shape[1]
    turn[...] = jnp.zeros(turn.shape, f32)
    for i, gain in enumerate(gains):
        turn[i : i + 1, : gain.shape[0]] = gain[...].astype(f32).reshape(1, -1)
    gsh[...] = jnp.zeros(gsh.shape, bf16)
    gsh[:, :8] = jnp.transpose(turn[...])[: gsh.shape[0]].astype(bf16)
    enter(here.partners())
    srcs = [gsh] + [shards[i].at[:, s : s + w] for i, s, w in chunks]
    gs = []
    for i in range(n):
        kind = GatherPlane if i in (11, 12) else Gather
        gs.append(kind(here, srcs[i], g[i], (ssem.at[i], rsem.at[i]), local.at[i]))
    sizes = [gsh.shape[-1] / d] + [r.shape[-1] * r.shape[-2] / (d * gsh.shape[0]) for r in g[1:]]
    plan = Planner(gs, sizes)
    plan.ahead = AHEAD
    plan.held = [i for i in range(AHEAD, n) if i not in (11, 12)]
    for i in range(n):
        if i not in plan.held:
            plan.emit(i)
    pictures = pltpu.make_async_copy(images.at[pl.ds(seq * b, b)], raw, isem.at[0])
    pictures.start()
    mb[...] = jnp.full(mb.shape, -1e30, f32)
    for i in range(b):
        row = mask[pl.ds(seq * b + i, 1), :]
        mb[i : i + 1, :patches] = jnp.where(row > 0, 0.0, -1e30)
    copies = []

    def flush(src, dst):
        cp = pltpu.make_async_copy(src, dst, csem.at[len(copies)])
        cp.start()
        copies.append(cp)

    def save(*which):
        for k in which:
            flush(keep[k], res[k])

    names = {}
    for k, (i, s, wide) in enumerate(chunks):
        names.setdefault(i, []).append(k + 1)
    lanes = head_lanes()
    heads = d // HEAD
    pairs = heads // 2
    tok = [slice(i * t, (i + 1) * t) for i in range(b)]
    pat = [slice(i * kp, (i + 1) * kp) for i in range(b)]

    def first():
        grow[...] = jnp.transpose(matrix(g[0]).astype(f32))[:8]

        def rows(r):
            h, _ = stats(xs[pl.ds(r, t)].astype(f32))
            n1[pl.ds(r, t)] = (h * grow[0:1]).astype(bf16)

        tiles(b * t, t, rows)
        save(0, 14)

    def project(src, k, dst, at):
        def tile(s):
            v = src()
            dst[:, span(at + s, 256)] = dot(v, matrix(g[k], s, 256)).astype(bf16)

        return lambda: tiles(g[k].shape[-1], 256, tile)

    def self_pairs(lo, hi):
        def body(j, _):
            causal = lax.broadcasted_iota(jnp.int32, (t, t), 0) >= lax.broadcasted_iota(
                jnp.int32, (t, t), 1
            )
            for i, r in enumerate(tok):
                q, k, v = (pair(qkv, r, m * d, j)[...] for m in range(3))
                o = jnp.zeros((t, 2 * HEAD), f32)
                for a in range(2):
                    s = dot_nt(q, k * lanes[a]) * SCALE
                    p = softmax(jnp.where(causal, s, -1e30))
                    p1[i * heads + 2 * j + a] = p
                    o = o + dot(p, v * lanes[a])
                pair(o1, r, 0, j)[...] = o.astype(bf16)
            return 0

        return lambda: lax.fori_loop(lo, hi, body, 0)

    def cross_pairs(lo, hi):
        def body(j, _):
            for i, r in enumerate(tok):
                q = pair(q2, r, 0, j)[...]
                k, v = (pair(kv2, pat[i], m * d, j)[...] for m in range(2))
                bias = mb[i : i + 1]
                o = jnp.zeros((t, 2 * HEAD), f32)
                for a in range(2):
                    p = softmax(dot_nt(q, k * lanes[a]) * SCALE + bias)
                    p2[i * heads + 2 * j + a] = p
                    o = o + dot(p, v * lanes[a])
                pair(o2, r, 0, j)[...] = o.astype(bf16)
            return 0

        return lambda: lax.fori_loop(lo, hi, body, 0)

    def residual(base, o, k, dst, row, normed):
        def rows(s):
            r = pl.ds(s, t)
            v = base[r].astype(f32) + dot(o[r], matrix(g[k]))
            dst[r] = v
            h, _ = stats(v)
            normed[r] = (h * grow[row : row + 1]).astype(bf16)

        return lambda: tiles(b * t, t, rows)

    def mlp_up(k, at):
        def tile(s):
            h = dot(n3[...], matrix(g[k], s, 256))
            cols = span(at + s, 256)
            cdf = 0.5 * (1.0 + lax.erf(h * (0.5**0.5)))
            act[:, cols] = (h * cdf).astype(bf16)
            pdf = jnp.exp(-0.5 * h * h) * (0.5 / jnp.pi) ** 0.5
            dg[:, cols] = (cdf + h * pdf).astype(bf16)

        return lambda: tiles(g[k].shape[-1], 256, tile)

    def mlp_down(k, at):
        wide = g[k].shape[-1]

        def rows(s):
            r = pl.ds(s, t)
            y = x2[r, at : at + wide] + dot(act[r], matrix(g[k]))
            out[r, at : at + wide] = y.astype(bf16)

        return lambda: tiles(b * t, t, rows)

    def images_here():
        pictures.wait()
        whole = patches // 16 * 16
        for i in range(b):
            img[i * kp : i * kp + whole] = raw[i, :whole]
            if whole < patches:
                img[i * kp + whole : (i + 1) * kp] = jnp.zeros((kp - whole, d), bf16)
                img[i * kp + whole : i * kp + patches] = raw[i, whole:]
        save(15)

    third = [(i * pairs // 3, (i + 1) * pairs // 3) for i in range(3)]

    landed = set()

    def arrived(c):
        flush(g[c], fulls[c])
        landed.add(c)
        while queued[0] in landed:
            use(queued[0])
            queued[0] += 1

    queued = [0]

    def use(c):
        add = plan.later
        if c == 0:
            add(2.0, first)
            add(0.0, images_here)
            return
        i, s, wide = chunks[c - 1]
        last = c == names[i][-1]
        if i == 0:
            add(1.7, project(lambda: n1[...], c, qkv, s))
            if last:
                add(0.0, lambda: save(1))
                for lo, hi in third:
                    add(2.5, self_pairs(lo, hi))
                add(0.0, lambda: save(2, 3))
        elif i == 1:
            add(2.5, residual(xs, o1, c, x1, 1, n2))
            add(0.0, lambda: save(4, 5))
        elif i == 2:
            add(1.7, project(lambda: n2[...], c, q2, 0))
            add(0.0, lambda: save(6))
        elif i == 3:
            add(2.5, project(lambda: img[...], c, kv2, s))
            if last:
                add(0.0, lambda: save(7))
                for lo, hi in third:
                    add(3.0, cross_pairs(lo, hi))
                add(0.0, lambda: save(8, 9))
        elif i == 4:
            add(2.5, residual(x1, o2, c, x2, 2, n3))
            add(0.0, lambda: save(10, 11))
        elif i == 5:
            add(3.5, mlp_up(c, s))
            if last:
                add(0.0, lambda: save(12, 13))
        else:
            add(2.0, mlp_down(c, s))

    plan.arrived = arrived
    plan.finish()
    for cp in copies:
        cp.wait()


N_RES = 16
AHEAD = 99


def residual_shapes(b, t, d, kp, ff):
    m, heads = b * t, d // HEAD
    S = jax.ShapeDtypeStruct
    tok, tokf = S((m, d), bf16), S((m, d), f32)
    return [
        tok, S((m, 3 * d), bf16), S((b * heads, t, t), bf16), tok, tokf, tok, tok,
        S((b * kp, 2 * d), bf16), S((b * heads, t, kp), bf16), tok, tokf, tok,
        S((m, ff), bf16), S((m, ff), bf16), S((8, d), f32), S((b * kp, d), bf16),
    ]


def forward(nz, xs, images, mask, gains, weights):
    b, t, d = xs.shape
    kp, ff = padded(images.shape[1]), weights[5].shape[1]
    chunks = chunk_cols(weights, d)
    n = len(chunks) + 1
    res = residual_shapes(b, t, d, kp, ff)
    block = (weights[0].shape[0], LANES)
    blocks = [block] + [(weights[i].shape[0], w) for i, _, w in chunks]
    fulls = [jax.ShapeDtypeStruct((nz, 2, 2, 2, *s), bf16) for s in blocks]
    count = Gather.count(nz)
    hbm, vm = pl.BlockSpec(memory_space=HBM), pl.BlockSpec(memory_space=VMEM)
    outs = pl.pallas_call(
        functools.partial(forward_kernel, nz, (b, t, d, kp, ff), chunks),
        out_shape=[jax.ShapeDtypeStruct((b * t, d), bf16), *res, *fulls],
        in_specs=[*([vm] * 5), *([hbm] * 8)],
        out_specs=[vm, *([hbm] * (N_RES + n))],
        scratch_shapes=[
            *(pltpu.VMEM(s.shape, s.dtype) for s in (*res, *fulls)),
            pltpu.VMEM((b, *images.shape[1:]), bf16),
            pltpu.VMEM((b + -b % 8, kp), f32),
            pltpu.VMEM(block, bf16),
            pltpu.VMEM((8, LANES), f32),
            pltpu.SemaphoreType.DMA((n,)),
            pltpu.SemaphoreType.DMA((n, count)),
            pltpu.SemaphoreType.DMA((n, count)),
            pltpu.SemaphoreType.DMA((N_RES + n,)),
            pltpu.SemaphoreType.DMA((1,)),
        ],
        compiler_params=pltpu.CompilerParams(
            collective_id=0, has_side_effects=True, vmem_limit_bytes=60 << 20
        ),
    )(xs.reshape(b * t, d), mask, *gains, images, *weights)
    return outs[0], outs[1 : 1 + N_RES], outs[1 + N_RES :]


def padded(patches):
    return patches + -patches % 16


def backward_kernel(nz, dims, chunks, *refs):
    b, t, d, kp, ff = dims
    heads = d // HEAD
    pairs = heads // 2
    m = b * t
    n_c = len(chunks)
    order = [*range(n_c - 3, n_c), *range(n_c - 7, n_c - 3), 7, 5, 6, 4, 3, None, 0, 1, 2]
    n = len(order)
    h_in = refs[: 2 + N_RES + n_c]
    h_cot, h_xs = h_in[:2]
    res = dict(zip(RES_NAMES, h_in[2 : 2 + N_RES]))
    full = h_in[2 + N_RES :]
    at = len(h_in)
    gx_out, img_out = refs[at : at + 2]
    outs = refs[at + 2 : at + 9]
    gg_out = refs[at + 9]
    rest = list(refs[at + 10 :])
    take = lambda k: [rest.pop(0) for _ in range(k)]
    cot, act, dg, n3, xf, o2, p2, q2, kv2, img, n2, o1, p1, n1, xs, grow = take(16)
    gx, gxb, go, gi, ggr = take(5)
    wd, ws = take(3), take(6)
    pd, ps, pg = take(3), take(4), take(1)[0]
    bufs = [take(4) for _ in range(n)]
    lsem, ssem, rsem, isem, jsem, osem = rest
    here, broad = Place(nz), Place(nz, wide=True)
    dp, seq = lax.axis_index("dp"), lax.axis_index("seq")
    peers = [(dp, lax.rem(seq + k, 4)) for k in range(1, 4)]

    loads, waits = {}, {}

    def load(name, src, dst):
        cp = pltpu.make_async_copy(src, dst, lsem.at[len(loads)])
        loads[name] = cp
        cp.start()

    def need(*names):
        for k in names:
            if k in loads and k not in waits:
                loads[k].wait()
                waits[k] = True

    q_at = act.at[:, : 3 * d]
    load("act", res["act"], act)
    load("cot", h_cot, cot)
    for j in range(3):
        load("wd%d" % j, full[n_c - 3 + j], wd[j])
    load("dg", res["dg"], dg)
    load("n3", res["n3"], n3)
    for j in range(4):
        load("up%d" % j, full[n_c - 7 + j], ws[j])
    load("x2", res["x2"], xf)
    load("grow", res["grow"], grow)
    for name, dst in (("o2", o2), ("p2", p2), ("q2", q2), ("kv2", kv2)):
        load(name, res[name], dst)
    load("img", res["img"], img)
    load("co", full[7], ws[4])
    load("ckv0", full[5], ws[5])
    for name, dst in (("n2", n2), ("o1", o1), ("p1", p1), ("n1", n1)):
        load(name, res[name], dst)
    load("xs", h_xs, xs)
    enter([*here.partners(), *peers])
    ggr[...] = jnp.zeros_like(ggr)

    parts, small = [], 0
    for k in order:
        if k is None:
            parts.append(pg)
        elif k >= n_c - 3:
            parts.append(pd[k - (n_c - 3)])
        else:
            parts.append(ps[small % 4])
            small += 1
    place = {k: i for i, k in enumerate(order)}
    dst = [
        gg_out if k is None else outs[chunks[k][0]].at[:, chunks[k][1] : chunks[k][1] + chunks[k][2]]
        for k in order
    ]
    sc = []
    for i in range(n):
        kind = ScatterPlane if i in PLANES else Scatter
        at = broad if i in BROAD else here
        sc.append(kind(at, parts[i], bufs[i], dst[i], (ssem.at[i], rsem.at[i])))
    sizes = [0.2 if k is None else 1.35 if k >= n_c - 3 else 1.0 for k in order]
    plan = Planner(sc, sizes)
    smalls = [i for i, k in enumerate(order) if k is not None and k < n_c - 3]

    def slot_ready(i):
        if i in smalls and smalls.index(i) >= 4:
            plan.free_slot(smalls[smalls.index(i) - 4])

    lanes = head_lanes()
    tok = [slice(i * t, (i + 1) * t) for i in range(b)]
    pat = [slice(i * kp, (i + 1) * kp) for i in range(b)]

    def grad_small(k, x, dy, first, cost):
        i = place[k]
        slot_ready(i)

        def work():
            rows = x()
            for s in range(0, d, 256):
                r = dot_tn(rows, dy[:, first + s : first + s + 256])
                parts[i][:, :, :, :, :, s : s + 256] = r.reshape(nz, 2, 2, 2, -1, 256).astype(bf16)

        plan.compute(cost, work)
        plan.emit(i)

    def grad_down(j):
        k = n_c - 3 + j
        i = place[k]
        wide = d // 3

        rows = ff // nz

        def work(z, _):
            r = dot_tn(act[:, span(z * rows, rows)], cot[:, j * wide : (j + 1) * wide])
            parts[i][z] = r.reshape(2, 2, 2, -1, wide).astype(bf16)
            return 0

        plan.compute(1.8, lambda: lax.fori_loop(0, nz, work, 0))
        plan.emit(i)

    def hidden(z):
        half, wide = ff // nz // 2, d // 3

        def work(x, _):
            g = None
            for j in range(3):
                w = wd[j][z, x].reshape(half, wide)
                term = dot_nt(cot[:, j * wide : (j + 1) * wide], w)
                g = term if g is None else g + term
            at = span((2 * z + x) * half, half)
            dg[:, at] = (g * dg[:, at].astype(f32)).astype(bf16)
            return 0

        plan.compute(1.3, lambda: lax.fori_loop(0, 2, work, 0))

    def norm_grad(src, ups, base, row, first):
        ggr[row : row + 1] = jnp.zeros((1, d), f32)

        def work(s):
            r = pl.ds(s, t)
            e = None
            for j, w in enumerate(ups):
                term = dot_nt(src[r, j * d : (j + 1) * d], matrix(w))
                e = term if e is None else e + term
            h, rs = stats(base[r].astype(f32))
            u = e * grow[row : row + 1]
            mu = jnp.mean(u, axis=-1, keepdims=True)
            mx = jnp.mean(u * h, axis=-1, keepdims=True)
            prev = cot[r].astype(f32) if first else gx[r]
            v = prev + rs * (u - mu - h * mx)
            gx[r] = v
            gxb[r] = v.astype(bf16)
            ggr[row : row + 1] += jnp.sum(e * h, axis=0, keepdims=True)

        plan.compute(1.5 + 1.2 * len(ups), lambda: tiles(m, t, work))

    def back_project(w):
        half = d // 2

        def work(s, _):
            rows = w[pl.ds(s * (nz // 2), nz // 2)].reshape(half, d)
            go[:, span(s * half, half)] = dot_nt(gxb[...], rows).astype(bf16)
            return 0

        plan.compute(1.4, lambda: lax.fori_loop(0, 2, work, 0))

    def pairs_back(lo, hi, p_ref, q_ref, q_base, kv_ref, kv_base, rows):
        def body(j, _):
            for i, r in enumerate(tok):
                rk = rows[i]
                q, g = pair(q_ref, r, q_base, j)[...], pair(go, r, 0, j)[...]
                k, v = (pair(kv_ref, rk, kv_base + x * d, j)[...] for x in range(2))
                dq = dk = dv = None
                for a in range(2):
                    lane = lanes[a]
                    pb = p_ref[i * heads + 2 * j + a]
                    p = pb.astype(f32)
                    dpr = dot_nt(g, v * lane)
                    pd = dpr * p
                    ds = ((pd - p * jnp.sum(pd, axis=-1, keepdims=True)) * SCALE).astype(bf16)
                    terms = (dot(ds, k * lane), dot_tn(ds, q * lane), dot_tn(pb, g * lane))
                    if a == 0:
                        dq, dk, dv = terms
                    else:
                        dq, dk, dv = dq + terms[0], dk + terms[1], dv + terms[2]
                pair(q_ref, r, q_base, j)[...] = dq.astype(bf16)
                pair(kv_ref, rk, kv_base, j)[...] = dk.astype(bf16)
                pair(kv_ref, rk, kv_base + d, j)[...] = dv.astype(bf16)
            return 0

        return lambda: lax.fori_loop(lo, hi, body, 0)

    thirds = [(i * pairs // 3, (i + 1) * pairs // 3) for i in range(3)]

    need("act", "cot")
    for j in range(3):
        grad_down(j)
    load("qkv", res["qkv"], q_at)
    need("wd0", "wd1", "wd2", "dg")
    for z in range(nz):
        hidden(z)
    need("n3")
    for j in range(4):
        grad_small(n_c - 7 + j, lambda: n3[...], dg, j * d, 1.4)
    need("up0", "up1", "up2", "up3", "x2", "grow")
    norm_grad(dg, ws[:4], xf, 2, True)
    load("x1", res["x1"], xf)
    load("ckv1", full[6], ws[0])
    load("cq", full[4], ws[1])
    load("so", full[3], ws[2])
    load("qkv0", full[0], ws[3])
    need("co")
    back_project(ws[4])
    load("qkv1", full[1], ws[4])
    need("o2")
    grad_small(7, lambda: o2[...], gxb, 0, 1.4)
    need("p2", "q2", "kv2")
    for lo, hi in thirds:
        plan.compute(4.0, pairs_back(lo, hi, p2, q2, 0, kv2, 0, pat))
    need("img")
    grad_small(5, lambda: img[...], kv2, 0, 2.0)
    grad_small(6, lambda: img[...], kv2, d, 2.0)
    need("ckv0", "ckv1")
    wide = d // 4

    def image_grad(i, _):
        r = span(i * kp, kp, 16)
        y = dot_nt(matrix(ws[5]), kv2[r, :d]) + dot_nt(matrix(ws[0]), kv2[r, d:])
        y = y.astype(bf16)
        for s in range(4):
            gi[s, i] = y[s * wide : (s + 1) * wide]
        return 0

    plan.compute(4.0, lambda: lax.fori_loop(0, b, image_grad, 0))
    keep = pltpu.make_async_copy(gi.at[seq], img_out.at[seq], osem.at[0])
    keep.start()
    moves = [
        remote(gi.at[lax.rem(seq + k, 4)], img_out.at[seq], (isem, jsem), k - 1, peers[k - 1])
        for k in range(1, 4)
    ]
    for mv in moves:
        mv.start()
    load("qkv2", full[2], ws[5])
    need("n2", "cq", "x1")
    norm_grad(q2, [ws[1]], xf, 1, False)
    need("so")
    back_project(ws[2])
    grad_small(4, lambda: n2[...], q2, 0, 1.4)
    need("o1")
    grad_small(3, lambda: o1[...], gxb, 0, 1.4)
    need("p1", "qkv")
    for lo, hi in thirds:
        plan.compute(3.0, pairs_back(lo, hi, p1, act, 0, act, d, tok))
    need("xs", "qkv0", "qkv1", "qkv2", "n1")
    norm_grad(act, [ws[3], ws[4], ws[5]], xs, 0, False)
    gx_copy = pltpu.make_async_copy(gx, gx_out, osem.at[1])
    gx_copy.start()

    def gain_terms():
        r = jnp.transpose(ggr[...])
        pg[...] = r.reshape(nz, 2, 2, 2, -1, LANES).astype(bf16)

    plan.compute(0.7, gain_terms)
    plan.emit(place[None])
    for j in range(3):
        grad_small(j, lambda: n1[...], act, j * d, 1.4)
    plan.finish()
    keep.wait()
    gx_copy.wait()
    for mv in moves:
        mv.wait()


PLANES = (0, 3)
BROAD = (8, 9, 10, 11)

RES_NAMES = (
    "n1", "qkv", "p1", "o1", "x1", "n2", "q2", "kv2",
    "p2", "o2", "x2", "n3", "act", "dg", "grow", "img",
)


def backward(nz, cot, patches, xs, weights, res, fulls):
    b, t, d = xs.shape
    kp, ff = padded(patches), weights[5].shape[1]
    m, heads = b * t, d // HEAD
    chunks = chunk_cols(weights, d)
    n_c = len(chunks)
    n = n_c + 1
    rows = weights[0].shape[0]
    down = (weights[6].shape[0], d // 3)
    tok, tokf = pltpu.VMEM((m, d), bf16), pltpu.VMEM((m, d), f32)
    part = lambda blk: pltpu.VMEM((nz, 2, 2, 2, *blk), bf16)
    blocks = [down] * 3 + [(rows, d)] * 9 + [(rows, LANES)] + [(rows, d)] * 3
    bufs = []
    for i, blk in enumerate(blocks):
        kind = ScatterPlane if i in PLANES else Scatter
        bufs += [pltpu.VMEM(s, bf16) for s in kind.shapes(nz, blk)]
    count = Scatter.count(nz)
    hbm, vm = pl.BlockSpec(memory_space=HBM), pl.BlockSpec(memory_space=VMEM)
    hid = pltpu.VMEM((m, ff), bf16)
    S = jax.ShapeDtypeStruct
    outs = pl.pallas_call(
        functools.partial(backward_kernel, nz, (b, t, d, kp, ff), chunks),
        out_shape=[
            S((m, d), f32), S((4, b, d // 4, kp), bf16),
            *(S(w.shape, f32) for w in weights), S((rows, LANES), f32),
        ],
        in_specs=[hbm] * (2 + N_RES + n_c),
        out_specs=[hbm, hbm, *([vm] * 8)],
        scratch_shapes=[
            tok, hid, hid, tok, tokf, tok, pltpu.VMEM((b * heads, t, kp), bf16), tok,
            pltpu.VMEM((b * kp, 2 * d), bf16), pltpu.VMEM((b * kp, d), bf16), tok, tok,
            pltpu.VMEM((b * heads, t, t), bf16), tok, tok, pltpu.VMEM((8, d), f32),
            tokf, tok, tok, pltpu.VMEM((4, b, d // 4, kp), bf16), pltpu.VMEM((LANES, d), f32),
            *([part(down)] * 3), *([part((rows, d))] * 6),
            *([part(down)] * 3), *([part((rows, d))] * 4), part((rows, LANES)),
            *bufs,
            pltpu.SemaphoreType.DMA((2 + N_RES + n_c,)),
            pltpu.SemaphoreType.DMA((n, count)),
            pltpu.SemaphoreType.DMA((n, count)),
            pltpu.SemaphoreType.DMA((3,)),
            pltpu.SemaphoreType.DMA((3,)),
            pltpu.SemaphoreType.DMA((2,)),
        ],
        compiler_params=pltpu.CompilerParams(
            collective_id=1, has_side_effects=True, vmem_limit_bytes=63 << 20
        ),
    )(cot.reshape(m, d), xs.reshape(m, d), *res, *fulls)
    return outs


def finish_kernel(n, *refs):
    ins, gi, gg = refs[:n], refs[n], refs[n + 1]
    outs, go, gains = refs[n + 2 : 2 * n + 2], refs[2 * n + 2], refs[2 * n + 3 : 2 * n + 6]
    held, pics, wide = refs[2 * n + 6 : 3 * n + 6], refs[3 * n + 6], refs[3 * n + 7]
    isem, osem = refs[3 * n + 8 :]
    arrive = [pltpu.make_async_copy(ins[i], held[i], isem.at[i]) for i in range(n)]
    leave = [pltpu.make_async_copy(held[i], outs[i], osem.at[i]) for i in range(n)]
    half = gi.shape[0] // 2
    parts = [pl.ds(k * half, half) for k in range(2)]
    p_in = [pltpu.make_async_copy(gi.at[r], pics.at[r], isem.at[n + k]) for k, r in enumerate(parts)]
    p_out = [pltpu.make_async_copy(wide.at[r], go.at[r], osem.at[n + k]) for k, r in enumerate(parts)]
    for cp in (*p_in, *arrive):
        cp.start()

    def widen(i, _):
        wide[i] = pics[i].astype(f32)[:, : wide.shape[2]]
        return 0

    for k in range(2):
        p_in[k].wait()
        lax.fori_loop(k * half, (k + 1) * half, widen, 0)
        p_out[k].start()
    for i in range(n):
        arrive[i].wait()
        leave[i].start()
    row = jnp.transpose(gg[...])
    for k, r in enumerate(gains):
        r[...] = row[k, : r.shape[0]]
    for cp in (*p_out, *leave):
        cp.wait()


def finish(arrays, gi, gg, patches):
    n = len(arrays)
    hbm, vm = pl.BlockSpec(memory_space=HBM), pl.BlockSpec(memory_space=VMEM)
    S = jax.ShapeDtypeStruct
    vec = S((gg.shape[0],), f32)
    return pl.pallas_call(
        functools.partial(finish_kernel, n),
        out_shape=[
            *(S(a.shape, a.dtype) for a in arrays), S((*gi.shape[:2], patches), f32), vec, vec, vec
        ],
        in_specs=[*([hbm] * (n + 1)), vm],
        out_specs=[*([hbm] * (n + 1)), vm, vm, vm],
        scratch_shapes=[
            *(pltpu.VMEM(a.shape, a.dtype) for a in arrays),
            pltpu.VMEM(gi.shape, bf16), pltpu.VMEM((*gi.shape[:2], patches), f32),
            pltpu.SemaphoreType.DMA((n + 2,)), pltpu.SemaphoreType.DMA((n + 2,)),
        ],
        compiler_params=pltpu.CompilerParams(vmem_limit_bytes=62 << 20),
    )(*arrays, gi, gg)


def norm_stats(v):
    mean = jnp.mean(v, axis=-1, keepdims=True)
    centered = v - mean
    r = lax.rsqrt(jnp.mean(centered * centered, axis=-1, keepdims=True) + EPS)
    return centered * r, r


def norm_back(xhat, r, gain, e):
    u = e * gain
    mu = jnp.mean(u, axis=-1, keepdims=True)
    mx = jnp.mean(u * xhat, axis=-1, keepdims=True)
    return r * (u - mu - xhat * mx), jnp.sum(e * xhat, axis=(0, 1))


def mm(a, b):
    return jnp.einsum("btd,de->bte", a, b, preferred_element_type=f32)


def mm_t(a, b):
    return jnp.einsum("bte,de->btd", a, b, preferred_element_type=f32)


def wgrad(a, b):
    return jnp.einsum("btd,bte->de", a, b, preferred_element_type=f32)


def split_heads(a):
    b, t, _ = a.shape
    return a.reshape(b, t, -1, HEAD)


def attend(q, k, v, allowed):
    s = jnp.einsum("bqhe,bkhe->bhqk", q, k, preferred_element_type=f32) * HEAD ** (-0.5)
    s = jnp.where(allowed, s, -1e30)
    ex = jnp.exp(s - jnp.max(s, axis=-1, keepdims=True))
    p = ex / jnp.sum(ex, axis=-1, keepdims=True)
    o = jnp.einsum("bhqk,bkhe->bqhe", p.astype(bf16), v, preferred_element_type=f32)
    return p, o.astype(bf16)


def attend_back(q, k, v, p, g):
    dp = jnp.einsum("bqhe,bkhe->bhqk", g, v, preferred_element_type=f32)
    ds = (p * (dp - jnp.sum(dp * p, axis=-1, keepdims=True)) * HEAD ** (-0.5)).astype(bf16)
    dq = jnp.einsum("bhqk,bkhe->bqhe", ds, k, preferred_element_type=f32).astype(bf16)
    dk = jnp.einsum("bhqk,bqhe->bkhe", ds, q, preferred_element_type=f32).astype(bf16)
    dv = jnp.einsum("bhqk,bqhe->bkhe", p.astype(bf16), g, preferred_element_type=f32).astype(bf16)
    return dq, dk, dv


def layer(x0, img, mask, gains, weights, cot):
    g1, g2, g3 = (g.astype(f32) for g in gains)
    w_qkv, w_so, w_cq, w_ckv, w_co, w_up, w_down = weights
    b, t, d = x0.shape
    x = x0.astype(f32)
    pos = jnp.arange(t)
    causal = (pos[:, None] >= pos[None, :])[None, None]
    allowed = (mask > 0)[:, None, None, :]
    h1, r1 = norm_stats(x)
    n1 = (h1 * g1).astype(bf16)
    qkv = mm(n1, w_qkv).astype(bf16)
    q1, k1, v1 = (split_heads(qkv[..., i * d : (i + 1) * d]) for i in range(3))
    p1, o1 = attend(q1, k1, v1, causal)
    o1 = o1.reshape(b, t, d)
    x1 = x + mm(o1, w_so)
    h2, r2 = norm_stats(x1)
    n2 = (h2 * g2).astype(bf16)
    q2 = split_heads(mm(n2, w_cq).astype(bf16))
    kv = mm(img, w_ckv).astype(bf16)
    k2, v2 = split_heads(kv[..., :d]), split_heads(kv[..., d:])
    p2, o2 = attend(q2, k2, v2, allowed)
    o2 = o2.reshape(b, t, d)
    x2 = x1 + mm(o2, w_co)
    h3, r3 = norm_stats(x2)
    n3 = (h3 * g3).astype(bf16)
    hpre = mm(n3, w_up)
    cdf = 0.5 * (1.0 + lax.erf(hpre * (0.5**0.5)))
    act = (hpre * cdf).astype(bf16)
    out = (x2 + mm(act, w_down)).astype(bf16)

    gw_down = wgrad(act, cot)
    pdf = jnp.exp(-0.5 * hpre * hpre) * (0.5 / jnp.pi) ** 0.5
    gh = (mm_t(cot, w_down) * (cdf + hpre * pdf)).astype(bf16)
    gw_up = wgrad(n3, gh)
    dx2, gg3 = norm_back(h3, r3, g3, mm_t(gh, w_up))
    gx2 = cot.astype(f32) + dx2
    gx2b = gx2.astype(bf16)
    gw_co = wgrad(o2, gx2b)
    go2 = split_heads(mm_t(gx2b, w_co).astype(bf16))
    dq2, dk2, dv2 = attend_back(q2, k2, v2, p2, go2)
    dq2 = dq2.reshape(b, t, d)
    dkv = jnp.concatenate([dk2.reshape(b, -1, d), dv2.reshape(b, -1, d)], axis=-1)
    gw_ckv = wgrad(img, dkv)
    gimg = mm_t(dkv, w_ckv).astype(bf16)
    gw_cq = wgrad(n2, dq2)
    dx1, gg2 = norm_back(h2, r2, g2, mm_t(dq2, w_cq))
    gx1 = gx2 + dx1
    gx1b = gx1.astype(bf16)
    gw_so = wgrad(o1, gx1b)
    go1 = split_heads(mm_t(gx1b, w_so).astype(bf16))
    dq1, dk1, dv1 = attend_back(q1, k1, v1, p1, go1)
    dqkv = jnp.concatenate([a.reshape(b, t, d) for a in (dq1, dk1, dv1)], axis=-1)
    gw_qkv = wgrad(n1, dqkv)
    dx0, gg1 = norm_back(h1, r1, g1, mm_t(dqkv, w_qkv))
    gx0 = gx1 + dx0
    return out, gx0, gimg, (gg1, gg2, gg3), (gw_qkv, gw_so, gw_cq, gw_ckv, gw_co, gw_up, gw_down)


def native(captions, img, mask, gains, weights, cotangent):
    full = [lax.all_gather(w, BOTH, axis=0, tiled=True) for w in weights]
    gains = lax.all_gather(gains, BOTH, axis=0, tiled=True)
    gains = tuple(gains[:, i] for i in range(3))
    out, gx0, gimg, gg, gw = layer(captions, img, mask, gains, full, cotangent)
    gg = lax.psum_scatter(jnp.stack(gg, axis=1), BOTH, scatter_dimension=0, tiled=True)
    shards = [
        lax.psum_scatter(g.astype(bf16), BOTH, scatter_dimension=0, tiled=True).astype(f32)
        for g in gw
    ]
    gimg = lax.all_to_all(gimg, "seq", split_axis=2, concat_axis=0, tiled=True)
    return (out, gx0, gimg.astype(f32), gg[:, 0], gg[:, 1], gg[:, 2], *shards)


def on_device(captions, images, tissue_mask, gain_self, gain_cross, gain_mlp, *rest):
    weights, cotangent = rest[:-1], rest[-1]
    n_dp, n_seq = lax.axis_size("dp"), lax.axis_size("seq")
    b, t, d = captions.shape
    patches = images.shape[1]
    if n_seq != 4 or n_dp % 4 or any(w.shape[0] % 8 for w in weights):
        start = lax.axis_index("seq") * b
        img = lax.dynamic_slice_in_dim(images, start, b, 0)
        mask = lax.dynamic_slice_in_dim(tissue_mask, start, b, 0)
        gains = jnp.stack([gain_self, gain_cross, gain_mlp], axis=1)
        return native(captions, img, mask, gains, weights, cotangent)
    nz = n_dp // 2
    gains = (gain_self, gain_cross, gain_mlp)
    out, res, fulls = forward(nz, captions, images, tissue_mask, gains, weights)
    gx, gimg, *gw, gg = backward(nz, cotangent, patches, captions, weights, res, fulls[1:])
    gimg = gimg.reshape(4 * b, *gimg.shape[2:])
    out, gx, *gw, gimg, gs, gc, gm = finish([out, gx, *gw], gimg, gg, patches)
    out, gx = out.reshape(b, t, d), gx.reshape(b, t, d)
    return (out, gx, gimg.swapaxes(1, 2), gs, gc, gm, *gw)


def solution(mesh):
    tok = P(BOTH, None, None)
    vec = P(BOTH)
    mat = P(BOTH, None)
    return jax.shard_map(
        on_device,
        mesh=mesh,
        in_specs=(tok, P("dp", None, None), P("dp", None), vec, vec, vec, *([mat] * 7), tok),
        out_specs=(tok, tok, P("dp", None, "seq"), vec, vec, vec, *([mat] * 7)),
        check_vma=False,
    )
```

```python
import functools

import jax
import jax.numpy as jnp
from jax import lax
from jax.experimental import pallas as pl
from jax.experimental.pallas import tpu as pltpu
from jax.sharding import PartitionSpec as P

HEADS = 12
HEAD = 64
EPS = 1e-05
BOTH = ("dp", "seq")
f32 = jnp.float32
bf16 = jnp.bfloat16
MESH = pl.DeviceIdType.MESH
HBM = pltpu.MemorySpace.HBM
VMEM = pltpu.MemorySpace.VMEM
LANES = 128


class Place:
    def __init__(self, nz, wide=False):
        dp, seq = lax.axis_index("dp"), lax.axis_index("seq")
        self.nz = nz
        self.z, self.x = dp // 2, lax.rem(dp, 2)
        self.y, self.c = seq // 2, lax.rem(seq, 2)
        x, y = self.x, self.y
        self.role = role = 1 if wide else self.c
        self.p = x + role * (y - x)
        self.s = y + role * (x - y)
        self.sib = (dp, 2 * y + (1 - self.c))
        self.p_xy = (x + (1 - role) * (1 - 2 * x), y + role * (1 - 2 * y))
        self.s_xy = (x + role * (1 - 2 * x), y + (1 - role) * (1 - 2 * y))
        self.ps_xy = (1 - x, 1 - y)
        self.p_dev = self.dev(self.z, self.p_xy)
        self.s_dev = self.dev(self.z, self.s_xy)
        self.z_of = [lax.rem(self.z + k, nz) for k in range(nz)]
        self.z_devs = [self.dev(self.z_of[k], (x, y)) for k in range(nz)]

    def dev(self, z, xy):
        return (2 * z + xy[0], 2 * xy[1] + self.c)

    def column(self, p, s):
        return p + self.role * (s - p), s + self.role * (p - s)

    def partners(self):
        return [*self.z_devs[1:], self.p_dev, self.s_dev, self.sib]


def enter(partners):
    barrier = pltpu.get_barrier_semaphore()
    for d in partners:
        pl.semaphore_signal(barrier, inc=1, device_id=d, device_id_type=MESH)
    pl.semaphore_wait(barrier, len(partners))


def remote(src, dst, sems, i, dev):
    return pltpu.make_async_remote_copy(
        src_ref=src, dst_ref=dst, send_sem=sems[0].at[i], recv_sem=sems[1].at[i],
        device_id=dev, device_id_type=MESH,
    )


class Gather:
    LOADS = (("z", 8), ("xy", 8), ("xy", 4), ("core", 8), None)
    WORK = (0.3, 0.3, 0.2, 0.2, 0.1)

    def __init__(self, here, shard, full, sems, local):
        h = here
        x, y, c = h.x, h.y, h.c
        mine = full.at[h.z, x, y, c]

        def col(xy):
            return full.at[:, xy[0], xy[1], c]

        self.own = pltpu.make_async_copy(shard, mine, local)
        nz = h.nz
        self.zs = [remote(shard, mine, sems, k - 1, h.z_devs[k]) for k in range(1, nz)]
        own, px, sx, psx = (x, y), h.p_xy, h.s_xy, h.ps_xy
        n = nz - 1
        self.p_own = remote(col(own), col(own), sems, n, h.p_dev)
        self.s_own = remote(col(own), col(own), sems, n + 1, h.s_dev)
        self.s_p = remote(col(px), col(px), sems, n + 2, h.s_dev)
        self.sibs = [
            remote(col(xy), col(xy), sems, n + 3 + i, h.sib)
            for i, xy in enumerate((own, px, sx, psx))
        ]

    @staticmethod
    def count(nz):
        return nz + 6

    def step(self, i):
        if i == 0:
            self.own.start()
            for t in self.zs:
                t.start()
        elif i == 1:
            self.own.wait()
            for t in self.zs:
                t.wait_recv()
            self.p_own.start()
            self.s_own.start()
            self.sibs[0].start()
        elif i == 2:
            self.p_own.wait_recv()
            self.s_p.start()
            self.sibs[1].start()
        elif i == 3:
            self.s_own.wait_recv()
            self.sibs[2].start()
            self.s_p.wait_recv()
            self.sibs[3].start()
        elif i == 4:
            for t in self.sibs:
                t.wait_recv()
        elif i == 5:
            for t in (*self.zs, self.p_own, self.s_own, self.s_p, *self.sibs):
                t.wait_send()


class GatherPlane(Gather):
    LOADS = (("xy", 2), ("xy", 1), ("z", 32), ("core", 12), None)

    def __init__(self, here, shard, full, sems, local):
        h = here
        x, y, c, z = h.x, h.y, h.c, h.z
        mine = full.at[z, x, y, c]
        pb = full.at[z, h.p_xy[0], h.p_xy[1], c]

        def plane(i):
            return full.at[i, :, :, c]

        self.own = pltpu.make_async_copy(shard, mine, local)
        nz = h.nz
        self.p_own = remote(shard, mine, sems, 0, h.p_dev)
        self.s_own = remote(shard, mine, sems, 1, h.s_dev)
        self.s_p = remote(pb, pb, sems, 2, h.s_dev)
        self.zs = [remote(plane(z), plane(z), sems, 2 + k, h.z_devs[k]) for k in range(1, nz)]
        self.sibs = [
            remote(plane(h.z_of[-k]), plane(h.z_of[-k]), sems, 2 + nz + k, h.sib)
            for k in range(nz)
        ]

    def step(self, i):
        if i == 0:
            self.own.start()
            self.p_own.start()
            self.s_own.start()
        elif i == 1:
            self.p_own.wait_recv()
            self.s_p.start()
        elif i == 2:
            self.own.wait()
            self.s_own.wait_recv()
            self.s_p.wait_recv()
            for t in self.zs:
                t.start()
            self.sibs[0].start()
        elif i == 3:
            for k, t in enumerate(self.zs):
                t.wait_recv()
                self.sibs[k + 1].start()
        else:
            super().step(i)


def add_blocks(count, dst, a, b):
    def body(i, _):
        dst(i)[...] = (a(i)[...].astype(f32) + b(i)[...].astype(f32)).astype(bf16)
        return 0

    lax.fori_loop(0, count, body, 0)


class Scatter:
    LOADS = (("core", 16), ("xy", 8), ("xy", 4), ("z", 8), None)
    WORK = (0.3, 1.2, 0.7, 0.4, 0.3)

    @staticmethod
    def shapes(nz, blk):
        return (nz, 2, 2, *blk), (2, nz, *blk), (nz, *blk), (nz - 1, *blk)

    @staticmethod
    def count(nz):
        return nz + 3

    def __init__(self, here, part, bufs, out, sems):
        self.h, self.out = here, out
        self.rc, self.rs, self.rp, self.rz = bufs
        h, nz = here, here.nz
        self.own = part.at[:, :, :, h.c]
        self.core = remote(part.at[:, :, :, 1 - h.c], self.rc, sems, 0, h.sib)
        self.s = [
            remote(self.rc.at[:, *h.column(p, 1 - h.s)], self.rs.at[p], sems, 1 + i, h.s_dev)
            for i, p in enumerate((1 - h.p, h.p))
        ]
        self.pp = remote(self.rs.at[1 - h.p], self.rp, sems, 3, h.p_dev)
        self.zs = [
            remote(self.rp.at[h.z_of[k]], self.rz.at[k - 1], sems, 3 + k, h.z_devs[k])
            for k in range(1, nz)
        ]

    def sum_core(self):
        at = lambda r: lambda i: r.at[lax.div(i, 4), lax.rem(lax.div(i, 2), 2), lax.rem(i, 2)]
        add_blocks(4 * self.h.nz, at(self.rc), at(self.rc), at(self.own))

    def step(self, i):
        h, nz = self.h, self.h.nz
        if i == 0:
            self.core.start()
        elif i == 1:
            self.core.wait_recv()
            self.sum_core()
            for t in self.s:
                t.start()
            self.core.wait_send()
        elif i == 2:
            for t in self.s:
                t.wait_recv()

            def kept(i):
                return self.rc.at[lax.rem(i, nz), *h.column(lax.div(i, nz), h.s)]

            mine = lambda i: self.rs.at[lax.div(i, nz), lax.rem(i, nz)]
            add_blocks(2 * nz, mine, mine, kept)
            self.pp.start()
        elif i == 3:
            self.pp.wait_recv()
            mine = lambda i: self.rp.at[i]
            add_blocks(nz, mine, mine, lambda i: self.rs.at[h.p, i])
            for t in self.zs:
                t.start()
        elif i == 4:
            for t in self.zs:
                t.wait_recv()
            total = self.rp[h.z].astype(f32)
            for k in range(nz - 1):
                total = total + self.rz[k].astype(f32)
            self.out[...] = total
        elif i == 5:
            for t in (*self.s, self.pp, *self.zs):
                t.wait_send()


class ScatterPlane(Scatter):
    LOADS = (("core", 16), ("z", 32), ("xy", 2), ("xy", 1), None)

    @staticmethod
    def shapes(nz, blk):
        return (nz, 2, 2, *blk), (nz - 1, 2, 2, *blk), (2, *blk), blk

    def __init__(self, here, part, bufs, out, sems):
        self.h, self.out = here, out
        self.rc, self.rz, self.rs, self.rp = bufs
        h, nz = here, here.nz
        self.own = part.at[:, :, :, h.c]
        self.core = remote(part.at[:, :, :, 1 - h.c], self.rc, sems, 0, h.sib)
        self.zs = [
            remote(self.rc.at[h.z_of[k]], self.rz.at[k - 1], sems, k, h.z_devs[k])
            for k in range(1, nz)
        ]
        self.s = [
            remote(self.rc.at[h.z, *h.column(p, 1 - h.s)], self.rs.at[p], sems, nz + p, h.s_dev)
            for p in range(2)
        ]
        self.pp = remote(self.rs.at[1 - h.p], self.rp, sems, nz + 2, h.p_dev)

    def step(self, i):
        h, nz = self.h, self.h.nz
        if i == 1:
            self.core.wait_recv()
            self.sum_core()
            for t in self.zs:
                t.start()
            self.core.wait_send()
        elif i == 2:
            for t in self.zs:
                t.wait_recv()

            def body(i, _):
                mine = self.rc.at[h.z, lax.div(i, 2), lax.rem(i, 2)]
                total = mine[...].astype(f32)
                for k in range(nz - 1):
                    total = total + self.rz[k, lax.div(i, 2), lax.rem(i, 2)].astype(f32)
                mine[...] = total.astype(bf16)
                return 0

            lax.fori_loop(0, 4, body, 0)
            for t in self.s:
                t.start()
        elif i == 3:
            for t in self.s:
                t.wait_recv()
            mine = lambda i: self.rs.at[i]
            add_blocks(2, mine, mine, lambda i: self.rc.at[h.z, *h.column(i, h.s)])
            self.pp.start()
        elif i == 4:
            self.pp.wait_recv()
            self.out[...] = self.rs[h.p].astype(f32) + self.rp[...].astype(f32)
        else:
            super().step(i)


class Planner:
    UNIT = {"xy": 0.8, "z": 0.8, "core": 0.1}

    def __init__(self, chunks, sizes, hop):
        self.chunks, self.sizes, self.hop = chunks, sizes, hop
        self.now, self.free = 0.0, dict.fromkeys(self.UNIT, 0.0)
        self.ready, self.queue, self.arrived = {}, [], None
        self.held, self.ahead = [], 0

    def emit(self, i):
        step, when = self.ready.get(i, (0, 0.0))
        chunk, size = self.chunks[i], self.sizes[i]
        self.now = max(self.now, when) + chunk.WORK[step] * size
        chunk.step(step)
        load = chunk.LOADS[step]
        if load is None:
            del self.ready[i]
            if self.arrived:
                self.arrived(i)
            return
        if step == 1 and i + self.ahead in self.held:
            self.held.remove(i + self.ahead)
            self.emit(i + self.ahead)
        link, amount = load
        self.free[link] = max(self.free[link], self.now) + self.UNIT[link] * amount * size
        self.ready[i] = (step + 1, self.free[link] + self.hop)

    def settle(self):
        while True:
            due = [(-s, i) for i, (s, when) in self.ready.items() if when <= self.now]
            if not due:
                return
            self.emit(min(due)[1])

    def free_slot(self, i):
        while i in self.ready and self.ready[i][0] == 1:
            self.emit(i)

    def compute(self, cost, work):
        self.settle()
        work()
        self.now += cost

    def later(self, cost, work):
        self.queue.append((cost, work))

    def finish(self):
        while self.ready or self.queue:
            self.settle()
            if self.queue:
                self.compute(*self.queue.pop(0))
            elif self.ready:
                self.emit(min(self.ready, key=lambda k: (self.ready[k][1], k)))
        for c in self.chunks:
            c.step(5)


def stats(v):
    mean = jnp.mean(v, axis=-1, keepdims=True)
    cen = v - mean
    r = lax.rsqrt(jnp.mean(cen * cen, axis=-1, keepdims=True) + EPS)
    return cen * r, r


def dot(a, b):
    return jnp.dot(a, b, preferred_element_type=f32)


def dot_nt(a, b):
    return lax.dot_general(a, b, (((1,), (1,)), ((), ())), preferred_element_type=f32)


def dot_tn(a, b):
    return lax.dot_general(a, b, (((0,), (0,)), ((), ())), preferred_element_type=f32)


def matrix(ref, lo=None, size=None):
    v = ref[...] if lo is None else ref[..., pl.ds(lo, size)]
    return v.reshape(-1, v.shape[-1])


def tiles(total, size, work):
    def body(i, _):
        work(pl.multiple_of(i * size, size))
        return 0

    lax.fori_loop(0, total // size, body, 0)


def span(start, size, unit=2 * HEAD):
    return pl.ds(pl.multiple_of(start, unit), size)


def head_lanes():
    lane = lax.broadcasted_iota(jnp.int32, (1, 2 * HEAD), 1)
    low = jnp.where(lane < HEAD, 1.0, 0.0)
    return low.astype(bf16), (1.0 - low).astype(bf16)


def softmax(s):
    e = jnp.exp(s - jnp.max(s, axis=-1, keepdims=True))
    return (e * (1.0 / jnp.sum(e, axis=-1, keepdims=True))).astype(bf16)


def pair(ref, rows, base, j):
    return ref.at[rows, pl.ds(pl.multiple_of(base + j * 2 * HEAD, 2 * HEAD), 2 * HEAD)]


SCALE = HEAD ** (-0.5)


def chunk_cols(weights, d):
    out = []
    for i, w in enumerate(weights):
        wide = d if w.shape[1] % d == 0 and i < 6 else d // 3
        out += [(i, s, wide) for s in range(0, w.shape[1], wide)]
    return out


def forward_kernel(nz, dims, chunks, *refs):
    b, t, d, kp, ff = dims
    n = len(chunks) + 1
    xs, mask = refs[:2]
    gains = refs[2:5]
    images = refs[5]
    shards = refs[6:13]
    out = refs[13]
    res = refs[14 : 14 + N_RES]
    fulls = refs[14 + N_RES : 14 + N_RES + n]
    rest = refs[14 + N_RES + n :]
    (n1, qkv, p1, o1, x1, n2, q2, kv2, p2, o2, x2, n3, act, dg, grow, img) = keep = rest[:N_RES]
    g = rest[N_RES : N_RES + n]
    raw, mb, gsh, turn, local, ssem, rsem, csem, isem = rest[N_RES + n :]
    here = Place(nz)
    seq = lax.axis_index("seq")
    patches = mask.shape[1]
    turn[...] = jnp.zeros(turn.shape, f32)
    for i, gain in enumerate(gains):
        turn[i : i + 1, : gain.shape[0]] = gain[...].astype(f32).reshape(1, -1)
    gsh[...] = jnp.zeros(gsh.shape, bf16)
    gsh[:, :8] = jnp.transpose(turn[...])[: gsh.shape[0]].astype(bf16)
    enter(here.partners())
    srcs = [gsh] + [shards[i].at[:, s : s + w] for i, s, w in chunks]
    gs = []
    for i in range(n):
        kind = GatherPlane if i in (11, 12) else Gather
        gs.append(kind(here, srcs[i], g[i], (ssem.at[i], rsem.at[i]), local.at[i]))
    sizes = [gsh.shape[-1] / d] + [r.shape[-1] * r.shape[-2] / (d * gsh.shape[0]) for r in g[1:]]
    plan = Planner(gs, sizes, 5.0)
    plan.ahead = AHEAD
    plan.held = [i for i in range(AHEAD, n) if i not in (11, 12)]
    for i in range(n):
        if i not in plan.held:
            plan.emit(i)
    pictures = pltpu.make_async_copy(images.at[pl.ds(seq * b, b)], raw, isem.at[0])
    pictures.start()
    mb[...] = jnp.full(mb.shape, -1e30, f32)
    for i in range(b):
        row = mask[pl.ds(seq * b + i, 1), :]
        mb[i : i + 1, :patches] = jnp.where(row > 0, 0.0, -1e30)
    copies = []

    def flush(src, dst):
        cp = pltpu.make_async_copy(src, dst, csem.at[len(copies)])
        cp.start()
        copies.append(cp)

    def save(*which):
        for k in which:
            flush(keep[k], res[k])

    names = {}
    for k, (i, s, wide) in enumerate(chunks):
        names.setdefault(i, []).append(k + 1)
    lanes = head_lanes()
    heads = d // HEAD
    pairs = heads // 2
    tok = [slice(i * t, (i + 1) * t) for i in range(b)]
    pat = [slice(i * kp, (i + 1) * kp) for i in range(b)]

    def first():
        grow[...] = jnp.transpose(matrix(g[0]).astype(f32))[:8]

        def rows(r):
            h, _ = stats(xs[pl.ds(r, t)].astype(f32))
            n1[pl.ds(r, t)] = (h * grow[0:1]).astype(bf16)

        tiles(b * t, t, rows)
        save(0, 14)

    def project(src, k, dst, at):
        def tile(s):
            v = src()
            dst[:, span(at + s, 256)] = dot(v, matrix(g[k], s, 256)).astype(bf16)

        return lambda: tiles(g[k].shape[-1], 256, tile)

    def self_pairs(lo, hi):
        def body(j, _):
            causal = lax.broadcasted_iota(jnp.int32, (t, t), 0) >= lax.broadcasted_iota(
                jnp.int32, (t, t), 1
            )
            for i, r in enumerate(tok):
                q, k, v = (pair(qkv, r, m * d, j)[...] for m in range(3))
                o = jnp.zeros((t, 2 * HEAD), f32)
                for a in range(2):
                    s = dot_nt(q, k * lanes[a]) * SCALE
                    p = softmax(jnp.where(causal, s, -1e30))
                    p1[i * heads + 2 * j + a] = p
                    o = o + dot(p, v * lanes[a])
                pair(o1, r, 0, j)[...] = o.astype(bf16)
            return 0

        return lambda: lax.fori_loop(lo, hi, body, 0)

    def cross_pairs(lo, hi):
        def body(j, _):
            for i, r in enumerate(tok):
                q = pair(q2, r, 0, j)[...]
                k, v = (pair(kv2, pat[i], m * d, j)[...] for m in range(2))
                bias = mb[i : i + 1]
                o = jnp.zeros((t, 2 * HEAD), f32)
                for a in range(2):
                    p = softmax(dot_nt(q, k * lanes[a]) * SCALE + bias)
                    p2[i * heads + 2 * j + a] = p
                    o = o + dot(p, v * lanes[a])
                pair(o2, r, 0, j)[...] = o.astype(bf16)
            return 0

        return lambda: lax.fori_loop(lo, hi, body, 0)

    def residual(base, o, k, dst, row, normed):
        def rows(s):
            r = pl.ds(s, t)
            v = base[r].astype(f32) + dot(o[r], matrix(g[k]))
            dst[r] = v
            h, _ = stats(v)
            normed[r] = (h * grow[row : row + 1]).astype(bf16)

        return lambda: tiles(b * t, t, rows)

    def mlp_up(k, at):
        def tile(s):
            h = dot(n3[...], matrix(g[k], s, 256))
            cols = span(at + s, 256)
            cdf = 0.5 * (1.0 + lax.erf(h * (0.5**0.5)))
            act[:, cols] = (h * cdf).astype(bf16)
            pdf = jnp.exp(-0.5 * h * h) * (0.5 / jnp.pi) ** 0.5
            dg[:, cols] = (cdf + h * pdf).astype(bf16)

        return lambda: tiles(g[k].shape[-1], 256, tile)

    def mlp_down(k, at):
        wide = g[k].shape[-1]

        def rows(s):
            r = pl.ds(s, t)
            y = x2[r, at : at + wide] + dot(act[r], matrix(g[k]))
            out[r, at : at + wide] = y.astype(bf16)

        return lambda: tiles(b * t, t, rows)

    def images_here():
        pictures.wait()
        whole = patches // 16 * 16
        for i in range(b):
            img[i * kp : i * kp + whole] = raw[i, :whole]
            if whole < patches:
                img[i * kp + whole : (i + 1) * kp] = jnp.zeros((kp - whole, d), bf16)
                img[i * kp + whole : i * kp + patches] = raw[i, whole:]
        save(15)

    third = [(i * pairs // 3, (i + 1) * pairs // 3) for i in range(3)]

    landed = set()

    def arrived(c):
        flush(g[c], fulls[c])
        landed.add(c)
        while queued[0] in landed:
            use(queued[0])
            queued[0] += 1

    queued = [0]

    def use(c):
        add = plan.later
        if c == 0:
            add(2.0, first)
            add(0.0, images_here)
            return
        i, s, wide = chunks[c - 1]
        last = c == names[i][-1]
        if i == 0:
            add(1.7, project(lambda: n1[...], c, qkv, s))
            if last:
                add(0.0, lambda: save(1))
                for lo, hi in third:
                    add(2.5, self_pairs(lo, hi))
                add(0.0, lambda: save(2, 3))
        elif i == 1:
            add(2.5, residual(xs, o1, c, x1, 1, n2))
            add(0.0, lambda: save(4, 5))
        elif i == 2:
            add(1.7, project(lambda: n2[...], c, q2, 0))
            add(0.0, lambda: save(6))
        elif i == 3:
            add(2.5, project(lambda: img[...], c, kv2, s))
            if last:
                add(0.0, lambda: save(7))
                for lo, hi in third:
                    add(3.0, cross_pairs(lo, hi))
                add(0.0, lambda: save(8, 9))
        elif i == 4:
            add(2.5, residual(x1, o2, c, x2, 2, n3))
            add(0.0, lambda: save(10, 11))
        elif i == 5:
            add(3.5, mlp_up(c, s))
            if last:
                add(0.0, lambda: save(12, 13))
        else:
            add(2.0, mlp_down(c, s))

    plan.arrived = arrived
    plan.finish()
    for cp in copies:
        cp.wait()


N_RES = 16
AHEAD = 99


def residual_shapes(b, t, d, kp, ff):
    m, heads = b * t, d // HEAD
    S = jax.ShapeDtypeStruct
    tok, tokf = S((m, d), bf16), S((m, d), f32)
    return [
        tok, S((m, 3 * d), bf16), S((b * heads, t, t), bf16), tok, tokf, tok, tok,
        S((b * kp, 2 * d), bf16), S((b * heads, t, kp), bf16), tok, tokf, tok,
        S((m, ff), bf16), S((m, ff), bf16), S((8, d), f32), S((b * kp, d), bf16),
    ]


def forward(nz, xs, images, mask, gains, weights):
    b, t, d = xs.shape
    kp, ff = padded(images.shape[1]), weights[5].shape[1]
    chunks = chunk_cols(weights, d)
    n = len(chunks) + 1
    res = residual_shapes(b, t, d, kp, ff)
    block = (weights[0].shape[0], LANES)
    blocks = [block] + [(weights[i].shape[0], w) for i, _, w in chunks]
    fulls = [jax.ShapeDtypeStruct((nz, 2, 2, 2, *s), bf16) for s in blocks]
    count = Gather.count(nz)
    hbm, vm = pl.BlockSpec(memory_space=HBM), pl.BlockSpec(memory_space=VMEM)
    outs = pl.pallas_call(
        functools.partial(forward_kernel, nz, (b, t, d, kp, ff), chunks),
        out_shape=[jax.ShapeDtypeStruct((b * t, d), bf16), *res, *fulls],
        in_specs=[*([vm] * 5), *([hbm] * 8)],
        out_specs=[vm, *([hbm] * (N_RES + n))],
        scratch_shapes=[
            *(pltpu.VMEM(s.shape, s.dtype) for s in (*res, *fulls)),
            pltpu.VMEM((b, *images.shape[1:]), bf16),
            pltpu.VMEM((b + -b % 8, kp), f32),
            pltpu.VMEM(block, bf16),
            pltpu.VMEM((8, LANES), f32),
            pltpu.SemaphoreType.DMA((n,)),
            pltpu.SemaphoreType.DMA((n, count)),
            pltpu.SemaphoreType.DMA((n, count)),
            pltpu.SemaphoreType.DMA((N_RES + n,)),
            pltpu.SemaphoreType.DMA((1,)),
        ],
        compiler_params=pltpu.CompilerParams(
            collective_id=0, has_side_effects=True, vmem_limit_bytes=60 << 20
        ),
    )(xs.reshape(b * t, d), mask, *gains, images, *weights)
    return outs[0], outs[1 : 1 + N_RES], outs[1 + N_RES :]


def padded(patches):
    return patches + -patches % 16


def backward_kernel(nz, dims, chunks, *refs):
    b, t, d, kp, ff = dims
    heads = d // HEAD
    pairs = heads // 2
    m = b * t
    n_c = len(chunks)
    order = [*range(n_c - 3, n_c), *range(n_c - 7, n_c - 3), 7, 5, 6, 4, 3, None, 0, 1, 2]
    n = len(order)
    h_in = refs[: 2 + N_RES + n_c]
    h_cot, h_xs = h_in[:2]
    res = dict(zip(RES_NAMES, h_in[2 : 2 + N_RES]))
    full = h_in[2 + N_RES :]
    at = len(h_in)
    gx_out, img_out = refs[at : at + 2]
    outs = refs[at + 2 : at + 9]
    gg_out = refs[at + 9]
    rest = list(refs[at + 10 :])
    take = lambda k: [rest.pop(0) for _ in range(k)]
    cot, act, dg, n3, xf, o2, p2, q2, kv2, img, n2, o1, p1, n1, xs, grow = take(16)
    gx, gxb, go, gi, ggr = take(5)
    wd, ws = take(3), take(6)
    pd, ps, pg = take(3), take(4), take(1)[0]
    bufs = [take(4) for _ in range(n)]
    lsem, ssem, rsem, isem, jsem, osem = rest
    here, broad = Place(nz), Place(nz, wide=True)
    dp, seq = lax.axis_index("dp"), lax.axis_index("seq")
    peers = [(dp, lax.rem(seq + k, 4)) for k in range(1, 4)]

    loads, waits = {}, {}

    def load(name, src, dst):
        cp = pltpu.make_async_copy(src, dst, lsem.at[len(loads)])
        loads[name] = cp
        cp.start()

    def need(*names):
        for k in names:
            if k in loads and k not in waits:
                loads[k].wait()
                waits[k] = True

    q_at = act.at[:, : 3 * d]
    load("act", res["act"], act)
    load("cot", h_cot, cot)
    for j in range(3):
        load("wd%d" % j, full[n_c - 3 + j], wd[j])
    load("dg", res["dg"], dg)
    load("n3", res["n3"], n3)
    for j in range(4):
        load("up%d" % j, full[n_c - 7 + j], ws[j])
    load("x2", res["x2"], xf)
    load("grow", res["grow"], grow)
    for name, dst in (("o2", o2), ("p2", p2), ("q2", q2), ("kv2", kv2)):
        load(name, res[name], dst)
    load("img", res["img"], img)
    load("co", full[7], ws[4])
    load("ckv0", full[5], ws[5])
    for name, dst in (("n2", n2), ("o1", o1), ("p1", p1), ("n1", n1)):
        load(name, res[name], dst)
    load("xs", h_xs, xs)
    enter([*here.partners(), *peers])
    ggr[...] = jnp.zeros_like(ggr)

    parts, small = [], 0
    for k in order:
        if k is None:
            parts.append(pg)
        elif k >= n_c - 3:
            parts.append(pd[k - (n_c - 3)])
        else:
            parts.append(ps[small % 4])
            small += 1
    place = {k: i for i, k in enumerate(order)}
    dst = [
        gg_out if k is None else outs[chunks[k][0]].at[:, chunks[k][1] : chunks[k][1] + chunks[k][2]]
        for k in order
    ]
    sc = []
    for i in range(n):
        kind = ScatterPlane if i in PLANES else Scatter
        at = broad if i in BROAD else here
        sc.append(kind(at, parts[i], bufs[i], dst[i], (ssem.at[i], rsem.at[i])))
    sizes = [0.2 if k is None else 1.35 if k >= n_c - 3 else 1.0 for k in order]
    plan = Planner(sc, sizes, 3.0)
    smalls = [i for i, k in enumerate(order) if k is not None and k < n_c - 3]

    def slot_ready(i):
        if i in smalls and smalls.index(i) >= 4:
            plan.free_slot(smalls[smalls.index(i) - 4])

    lanes = head_lanes()
    tok = [slice(i * t, (i + 1) * t) for i in range(b)]
    pat = [slice(i * kp, (i + 1) * kp) for i in range(b)]

    def grad_small(k, x, dy, first, cost):
        i = place[k]
        slot_ready(i)

        def work():
            rows = x()
            for s in range(0, d, 256):
                r = dot_tn(rows, dy[:, first + s : first + s + 256])
                parts[i][:, :, :, :, :, s : s + 256] = r.reshape(nz, 2, 2, 2, -1, 256).astype(bf16)

        plan.compute(cost, work)
        plan.emit(i)

    def grad_down(j):
        k = n_c - 3 + j
        i = place[k]
        wide = d // 3

        rows = ff // nz

        def work(z, _):
            r = dot_tn(act[:, span(z * rows, rows)], cot[:, j * wide : (j + 1) * wide])
            parts[i][z] = r.reshape(2, 2, 2, -1, wide).astype(bf16)
            return 0

        plan.compute(1.8, lambda: lax.fori_loop(0, nz, work, 0))
        plan.emit(i)

    def hidden(z):
        half, wide = ff // nz // 2, d // 3

        def work(x, _):
            g = None
            for j in range(3):
                w = wd[j][z, x].reshape(half, wide)
                term = dot_nt(cot[:, j * wide : (j + 1) * wide], w)
                g = term if g is None else g + term
            at = span((2 * z + x) * half, half)
            dg[:, at] = (g * dg[:, at].astype(f32)).astype(bf16)
            return 0

        plan.compute(1.3, lambda: lax.fori_loop(0, 2, work, 0))

    def norm_grad(src, ups, base, row, first):
        ggr[row : row + 1] = jnp.zeros((1, d), f32)

        def work(s):
            r = pl.ds(s, t)
            e = None
            for j, w in enumerate(ups):
                term = dot_nt(src[r, j * d : (j + 1) * d], matrix(w))
                e = term if e is None else e + term
            h, rs = stats(base[r].astype(f32))
            u = e * grow[row : row + 1]
            mu = jnp.mean(u, axis=-1, keepdims=True)
            mx = jnp.mean(u * h, axis=-1, keepdims=True)
            prev = cot[r].astype(f32) if first else gx[r]
            v = prev + rs * (u - mu - h * mx)
            gx[r] = v
            gxb[r] = v.astype(bf16)
            ggr[row : row + 1] += jnp.sum(e * h, axis=0, keepdims=True)

        plan.compute(1.5 + 1.2 * len(ups), lambda: tiles(m, t, work))

    def back_project(w):
        half = d // 2

        def work(s, _):
            rows = w[pl.ds(s * (nz // 2), nz // 2)].reshape(half, d)
            go[:, span(s * half, half)] = dot_nt(gxb[...], rows).astype(bf16)
            return 0

        plan.compute(1.4, lambda: lax.fori_loop(0, 2, work, 0))

    def pairs_back(lo, hi, p_ref, q_ref, q_base, kv_ref, kv_base, rows):
        def body(j, _):
            for i, r in enumerate(tok):
                rk = rows[i]
                q, g = pair(q_ref, r, q_base, j)[...], pair(go, r, 0, j)[...]
                k, v = (pair(kv_ref, rk, kv_base + x * d, j)[...] for x in range(2))
                dq = dk = dv = None
                for a in range(2):
                    lane = lanes[a]
                    pb = p_ref[i * heads + 2 * j + a]
                    p = pb.astype(f32)
                    dpr = dot_nt(g, v * lane)
                    pd = dpr * p
                    ds = ((pd - p * jnp.sum(pd, axis=-1, keepdims=True)) * SCALE).astype(bf16)
                    terms = (dot(ds, k * lane), dot_tn(ds, q * lane), dot_tn(pb, g * lane))
                    if a == 0:
                        dq, dk, dv = terms
                    else:
                        dq, dk, dv = dq + terms[0], dk + terms[1], dv + terms[2]
                pair(q_ref, r, q_base, j)[...] = dq.astype(bf16)
                pair(kv_ref, rk, kv_base, j)[...] = dk.astype(bf16)
                pair(kv_ref, rk, kv_base + d, j)[...] = dv.astype(bf16)
            return 0

        return lambda: lax.fori_loop(lo, hi, body, 0)

    thirds = [(i * pairs // 3, (i + 1) * pairs // 3) for i in range(3)]

    need("act", "cot")
    for j in range(3):
        grad_down(j)
    load("qkv", res["qkv"], q_at)
    need("wd0", "wd1", "wd2", "dg")
    for z in range(nz):
        hidden(z)
    need("n3")
    for j in range(4):
        grad_small(n_c - 7 + j, lambda: n3[...], dg, j * d, 1.4)
    need("up0", "up1", "up2", "up3", "x2", "grow")
    norm_grad(dg, ws[:4], xf, 2, True)
    load("x1", res["x1"], xf)
    load("ckv1", full[6], ws[0])
    load("cq", full[4], ws[1])
    load("so", full[3], ws[2])
    load("qkv0", full[0], ws[3])
    need("co")
    back_project(ws[4])
    load("qkv1", full[1], ws[4])
    need("o2")
    grad_small(7, lambda: o2[...], gxb, 0, 1.4)
    need("p2", "q2", "kv2")
    for lo, hi in thirds:
        plan.compute(4.0, pairs_back(lo, hi, p2, q2, 0, kv2, 0, pat))
    need("img")
    grad_small(5, lambda: img[...], kv2, 0, 2.0)
    grad_small(6, lambda: img[...], kv2, d, 2.0)
    need("ckv0", "ckv1")
    wide = d // 4

    def image_grad(i, _):
        r = span(i * kp, kp, 16)
        y = dot_nt(matrix(ws[5]), kv2[r, :d]) + dot_nt(matrix(ws[0]), kv2[r, d:])
        y = y.astype(bf16)
        for s in range(4):
            gi[s, i] = y[s * wide : (s + 1) * wide]
        return 0

    plan.compute(4.0, lambda: lax.fori_loop(0, b, image_grad, 0))
    keep = pltpu.make_async_copy(gi.at[seq], img_out.at[seq], osem.at[0])
    keep.start()
    moves = [
        remote(gi.at[lax.rem(seq + k, 4)], img_out.at[seq], (isem, jsem), k - 1, peers[k - 1])
        for k in range(1, 4)
    ]
    for mv in moves:
        mv.start()
    load("qkv2", full[2], ws[5])
    need("n2", "cq", "x1")
    norm_grad(q2, [ws[1]], xf, 1, False)
    need("so")
    back_project(ws[2])
    grad_small(4, lambda: n2[...], q2, 0, 1.4)
    need("o1")
    grad_small(3, lambda: o1[...], gxb, 0, 1.4)
    need("p1", "qkv")
    for lo, hi in thirds:
        plan.compute(3.0, pairs_back(lo, hi, p1, act, 0, act, d, tok))
    need("xs", "qkv0", "qkv1", "qkv2", "n1")
    norm_grad(act, [ws[3], ws[4], ws[5]], xs, 0, False)
    gx_copy = pltpu.make_async_copy(gx, gx_out, osem.at[1])
    gx_copy.start()

    def gain_terms():
        r = jnp.transpose(ggr[...])
        pg[...] = r.reshape(nz, 2, 2, 2, -1, LANES).astype(bf16)

    plan.compute(0.7, gain_terms)
    plan.emit(place[None])
    for j in range(3):
        grad_small(j, lambda: n1[...], act, j * d, 1.4)
    plan.finish()
    keep.wait()
    gx_copy.wait()
    for mv in moves:
        mv.wait()


PLANES = (0, 3)
BROAD = (7, 8, 9, 10, 11, 13)

RES_NAMES = (
    "n1", "qkv", "p1", "o1", "x1", "n2", "q2", "kv2",
    "p2", "o2", "x2", "n3", "act", "dg", "grow", "img",
)


def backward(nz, cot, patches, xs, weights, res, fulls):
    b, t, d = xs.shape
    kp, ff = padded(patches), weights[5].shape[1]
    m, heads = b * t, d // HEAD
    chunks = chunk_cols(weights, d)
    n_c = len(chunks)
    n = n_c + 1
    rows = weights[0].shape[0]
    down = (weights[6].shape[0], d // 3)
    tok, tokf = pltpu.VMEM((m, d), bf16), pltpu.VMEM((m, d), f32)
    part = lambda blk: pltpu.VMEM((nz, 2, 2, 2, *blk), bf16)
    blocks = [down] * 3 + [(rows, d)] * 9 + [(rows, LANES)] + [(rows, d)] * 3
    bufs = []
    for i, blk in enumerate(blocks):
        kind = ScatterPlane if i in PLANES else Scatter
        bufs += [pltpu.VMEM(s, bf16) for s in kind.shapes(nz, blk)]
    count = Scatter.count(nz)
    hbm, vm = pl.BlockSpec(memory_space=HBM), pl.BlockSpec(memory_space=VMEM)
    hid = pltpu.VMEM((m, ff), bf16)
    S = jax.ShapeDtypeStruct
    outs = pl.pallas_call(
        functools.partial(backward_kernel, nz, (b, t, d, kp, ff), chunks),
        out_shape=[
            S((m, d), f32), S((4, b, d // 4, kp), bf16),
            *(S(w.shape, f32) for w in weights), S((rows, LANES), f32),
        ],
        in_specs=[hbm] * (2 + N_RES + n_c),
        out_specs=[hbm, hbm, *([vm] * 8)],
        scratch_shapes=[
            tok, hid, hid, tok, tokf, tok, pltpu.VMEM((b * heads, t, kp), bf16), tok,
            pltpu.VMEM((b * kp, 2 * d), bf16), pltpu.VMEM((b * kp, d), bf16), tok, tok,
            pltpu.VMEM((b * heads, t, t), bf16), tok, tok, pltpu.VMEM((8, d), f32),
            tokf, tok, tok, pltpu.VMEM((4, b, d // 4, kp), bf16), pltpu.VMEM((LANES, d), f32),
            *([part(down)] * 3), *([part((rows, d))] * 6),
            *([part(down)] * 3), *([part((rows, d))] * 4), part((rows, LANES)),
            *bufs,
            pltpu.SemaphoreType.DMA((2 + N_RES + n_c,)),
            pltpu.SemaphoreType.DMA((n, count)),
            pltpu.SemaphoreType.DMA((n, count)),
            pltpu.SemaphoreType.DMA((3,)),
            pltpu.SemaphoreType.DMA((3,)),
            pltpu.SemaphoreType.DMA((2,)),
        ],
        compiler_params=pltpu.CompilerParams(
            collective_id=1, has_side_effects=True, vmem_limit_bytes=63 << 20
        ),
    )(cot.reshape(m, d), xs.reshape(m, d), *res, *fulls)
    return outs


def finish_kernel(n, *refs):
    ins, gi, gg = refs[:n], refs[n], refs[n + 1]
    outs, go, gains = refs[n + 2 : 2 * n + 2], refs[2 * n + 2], refs[2 * n + 3 : 2 * n + 6]
    held, pics, wide = refs[2 * n + 6 : 3 * n + 6], refs[3 * n + 6], refs[3 * n + 7]
    isem, osem = refs[3 * n + 8 :]
    arrive = [pltpu.make_async_copy(ins[i], held[i], isem.at[i]) for i in range(n)]
    leave = [pltpu.make_async_copy(held[i], outs[i], osem.at[i]) for i in range(n)]
    half = gi.shape[0] // 2
    parts = [pl.ds(k * half, half) for k in range(2)]
    p_in = [pltpu.make_async_copy(gi.at[r], pics.at[r], isem.at[n + k]) for k, r in enumerate(parts)]
    p_out = [pltpu.make_async_copy(wide.at[r], go.at[r], osem.at[n + k]) for k, r in enumerate(parts)]
    for cp in (*p_in, *arrive):
        cp.start()

    def widen(i, _):
        wide[i] = pics[i].astype(f32)[:, : wide.shape[2]]
        return 0

    for k in range(2):
        p_in[k].wait()
        lax.fori_loop(k * half, (k + 1) * half, widen, 0)
        p_out[k].start()
        for i in range(k * n // 2, (k + 1) * n // 2):
            arrive[i].wait()
            leave[i].start()
    row = jnp.transpose(gg[...])
    for k, r in enumerate(gains):
        r[...] = row[k, : r.shape[0]]
    for cp in (*p_out, *leave):
        cp.wait()


def finish(arrays, gi, gg, patches):
    n = len(arrays)
    hbm, vm = pl.BlockSpec(memory_space=HBM), pl.BlockSpec(memory_space=VMEM)
    S = jax.ShapeDtypeStruct
    vec = S((gg.shape[0],), f32)
    return pl.pallas_call(
        functools.partial(finish_kernel, n),
        out_shape=[
            *(S(a.shape, a.dtype) for a in arrays), S((*gi.shape[:2], patches), f32), vec, vec, vec
        ],
        in_specs=[*([hbm] * (n + 1)), vm],
        out_specs=[*([hbm] * (n + 1)), vm, vm, vm],
        scratch_shapes=[
            *(pltpu.VMEM(a.shape, a.dtype) for a in arrays),
            pltpu.VMEM(gi.shape, bf16), pltpu.VMEM((*gi.shape[:2], patches), f32),
            pltpu.SemaphoreType.DMA((n + 2,)), pltpu.SemaphoreType.DMA((n + 2,)),
        ],
        compiler_params=pltpu.CompilerParams(vmem_limit_bytes=62 << 20),
    )(*arrays, gi, gg)


def norm_stats(v):
    mean = jnp.mean(v, axis=-1, keepdims=True)
    centered = v - mean
    r = lax.rsqrt(jnp.mean(centered * centered, axis=-1, keepdims=True) + EPS)
    return centered * r, r


def norm_back(xhat, r, gain, e):
    u = e * gain
    mu = jnp.mean(u, axis=-1, keepdims=True)
    mx = jnp.mean(u * xhat, axis=-1, keepdims=True)
    return r * (u - mu - xhat * mx), jnp.sum(e * xhat, axis=(0, 1))


def mm(a, b):
    return jnp.einsum("btd,de->bte", a, b, preferred_element_type=f32)


def mm_t(a, b):
    return jnp.einsum("bte,de->btd", a, b, preferred_element_type=f32)


def wgrad(a, b):
    return jnp.einsum("btd,bte->de", a, b, preferred_element_type=f32)


def split_heads(a):
    b, t, _ = a.shape
    return a.reshape(b, t, -1, HEAD)


def attend(q, k, v, allowed):
    s = jnp.einsum("bqhe,bkhe->bhqk", q, k, preferred_element_type=f32) * HEAD ** (-0.5)
    s = jnp.where(allowed, s, -1e30)
    ex = jnp.exp(s - jnp.max(s, axis=-1, keepdims=True))
    p = ex / jnp.sum(ex, axis=-1, keepdims=True)
    o = jnp.einsum("bhqk,bkhe->bqhe", p.astype(bf16), v, preferred_element_type=f32)
    return p, o.astype(bf16)


def attend_back(q, k, v, p, g):
    dp = jnp.einsum("bqhe,bkhe->bhqk", g, v, preferred_element_type=f32)
    ds = (p * (dp - jnp.sum(dp * p, axis=-1, keepdims=True)) * HEAD ** (-0.5)).astype(bf16)
    dq = jnp.einsum("bhqk,bkhe->bqhe", ds, k, preferred_element_type=f32).astype(bf16)
    dk = jnp.einsum("bhqk,bqhe->bkhe", ds, q, preferred_element_type=f32).astype(bf16)
    dv = jnp.einsum("bhqk,bqhe->bkhe", p.astype(bf16), g, preferred_element_type=f32).astype(bf16)
    return dq, dk, dv


def layer(x0, img, mask, gains, weights, cot):
    g1, g2, g3 = (g.astype(f32) for g in gains)
    w_qkv, w_so, w_cq, w_ckv, w_co, w_up, w_down = weights
    b, t, d = x0.shape
    x = x0.astype(f32)
    pos = jnp.arange(t)
    causal = (pos[:, None] >= pos[None, :])[None, None]
    allowed = (mask > 0)[:, None, None, :]
    h1, r1 = norm_stats(x)
    n1 = (h1 * g1).astype(bf16)
    qkv = mm(n1, w_qkv).astype(bf16)
    q1, k1, v1 = (split_heads(qkv[..., i * d : (i + 1) * d]) for i in range(3))
    p1, o1 = attend(q1, k1, v1, causal)
    o1 = o1.reshape(b, t, d)
    x1 = x + mm(o1, w_so)
    h2, r2 = norm_stats(x1)
    n2 = (h2 * g2).astype(bf16)
    q2 = split_heads(mm(n2, w_cq).astype(bf16))
    kv = mm(img, w_ckv).astype(bf16)
    k2, v2 = split_heads(kv[..., :d]), split_heads(kv[..., d:])
    p2, o2 = attend(q2, k2, v2, allowed)
    o2 = o2.reshape(b, t, d)
    x2 = x1 + mm(o2, w_co)
    h3, r3 = norm_stats(x2)
    n3 = (h3 * g3).astype(bf16)
    hpre = mm(n3, w_up)
    cdf = 0.5 * (1.0 + lax.erf(hpre * (0.5**0.5)))
    act = (hpre * cdf).astype(bf16)
    out = (x2 + mm(act, w_down)).astype(bf16)

    gw_down = wgrad(act, cot)
    pdf = jnp.exp(-0.5 * hpre * hpre) * (0.5 / jnp.pi) ** 0.5
    gh = (mm_t(cot, w_down) * (cdf + hpre * pdf)).astype(bf16)
    gw_up = wgrad(n3, gh)
    dx2, gg3 = norm_back(h3, r3, g3, mm_t(gh, w_up))
    gx2 = cot.astype(f32) + dx2
    gx2b = gx2.astype(bf16)
    gw_co = wgrad(o2, gx2b)
    go2 = split_heads(mm_t(gx2b, w_co).astype(bf16))
    dq2, dk2, dv2 = attend_back(q2, k2, v2, p2, go2)
    dq2 = dq2.reshape(b, t, d)
    dkv = jnp.concatenate([dk2.reshape(b, -1, d), dv2.reshape(b, -1, d)], axis=-1)
    gw_ckv = wgrad(img, dkv)
    gimg = mm_t(dkv, w_ckv).astype(bf16)
    gw_cq = wgrad(n2, dq2)
    dx1, gg2 = norm_back(h2, r2, g2, mm_t(dq2, w_cq))
    gx1 = gx2 + dx1
    gx1b = gx1.astype(bf16)
    gw_so = wgrad(o1, gx1b)
    go1 = split_heads(mm_t(gx1b, w_so).astype(bf16))
    dq1, dk1, dv1 = attend_back(q1, k1, v1, p1, go1)
    dqkv = jnp.concatenate([a.reshape(b, t, d) for a in (dq1, dk1, dv1)], axis=-1)
    gw_qkv = wgrad(n1, dqkv)
    dx0, gg1 = norm_back(h1, r1, g1, mm_t(dqkv, w_qkv))
    gx0 = gx1 + dx0
    return out, gx0, gimg, (gg1, gg2, gg3), (gw_qkv, gw_so, gw_cq, gw_ckv, gw_co, gw_up, gw_down)


def native(captions, img, mask, gains, weights, cotangent):
    full = [lax.all_gather(w, BOTH, axis=0, tiled=True) for w in weights]
    gains = lax.all_gather(gains, BOTH, axis=0, tiled=True)
    gains = tuple(gains[:, i] for i in range(3))
    out, gx0, gimg, gg, gw = layer(captions, img, mask, gains, full, cotangent)
    gg = lax.psum_scatter(jnp.stack(gg, axis=1), BOTH, scatter_dimension=0, tiled=True)
    shards = [
        lax.psum_scatter(g.astype(bf16), BOTH, scatter_dimension=0, tiled=True).astype(f32)
        for g in gw
    ]
    gimg = lax.all_to_all(gimg, "seq", split_axis=2, concat_axis=0, tiled=True)
    return (out, gx0, gimg.astype(f32), gg[:, 0], gg[:, 1], gg[:, 2], *shards)


def on_device(captions, images, tissue_mask, gain_self, gain_cross, gain_mlp, *rest):
    weights, cotangent = rest[:-1], rest[-1]
    n_dp, n_seq = lax.axis_size("dp"), lax.axis_size("seq")
    b, t, d = captions.shape
    patches = images.shape[1]
    if n_seq != 4 or n_dp % 4 or any(w.shape[0] % 8 for w in weights):
        start = lax.axis_index("seq") * b
        img = lax.dynamic_slice_in_dim(images, start, b, 0)
        mask = lax.dynamic_slice_in_dim(tissue_mask, start, b, 0)
        gains = jnp.stack([gain_self, gain_cross, gain_mlp], axis=1)
        return native(captions, img, mask, gains, weights, cotangent)
    nz = n_dp // 2
    gains = (gain_self, gain_cross, gain_mlp)
    out, res, fulls = forward(nz, captions, images, tissue_mask, gains, weights)
    gx, gimg, *gw, gg = backward(nz, cotangent, patches, captions, weights, res, fulls[1:])
    gimg = gimg.reshape(4 * b, *gimg.shape[2:])
    out, gx, *gw, gimg, gs, gc, gm = finish([out, gx, *gw], gimg, gg, patches)
    out, gx = out.reshape(b, t, d), gx.reshape(b, t, d)
    return (out, gx, gimg.swapaxes(1, 2), gs, gc, gm, *gw)


def solution(mesh):
    tok = P(BOTH, None, None)
    vec = P(BOTH)
    mat = P(BOTH, None)
    return jax.shard_map(
        on_device,
        mesh=mesh,
        in_specs=(tok, P("dp", None, None), P("dp", None), vec, vec, vec, *([mat] * 7), tok),
        out_specs=(tok, tok, P("dp", None, "seq"), vec, vec, vec, *([mat] * 7)),
        check_vma=False,
    )
```

```python
import functools

import jax
import jax.numpy as jnp
from jax import lax
from jax.experimental import pallas as pl
from jax.experimental.pallas import tpu as pltpu
from jax.sharding import PartitionSpec as P

HEADS = 12
HEAD = 64
EPS = 1e-05
BOTH = ("dp", "seq")
f32 = jnp.float32
bf16 = jnp.bfloat16
MESH = pl.DeviceIdType.MESH
HBM = pltpu.MemorySpace.HBM
VMEM = pltpu.MemorySpace.VMEM
LANES = 128


class Place:
    def __init__(self, nz, wide=False):
        dp, seq = lax.axis_index("dp"), lax.axis_index("seq")
        self.nz = nz
        self.z, self.x = dp // 2, lax.rem(dp, 2)
        self.y, self.c = seq // 2, lax.rem(seq, 2)
        x, y = self.x, self.y
        self.role = role = 1 if wide else self.c
        self.p = x + role * (y - x)
        self.s = y + role * (x - y)
        self.sib = (dp, 2 * y + (1 - self.c))
        self.p_xy = (x + (1 - role) * (1 - 2 * x), y + role * (1 - 2 * y))
        self.s_xy = (x + role * (1 - 2 * x), y + (1 - role) * (1 - 2 * y))
        self.ps_xy = (1 - x, 1 - y)
        self.p_dev = self.dev(self.z, self.p_xy)
        self.s_dev = self.dev(self.z, self.s_xy)
        self.z_of = [lax.rem(self.z + k, nz) for k in range(nz)]
        self.z_devs = [self.dev(self.z_of[k], (x, y)) for k in range(nz)]

    def dev(self, z, xy):
        return (2 * z + xy[0], 2 * xy[1] + self.c)

    def column(self, p, s):
        return p + self.role * (s - p), s + self.role * (p - s)

    def partners(self):
        return [*self.z_devs[1:], self.p_dev, self.s_dev, self.sib]


def enter(partners):
    barrier = pltpu.get_barrier_semaphore()
    for d in partners:
        pl.semaphore_signal(barrier, inc=1, device_id=d, device_id_type=MESH)
    pl.semaphore_wait(barrier, len(partners))


def remote(src, dst, sems, i, dev):
    return pltpu.make_async_remote_copy(
        src_ref=src, dst_ref=dst, send_sem=sems[0].at[i], recv_sem=sems[1].at[i],
        device_id=dev, device_id_type=MESH,
    )


class Gather:
    LOADS = (("z", 8), ("xy", 8), ("xy", 4), ("core", 8), None)
    WORK = (0.3, 0.3, 0.2, 0.2, 0.1)

    def __init__(self, here, shard, full, sems, local):
        h = here
        x, y, c = h.x, h.y, h.c
        mine = full.at[h.z, x, y, c]

        def col(xy):
            return full.at[:, xy[0], xy[1], c]

        self.own = pltpu.make_async_copy(shard, mine, local)
        nz = h.nz
        self.zs = [remote(shard, mine, sems, k - 1, h.z_devs[k]) for k in range(1, nz)]
        own, px, sx, psx = (x, y), h.p_xy, h.s_xy, h.ps_xy
        n = nz - 1
        self.p_own = remote(col(own), col(own), sems, n, h.p_dev)
        self.s_own = remote(col(own), col(own), sems, n + 1, h.s_dev)
        self.s_p = remote(col(px), col(px), sems, n + 2, h.s_dev)
        self.sibs = [
            remote(col(xy), col(xy), sems, n + 3 + i, h.sib)
            for i, xy in enumerate((own, px, sx, psx))
        ]

    @staticmethod
    def count(nz):
        return nz + 6

    def step(self, i):
        if i == 0:
            self.own.start()
            for t in self.zs:
                t.start()
        elif i == 1:
            self.own.wait()
            for t in self.zs:
                t.wait_recv()
            self.p_own.start()
            self.s_own.start()
            self.sibs[0].start()
        elif i == 2:
            self.p_own.wait_recv()
            self.s_p.start()
            self.sibs[1].start()
        elif i == 3:
            self.s_own.wait_recv()
            self.sibs[2].start()
            self.s_p.wait_recv()
            self.sibs[3].start()
        elif i == 4:
            for t in self.sibs:
                t.wait_recv()
        elif i == 5:
            for t in (*self.zs, self.p_own, self.s_own, self.s_p, *self.sibs):
                t.wait_send()


class GatherPlane(Gather):
    LOADS = (("xy", 2), ("xy", 1), ("z", 32), ("core", 12), None)

    def __init__(self, here, shard, full, sems, local):
        h = here
        x, y, c, z = h.x, h.y, h.c, h.z
        mine = full.at[z, x, y, c]
        pb = full.at[z, h.p_xy[0], h.p_xy[1], c]

        def plane(i):
            return full.at[i, :, :, c]

        self.own = pltpu.make_async_copy(shard, mine, local)
        nz = h.nz
        self.p_own = remote(shard, mine, sems, 0, h.p_dev)
        self.s_own = remote(shard, mine, sems, 1, h.s_dev)
        self.s_p = remote(pb, pb, sems, 2, h.s_dev)
        self.zs = [remote(plane(z), plane(z), sems, 2 + k, h.z_devs[k]) for k in range(1, nz)]
        self.sibs = [
            remote(plane(h.z_of[-k]), plane(h.z_of[-k]), sems, 2 + nz + k, h.sib)
            for k in range(nz)
        ]

    def step(self, i):
        if i == 0:
            self.own.start()
            self.p_own.start()
            self.s_own.start()
        elif i == 1:
            self.p_own.wait_recv()
            self.s_p.start()
        elif i == 2:
            self.own.wait()
            self.s_own.wait_recv()
            self.s_p.wait_recv()
            for t in self.zs:
                t.start()
            self.sibs[0].start()
        elif i == 3:
            for k, t in enumerate(self.zs):
                t.wait_recv()
                self.sibs[k + 1].start()
        else:
            super().step(i)


def add_blocks(count, dst, a, b):
    def body(i, _):
        dst(i)[...] = (a(i)[...].astype(f32) + b(i)[...].astype(f32)).astype(bf16)
        return 0

    lax.fori_loop(0, count, body, 0)


class Scatter:
    LOADS = (("core", 16), ("xy", 8), ("xy", 4), ("z", 8), None)
    WORK = (0.3, 1.2, 0.7, 0.4, 0.3)

    @staticmethod
    def shapes(nz, blk):
        return (nz, 2, 2, *blk), (2, nz, *blk), (nz, *blk), (nz - 1, *blk)

    @staticmethod
    def count(nz):
        return nz + 3

    def __init__(self, here, part, bufs, out, sems):
        self.h, self.out = here, out
        self.rc, self.rs, self.rp, self.rz = bufs
        h, nz = here, here.nz
        self.own = part.at[:, :, :, h.c]
        self.core = remote(part.at[:, :, :, 1 - h.c], self.rc, sems, 0, h.sib)
        self.s = [
            remote(self.rc.at[:, *h.column(p, 1 - h.s)], self.rs.at[p], sems, 1 + i, h.s_dev)
            for i, p in enumerate((1 - h.p, h.p))
        ]
        self.pp = remote(self.rs.at[1 - h.p], self.rp, sems, 3, h.p_dev)
        self.zs = [
            remote(self.rp.at[h.z_of[k]], self.rz.at[k - 1], sems, 3 + k, h.z_devs[k])
            for k in range(1, nz)
        ]

    def sum_core(self):
        at = lambda r: lambda i: r.at[lax.div(i, 4), lax.rem(lax.div(i, 2), 2), lax.rem(i, 2)]
        add_blocks(4 * self.h.nz, at(self.rc), at(self.rc), at(self.own))

    def step(self, i):
        h, nz = self.h, self.h.nz
        if i == 0:
            self.core.start()
        elif i == 1:
            self.core.wait_recv()

            def side(q):
                def at(r):
                    return lambda i: r.at[lax.rem(i, nz), *h.column(lax.div(i, nz), q)]

                add_blocks(2 * nz, at(self.rc), at(self.rc), at(self.own))

            side(1 - h.s)
            for t in self.s:
                t.start()
            side(h.s)
            self.core.wait_send()
        elif i == 2:
            for t in self.s:
                t.wait_recv()

            def kept(i):
                return self.rc.at[lax.rem(i, nz), *h.column(lax.div(i, nz), h.s)]

            mine = lambda i: self.rs.at[lax.div(i, nz), lax.rem(i, nz)]
            add_blocks(2 * nz, mine, mine, kept)
            self.pp.start()
        elif i == 3:
            self.pp.wait_recv()
            mine = lambda i: self.rp.at[i]
            add_blocks(nz, mine, mine, lambda i: self.rs.at[h.p, i])
            for t in self.zs:
                t.start()
        elif i == 4:
            for t in self.zs:
                t.wait_recv()
            total = self.rp[h.z].astype(f32)
            for k in range(nz - 1):
                total = total + self.rz[k].astype(f32)
            self.out[...] = total
        elif i == 5:
            for t in (*self.s, self.pp, *self.zs):
                t.wait_send()


class ScatterPlane(Scatter):
    LOADS = (("core", 16), ("z", 32), ("xy", 2), ("xy", 1), None)

    @staticmethod
    def shapes(nz, blk):
        return (nz, 2, 2, *blk), (nz - 1, 2, 2, *blk), (2, *blk), blk

    def __init__(self, here, part, bufs, out, sems):
        self.h, self.out = here, out
        self.rc, self.rz, self.rs, self.rp = bufs
        h, nz = here, here.nz
        self.own = part.at[:, :, :, h.c]
        self.core = remote(part.at[:, :, :, 1 - h.c], self.rc, sems, 0, h.sib)
        self.zs = [
            remote(self.rc.at[h.z_of[k]], self.rz.at[k - 1], sems, k, h.z_devs[k])
            for k in range(1, nz)
        ]
        self.s = [
            remote(self.rc.at[h.z, *h.column(p, 1 - h.s)], self.rs.at[p], sems, nz + p, h.s_dev)
            for p in range(2)
        ]
        self.pp = remote(self.rs.at[1 - h.p], self.rp, sems, nz + 2, h.p_dev)

    def step(self, i):
        h, nz = self.h, self.h.nz
        if i == 1:
            self.core.wait_recv()
            self.sum_core()
            for t in self.zs:
                t.start()
            self.core.wait_send()
        elif i == 2:
            for t in self.zs:
                t.wait_recv()

            def body(i, _):
                mine = self.rc.at[h.z, lax.div(i, 2), lax.rem(i, 2)]
                total = mine[...].astype(f32)
                for k in range(nz - 1):
                    total = total + self.rz[k, lax.div(i, 2), lax.rem(i, 2)].astype(f32)
                mine[...] = total.astype(bf16)
                return 0

            lax.fori_loop(0, 4, body, 0)
            for t in self.s:
                t.start()
        elif i == 3:
            for t in self.s:
                t.wait_recv()
            mine = lambda i: self.rs.at[i]
            add_blocks(2, mine, mine, lambda i: self.rc.at[h.z, *h.column(i, h.s)])
            self.pp.start()
        elif i == 4:
            self.pp.wait_recv()
            self.out[...] = self.rs[h.p].astype(f32) + self.rp[...].astype(f32)
        else:
            super().step(i)


class Planner:
    UNIT = {"xy": 0.8, "z": 0.8, "core": 0.1}

    def __init__(self, chunks, sizes, hop):
        self.chunks, self.sizes, self.hop = chunks, sizes, hop
        self.now, self.free = 0.0, dict.fromkeys(self.UNIT, 0.0)
        self.ready, self.queue, self.arrived = {}, [], None
        self.held, self.ahead = [], 0

    def emit(self, i):
        step, when = self.ready.get(i, (0, 0.0))
        chunk, size = self.chunks[i], self.sizes[i]
        self.now = max(self.now, when) + chunk.WORK[step] * size
        chunk.step(step)
        load = chunk.LOADS[step]
        if load is None:
            del self.ready[i]
            if self.arrived:
                self.arrived(i)
            return
        if step == 1 and i + self.ahead in self.held:
            self.held.remove(i + self.ahead)
            self.emit(i + self.ahead)
        link, amount = load
        self.free[link] = max(self.free[link], self.now) + self.UNIT[link] * amount * size
        self.ready[i] = (step + 1, self.free[link] + self.hop)

    def settle(self):
        while True:
            due = [(-s, i) for i, (s, when) in self.ready.items() if when <= self.now]
            if not due:
                return
            self.emit(min(due)[1])

    def free_slot(self, i):
        while i in self.ready and self.ready[i][0] == 1:
            self.emit(i)

    def compute(self, cost, work):
        self.settle()
        work()
        self.now += cost

    def later(self, cost, work):
        self.queue.append((cost, work))

    def finish(self):
        while self.ready or self.queue:
            self.settle()
            if self.queue:
                self.compute(*self.queue.pop(0))
            elif self.ready:
                self.emit(min(self.ready, key=lambda k: (self.ready[k][1], k)))
        for c in self.chunks:
            c.step(5)


def stats(v):
    mean = jnp.mean(v, axis=-1, keepdims=True)
    cen = v - mean
    r = lax.rsqrt(jnp.mean(cen * cen, axis=-1, keepdims=True) + EPS)
    return cen * r, r


def dot(a, b):
    return jnp.dot(a, b, preferred_element_type=f32)


def dot_nt(a, b):
    return lax.dot_general(a, b, (((1,), (1,)), ((), ())), preferred_element_type=f32)


def dot_tn(a, b):
    return lax.dot_general(a, b, (((0,), (0,)), ((), ())), preferred_element_type=f32)


def matrix(ref, lo=None, size=None):
    v = ref[...] if lo is None else ref[..., pl.ds(lo, size)]
    return v.reshape(-1, v.shape[-1])


def tiles(total, size, work):
    def body(i, _):
        work(pl.multiple_of(i * size, size))
        return 0

    lax.fori_loop(0, total // size, body, 0)


def span(start, size, unit=2 * HEAD):
    return pl.ds(pl.multiple_of(start, unit), size)


def head_lanes():
    lane = lax.broadcasted_iota(jnp.int32, (1, 2 * HEAD), 1)
    low = jnp.where(lane < HEAD, 1.0, 0.0)
    return low.astype(bf16), (1.0 - low).astype(bf16)


def softmax(s):
    e = jnp.exp(s - jnp.max(s, axis=-1, keepdims=True))
    return (e * (1.0 / jnp.sum(e, axis=-1, keepdims=True))).astype(bf16)


def pair(ref, rows, base, j):
    return ref.at[rows, pl.ds(pl.multiple_of(base + j * 2 * HEAD, 2 * HEAD), 2 * HEAD)]


SCALE = HEAD ** (-0.5)


def chunk_cols(weights, d):
    out = []
    for i, w in enumerate(weights):
        wide = d if w.shape[1] % d == 0 and i < 6 else d // 3
        out += [(i, s, wide) for s in range(0, w.shape[1], wide)]
    return out


def forward_kernel(nz, dims, chunks, *refs):
    b, t, d, kp, ff = dims
    n = len(chunks) + 1
    xs, mask = refs[:2]
    gains = refs[2:5]
    images = refs[5]
    shards = refs[6:13]
    out = refs[13]
    res = refs[14 : 14 + N_RES]
    fulls = refs[14 + N_RES : 14 + N_RES + n]
    rest = refs[14 + N_RES + n :]
    (n1, qkv, p1, o1, x1, n2, q2, kv2, p2, o2, x2, n3, act, dg, grow, img) = keep = rest[:N_RES]
    g = rest[N_RES : N_RES + n]
    raw, mb, gsh, turn, local, ssem, rsem, csem, isem = rest[N_RES + n :]
    here = Place(nz)
    seq = lax.axis_index("seq")
    patches = mask.shape[1]
    turn[...] = jnp.zeros(turn.shape, f32)
    for i, gain in enumerate(gains):
        turn[i : i + 1, : gain.shape[0]] = gain[...].astype(f32).reshape(1, -1)
    gsh[...] = jnp.zeros(gsh.shape, bf16)
    gsh[:, :8] = jnp.transpose(turn[...])[: gsh.shape[0]].astype(bf16)
    enter(here.partners())
    srcs = [gsh] + [shards[i].at[:, s : s + w] for i, s, w in chunks]
    gs = []
    for i in range(n):
        kind = GatherPlane if i in (11, 12) else Gather
        gs.append(kind(here, srcs[i], g[i], (ssem.at[i], rsem.at[i]), local.at[i]))
    sizes = [gsh.shape[-1] / d] + [r.shape[-1] * r.shape[-2] / (d * gsh.shape[0]) for r in g[1:]]
    plan = Planner(gs, sizes, 5.0)
    plan.ahead = AHEAD
    plan.held = [i for i in range(AHEAD, n) if i not in (11, 12)]
    for i in range(n):
        if i not in plan.held:
            plan.emit(i)
    pictures = pltpu.make_async_copy(images.at[pl.ds(seq * b, b)], raw, isem.at[0])
    pictures.start()
    mb[...] = jnp.full(mb.shape, -1e30, f32)
    for i in range(b):
        row = mask[pl.ds(seq * b + i, 1), :]
        mb[i : i + 1, :patches] = jnp.where(row > 0, 0.0, -1e30)
    copies = []

    def flush(src, dst):
        cp = pltpu.make_async_copy(src, dst, csem.at[len(copies)])
        cp.start()
        copies.append(cp)

    def save(*which):
        for k in which:
            flush(keep[k], res[k])

    names = {}
    for k, (i, s, wide) in enumerate(chunks):
        names.setdefault(i, []).append(k + 1)
    lanes = head_lanes()
    heads = d // HEAD
    pairs = heads // 2
    tok = [slice(i * t, (i + 1) * t) for i in range(b)]
    pat = [slice(i * kp, (i + 1) * kp) for i in range(b)]

    def first():
        grow[...] = jnp.transpose(matrix(g[0]).astype(f32))[:8]

        def rows(r):
            h, _ = stats(xs[pl.ds(r, t)].astype(f32))
            n1[pl.ds(r, t)] = (h * grow[0:1]).astype(bf16)

        tiles(b * t, t, rows)
        save(0, 14)

    def project(src, k, dst, at):
        def tile(s):
            v = src()
            dst[:, span(at + s, 256)] = dot(v, matrix(g[k], s, 256)).astype(bf16)

        return lambda: tiles(g[k].shape[-1], 256, tile)

    def self_pairs(lo, hi):
        def body(j, _):
            causal = lax.broadcasted_iota(jnp.int32, (t, t), 0) >= lax.broadcasted_iota(
                jnp.int32, (t, t), 1
            )
            for i, r in enumerate(tok):
                q, k, v = (pair(qkv, r, m * d, j)[...] for m in range(3))
                o = jnp.zeros((t, 2 * HEAD), f32)
                for a in range(2):
                    s = dot_nt(q, k * lanes[a]) * SCALE
                    p = softmax(jnp.where(causal, s, -1e30))
                    p1[i * heads + 2 * j + a] = p
                    o = o + dot(p, v * lanes[a])
                pair(o1, r, 0, j)[...] = o.astype(bf16)
            return 0

        return lambda: lax.fori_loop(lo, hi, body, 0)

    def cross_pairs(lo, hi):
        def body(j, _):
            for i, r in enumerate(tok):
                q = pair(q2, r, 0, j)[...]
                k, v = (pair(kv2, pat[i], m * d, j)[...] for m in range(2))
                bias = mb[i : i + 1]
                o = jnp.zeros((t, 2 * HEAD), f32)
                for a in range(2):
                    p = softmax(dot_nt(q, k * lanes[a]) * SCALE + bias)
                    p2[i * heads + 2 * j + a] = p
                    o = o + dot(p, v * lanes[a])
                pair(o2, r, 0, j)[...] = o.astype(bf16)
            return 0

        return lambda: lax.fori_loop(lo, hi, body, 0)

    def residual(base, o, k, dst, row, normed):
        def rows(s):
            r = pl.ds(s, t)
            v = base[r].astype(f32) + dot(o[r], matrix(g[k]))
            dst[r] = v
            h, _ = stats(v)
            normed[r] = (h * grow[row : row + 1]).astype(bf16)

        return lambda: tiles(b * t, t, rows)

    def mlp_up(k, at):
        def tile(s):
            h = dot(n3[...], matrix(g[k], s, 256))
            cols = span(at + s, 256)
            cdf = 0.5 * (1.0 + lax.erf(h * (0.5**0.5)))
            act[:, cols] = (h * cdf).astype(bf16)
            pdf = jnp.exp(-0.5 * h * h) * (0.5 / jnp.pi) ** 0.5
            dg[:, cols] = (cdf + h * pdf).astype(bf16)

        return lambda: tiles(g[k].shape[-1], 256, tile)

    def mlp_down(k, at):
        wide = g[k].shape[-1]

        def rows(s):
            r = pl.ds(s, t)
            y = x2[r, at : at + wide] + dot(act[r], matrix(g[k]))
            out[r, at : at + wide] = y.astype(bf16)

        return lambda: tiles(b * t, t, rows)

    def images_here():
        pictures.wait()
        whole = patches // 16 * 16
        for i in range(b):
            img[i * kp : i * kp + whole] = raw[i, :whole]
            if whole < patches:
                img[i * kp + whole : (i + 1) * kp] = jnp.zeros((kp - whole, d), bf16)
                img[i * kp + whole : i * kp + patches] = raw[i, whole:]
        save(15)

    third = [(i * pairs // 3, (i + 1) * pairs // 3) for i in range(3)]

    landed = set()

    def arrived(c):
        flush(g[c], fulls[c])
        landed.add(c)
        while queued[0] in landed:
            use(queued[0])
            queued[0] += 1

    queued = [0]

    def use(c):
        add = plan.later
        if c == 0:
            add(2.0, first)
            add(0.0, images_here)
            return
        i, s, wide = chunks[c - 1]
        last = c == names[i][-1]
        if i == 0:
            add(1.7, project(lambda: n1[...], c, qkv, s))
            if last:
                add(0.0, lambda: save(1))
                for lo, hi in third:
                    add(2.5, self_pairs(lo, hi))
                add(0.0, lambda: save(2, 3))
        elif i == 1:
            add(2.5, residual(xs, o1, c, x1, 1, n2))
            add(0.0, lambda: save(4, 5))
        elif i == 2:
            add(1.7, project(lambda: n2[...], c, q2, 0))
            add(0.0, lambda: save(6))
        elif i == 3:
            add(2.5, project(lambda: img[...], c, kv2, s))
            if last:
                add(0.0, lambda: save(7))
                for lo, hi in third:
                    add(3.0, cross_pairs(lo, hi))
                add(0.0, lambda: save(8, 9))
        elif i == 4:
            add(2.5, residual(x1, o2, c, x2, 2, n3))
            add(0.0, lambda: save(10, 11))
        elif i == 5:
            add(3.5, mlp_up(c, s))
            if last:
                add(0.0, lambda: save(12, 13))
        else:
            add(2.0, mlp_down(c, s))

    plan.arrived = arrived
    plan.finish()
    for cp in copies:
        cp.wait()


N_RES = 16
AHEAD = 99


def residual_shapes(b, t, d, kp, ff):
    m, heads = b * t, d // HEAD
    S = jax.ShapeDtypeStruct
    tok, tokf = S((m, d), bf16), S((m, d), f32)
    return [
        tok, S((m, 3 * d), bf16), S((b * heads, t, t), bf16), tok, tokf, tok, tok,
        S((b * kp, 2 * d), bf16), S((b * heads, t, kp), bf16), tok, tokf, tok,
        S((m, ff), bf16), S((m, ff), bf16), S((8, d), f32), S((b * kp, d), bf16),
    ]


def forward(nz, xs, images, mask, gains, weights):
    b, t, d = xs.shape
    kp, ff = padded(images.shape[1]), weights[5].shape[1]
    chunks = chunk_cols(weights, d)
    n = len(chunks) + 1
    res = residual_shapes(b, t, d, kp, ff)
    block = (weights[0].shape[0], LANES)
    blocks = [block] + [(weights[i].shape[0], w) for i, _, w in chunks]
    fulls = [jax.ShapeDtypeStruct((nz, 2, 2, 2, *s), bf16) for s in blocks]
    count = Gather.count(nz)
    hbm, vm = pl.BlockSpec(memory_space=HBM), pl.BlockSpec(memory_space=VMEM)
    outs = pl.pallas_call(
        functools.partial(forward_kernel, nz, (b, t, d, kp, ff), chunks),
        out_shape=[jax.ShapeDtypeStruct((b * t, d), bf16), *res, *fulls],
        in_specs=[*([vm] * 5), *([hbm] * 8)],
        out_specs=[vm, *([hbm] * (N_RES + n))],
        scratch_shapes=[
            *(pltpu.VMEM(s.shape, s.dtype) for s in (*res, *fulls)),
            pltpu.VMEM((b, *images.shape[1:]), bf16),
            pltpu.VMEM((b + -b % 8, kp), f32),
            pltpu.VMEM(block, bf16),
            pltpu.VMEM((8, LANES), f32),
            pltpu.SemaphoreType.DMA((n,)),
            pltpu.SemaphoreType.DMA((n, count)),
            pltpu.SemaphoreType.DMA((n, count)),
            pltpu.SemaphoreType.DMA((N_RES + n,)),
            pltpu.SemaphoreType.DMA((1,)),
        ],
        compiler_params=pltpu.CompilerParams(
            collective_id=0, has_side_effects=True, vmem_limit_bytes=60 << 20
        ),
    )(xs.reshape(b * t, d), mask, *gains, images, *weights)
    return outs[0], outs[1 : 1 + N_RES], outs[1 + N_RES :]


def padded(patches):
    return patches + -patches % 16


def backward_kernel(nz, dims, chunks, *refs):
    b, t, d, kp, ff = dims
    heads = d // HEAD
    pairs = heads // 2
    m = b * t
    n_c = len(chunks)
    order = [*range(n_c - 3, n_c), *range(n_c - 7, n_c - 3), 7, 5, 6, 4, 3, None, 0, 1, 2]
    n = len(order)
    h_in = refs[: 2 + N_RES + n_c]
    h_cot, h_xs = h_in[:2]
    res = dict(zip(RES_NAMES, h_in[2 : 2 + N_RES]))
    full = h_in[2 + N_RES :]
    at = len(h_in)
    gx_out, img_out = refs[at : at + 2]
    outs = refs[at + 2 : at + 9]
    gg_out = refs[at + 9]
    rest = list(refs[at + 10 :])
    take = lambda k: [rest.pop(0) for _ in range(k)]
    cot, act, dg, n3, xf, o2, p2, q2, kv2, img, n2, o1, p1, n1, xs, grow = take(16)
    gx, gxb, go, gi, ggr = take(5)
    wd, ws = take(3), take(6)
    pd, ps, pg = take(3), take(4), take(1)[0]
    bufs = [take(4) for _ in range(n)]
    lsem, ssem, rsem, isem, jsem, osem = rest
    here, broad = Place(nz), Place(nz, wide=True)
    dp, seq = lax.axis_index("dp"), lax.axis_index("seq")
    peers = [(dp, lax.rem(seq + k, 4)) for k in range(1, 4)]

    loads, waits = {}, {}

    def load(name, src, dst):
        cp = pltpu.make_async_copy(src, dst, lsem.at[len(loads)])
        loads[name] = cp
        cp.start()

    def need(*names):
        for k in names:
            if k in loads and k not in waits:
                loads[k].wait()
                waits[k] = True

    q_at = act.at[:, : 3 * d]
    load("act", res["act"], act)
    load("cot", h_cot, cot)
    for j in range(3):
        load("wd%d" % j, full[n_c - 3 + j], wd[j])
    load("dg", res["dg"], dg)
    load("n3", res["n3"], n3)
    for j in range(4):
        load("up%d" % j, full[n_c - 7 + j], ws[j])
    load("x2", res["x2"], xf)
    load("grow", res["grow"], grow)
    for name, dst in (("o2", o2), ("p2", p2), ("q2", q2), ("kv2", kv2)):
        load(name, res[name], dst)
    load("img", res["img"], img)
    load("co", full[7], ws[4])
    load("ckv0", full[5], ws[5])
    for name, dst in (("n2", n2), ("o1", o1), ("p1", p1), ("n1", n1)):
        load(name, res[name], dst)
    load("xs", h_xs, xs)
    enter([*here.partners(), *peers])
    ggr[...] = jnp.zeros_like(ggr)

    parts, small = [], 0
    for k in order:
        if k is None:
            parts.append(pg)
        elif k >= n_c - 3:
            parts.append(pd[k - (n_c - 3)])
        else:
            parts.append(ps[small % 4])
            small += 1
    place = {k: i for i, k in enumerate(order)}
    dst = [
        gg_out if k is None else outs[chunks[k][0]].at[:, chunks[k][1] : chunks[k][1] + chunks[k][2]]
        for k in order
    ]
    sc = []
    for i in range(n):
        kind = ScatterPlane if i in PLANES else Scatter
        at = broad if i in BROAD else here
        sc.append(kind(at, parts[i], bufs[i], dst[i], (ssem.at[i], rsem.at[i])))
    sizes = [0.2 if k is None else 1.35 if k >= n_c - 3 else 1.0 for k in order]
    plan = Planner(sc, sizes, 3.0)
    smalls = [i for i, k in enumerate(order) if k is not None and k < n_c - 3]

    def slot_ready(i):
        if i in smalls and smalls.index(i) >= 4:
            plan.free_slot(smalls[smalls.index(i) - 4])

    lanes = head_lanes()
    tok = [slice(i * t, (i + 1) * t) for i in range(b)]
    pat = [slice(i * kp, (i + 1) * kp) for i in range(b)]

    def grad_small(k, x, dy, first, cost):
        i = place[k]
        slot_ready(i)

        def work():
            rows = x()
            for s in range(0, d, 256):
                r = dot_tn(rows, dy[:, first + s : first + s + 256])
                parts[i][:, :, :, :, :, s : s + 256] = r.reshape(nz, 2, 2, 2, -1, 256).astype(bf16)

        plan.compute(cost, work)
        plan.emit(i)

    def grad_down(j):
        k = n_c - 3 + j
        i = place[k]
        wide = d // 3

        rows = ff // nz

        def work(z, _):
            r = dot_tn(act[:, span(z * rows, rows)], cot[:, j * wide : (j + 1) * wide])
            parts[i][z] = r.reshape(2, 2, 2, -1, wide).astype(bf16)
            return 0

        plan.compute(1.8, lambda: lax.fori_loop(0, nz, work, 0))
        plan.emit(i)

    def hidden(z):
        half, wide = ff // nz // 2, d // 3

        def work(x, _):
            g = None
            for j in range(3):
                w = wd[j][z, x].reshape(half, wide)
                term = dot_nt(cot[:, j * wide : (j + 1) * wide], w)
                g = term if g is None else g + term
            at = span((2 * z + x) * half, half)
            dg[:, at] = (g * dg[:, at].astype(f32)).astype(bf16)
            return 0

        plan.compute(1.3, lambda: lax.fori_loop(0, 2, work, 0))

    def norm_grad(src, ups, base, row, first):
        ggr[row : row + 1] = jnp.zeros((1, d), f32)

        def work(s):
            r = pl.ds(s, t)
            e = None
            for j, w in enumerate(ups):
                term = dot_nt(src[r, j * d : (j + 1) * d], matrix(w))
                e = term if e is None else e + term
            h, rs = stats(base[r].astype(f32))
            u = e * grow[row : row + 1]
            mu = jnp.mean(u, axis=-1, keepdims=True)
            mx = jnp.mean(u * h, axis=-1, keepdims=True)
            prev = cot[r].astype(f32) if first else gx[r]
            v = prev + rs * (u - mu - h * mx)
            gx[r] = v
            gxb[r] = v.astype(bf16)
            ggr[row : row + 1] += jnp.sum(e * h, axis=0, keepdims=True)

        plan.compute(1.5 + 1.2 * len(ups), lambda: tiles(m, t, work))

    def back_project(w):
        half = d // 2

        def work(s, _):
            rows = w[pl.ds(s * (nz // 2), nz // 2)].reshape(half, d)
            go[:, span(s * half, half)] = dot_nt(gxb[...], rows).astype(bf16)
            return 0

        plan.compute(1.4, lambda: lax.fori_loop(0, 2, work, 0))

    def pairs_back(lo, hi, p_ref, q_ref, q_base, kv_ref, kv_base, rows):
        def body(j, _):
            for i, r in enumerate(tok):
                rk = rows[i]
                q, g = pair(q_ref, r, q_base, j)[...], pair(go, r, 0, j)[...]
                k, v = (pair(kv_ref, rk, kv_base + x * d, j)[...] for x in range(2))
                dq = dk = dv = None
                for a in range(2):
                    lane = lanes[a]
                    pb = p_ref[i * heads + 2 * j + a]
                    p = pb.astype(f32)
                    dpr = dot_nt(g, v * lane)
                    pd = dpr * p
                    ds = ((pd - p * jnp.sum(pd, axis=-1, keepdims=True)) * SCALE).astype(bf16)
                    terms = (dot(ds, k * lane), dot_tn(ds, q * lane), dot_tn(pb, g * lane))
                    if a == 0:
                        dq, dk, dv = terms
                    else:
                        dq, dk, dv = dq + terms[0], dk + terms[1], dv + terms[2]
                pair(q_ref, r, q_base, j)[...] = dq.astype(bf16)
                pair(kv_ref, rk, kv_base, j)[...] = dk.astype(bf16)
                pair(kv_ref, rk, kv_base + d, j)[...] = dv.astype(bf16)
            return 0

        return lambda: lax.fori_loop(lo, hi, body, 0)

    thirds = [(i * pairs // 3, (i + 1) * pairs // 3) for i in range(3)]

    need("act", "cot")
    for j in range(3):
        grad_down(j)
    load("qkv", res["qkv"], q_at)
    need("wd0", "wd1", "wd2", "dg")
    for z in range(nz):
        hidden(z)
    need("n3")
    for j in range(4):
        grad_small(n_c - 7 + j, lambda: n3[...], dg, j * d, 1.4)
    need("up0", "up1", "up2", "up3", "x2", "grow")
    norm_grad(dg, ws[:4], xf, 2, True)
    load("x1", res["x1"], xf)
    load("ckv1", full[6], ws[0])
    load("cq", full[4], ws[1])
    load("so", full[3], ws[2])
    load("qkv0", full[0], ws[3])
    need("co")
    back_project(ws[4])
    load("qkv1", full[1], ws[4])
    need("o2")
    grad_small(7, lambda: o2[...], gxb, 0, 1.4)
    need("p2", "q2", "kv2")
    for lo, hi in thirds:
        plan.compute(4.0, pairs_back(lo, hi, p2, q2, 0, kv2, 0, pat))
    need("img")
    grad_small(5, lambda: img[...], kv2, 0, 2.0)
    grad_small(6, lambda: img[...], kv2, d, 2.0)
    need("ckv0", "ckv1")
    wide = d // 4

    def image_grad(i, _):
        r = span(i * kp, kp, 16)
        y = dot_nt(matrix(ws[5]), kv2[r, :d]) + dot_nt(matrix(ws[0]), kv2[r, d:])
        y = y.astype(bf16)
        for s in range(4):
            gi[s, i] = y[s * wide : (s + 1) * wide]
        return 0

    plan.compute(4.0, lambda: lax.fori_loop(0, b, image_grad, 0))
    keep = pltpu.make_async_copy(gi.at[seq], img_out.at[seq], osem.at[0])
    keep.start()
    moves = [
        remote(gi.at[lax.rem(seq + k, 4)], img_out.at[seq], (isem, jsem), k - 1, peers[k - 1])
        for k in range(1, 4)
    ]
    for mv in moves:
        mv.start()
    load("qkv2", full[2], ws[5])
    need("n2", "cq", "x1")
    norm_grad(q2, [ws[1]], xf, 1, False)
    need("so")
    back_project(ws[2])
    grad_small(4, lambda: n2[...], q2, 0, 1.4)
    need("o1")
    grad_small(3, lambda: o1[...], gxb, 0, 1.4)
    need("p1", "qkv")
    for lo, hi in thirds:
        plan.compute(3.0, pairs_back(lo, hi, p1, act, 0, act, d, tok))
    need("xs", "qkv0", "qkv1", "qkv2", "n1")
    norm_grad(act, [ws[3], ws[4], ws[5]], xs, 0, False)
    gx_copy = pltpu.make_async_copy(gx, gx_out, osem.at[1])
    gx_copy.start()

    def gain_terms():
        r = jnp.transpose(ggr[...])
        pg[...] = r.reshape(nz, 2, 2, 2, -1, LANES).astype(bf16)

    plan.compute(0.7, gain_terms)
    plan.emit(place[None])
    for j in range(3):
        grad_small(j, lambda: n1[...], act, j * d, 1.4)
    plan.finish()
    keep.wait()
    gx_copy.wait()
    for mv in moves:
        mv.wait()


PLANES = (0, 3)
BROAD = (7, 8, 9, 10, 11, 13)

RES_NAMES = (
    "n1", "qkv", "p1", "o1", "x1", "n2", "q2", "kv2",
    "p2", "o2", "x2", "n3", "act", "dg", "grow", "img",
)


def backward(nz, cot, patches, xs, weights, res, fulls):
    b, t, d = xs.shape
    kp, ff = padded(patches), weights[5].shape[1]
    m, heads = b * t, d // HEAD
    chunks = chunk_cols(weights, d)
    n_c = len(chunks)
    n = n_c + 1
    rows = weights[0].shape[0]
    down = (weights[6].shape[0], d // 3)
    tok, tokf = pltpu.VMEM((m, d), bf16), pltpu.VMEM((m, d), f32)
    part = lambda blk: pltpu.VMEM((nz, 2, 2, 2, *blk), bf16)
    blocks = [down] * 3 + [(rows, d)] * 9 + [(rows, LANES)] + [(rows, d)] * 3
    bufs = []
    for i, blk in enumerate(blocks):
        kind = ScatterPlane if i in PLANES else Scatter
        bufs += [pltpu.VMEM(s, bf16) for s in kind.shapes(nz, blk)]
    count = Scatter.count(nz)
    hbm, vm = pl.BlockSpec(memory_space=HBM), pl.BlockSpec(memory_space=VMEM)
    hid = pltpu.VMEM((m, ff), bf16)
    S = jax.ShapeDtypeStruct
    outs = pl.pallas_call(
        functools.partial(backward_kernel, nz, (b, t, d, kp, ff), chunks),
        out_shape=[
            S((m, d), f32), S((4, b, d // 4, kp), bf16),
            *(S(w.shape, f32) for w in weights), S((rows, LANES), f32),
        ],
        in_specs=[hbm] * (2 + N_RES + n_c),
        out_specs=[hbm, hbm, *([vm] * 8)],
        scratch_shapes=[
            tok, hid, hid, tok, tokf, tok, pltpu.VMEM((b * heads, t, kp), bf16), tok,
            pltpu.VMEM((b * kp, 2 * d), bf16), pltpu.VMEM((b * kp, d), bf16), tok, tok,
            pltpu.VMEM((b * heads, t, t), bf16), tok, tok, pltpu.VMEM((8, d), f32),
            tokf, tok, tok, pltpu.VMEM((4, b, d // 4, kp), bf16), pltpu.VMEM((LANES, d), f32),
            *([part(down)] * 3), *([part((rows, d))] * 6),
            *([part(down)] * 3), *([part((rows, d))] * 4), part((rows, LANES)),
            *bufs,
            pltpu.SemaphoreType.DMA((2 + N_RES + n_c,)),
            pltpu.SemaphoreType.DMA((n, count)),
            pltpu.SemaphoreType.DMA((n, count)),
            pltpu.SemaphoreType.DMA((3,)),
            pltpu.SemaphoreType.DMA((3,)),
            pltpu.SemaphoreType.DMA((2,)),
        ],
        compiler_params=pltpu.CompilerParams(
            collective_id=1, has_side_effects=True, vmem_limit_bytes=63 << 20
        ),
    )(cot.reshape(m, d), xs.reshape(m, d), *res, *fulls)
    return outs


def finish_kernel(n, *refs):
    ins, gi, gg = refs[:n], refs[n], refs[n + 1]
    outs, go, gains = refs[n + 2 : 2 * n + 2], refs[2 * n + 2], refs[2 * n + 3 : 2 * n + 6]
    held, pics, wide = refs[2 * n + 6 : 3 * n + 6], refs[3 * n + 6], refs[3 * n + 7]
    isem, osem = refs[3 * n + 8 :]
    arrive = [pltpu.make_async_copy(ins[i], held[i], isem.at[i]) for i in range(n)]
    leave = [pltpu.make_async_copy(held[i], outs[i], osem.at[i]) for i in range(n)]
    half = gi.shape[0] // 2
    parts = [pl.ds(k * half, half) for k in range(2)]
    p_in = [pltpu.make_async_copy(gi.at[r], pics.at[r], isem.at[n + k]) for k, r in enumerate(parts)]
    p_out = [pltpu.make_async_copy(wide.at[r], go.at[r], osem.at[n + k]) for k, r in enumerate(parts)]
    for cp in (*p_in, *arrive):
        cp.start()

    def widen(i, _):
        wide[i] = pics[i].astype(f32)[:, : wide.shape[2]]
        return 0

    for k in range(2):
        p_in[k].wait()
        lax.fori_loop(k * half, (k + 1) * half, widen, 0)
        p_out[k].start()
        for i in range(k * n // 2, (k + 1) * n // 2):
            arrive[i].wait()
            leave[i].start()
    row = jnp.transpose(gg[...])
    for k, r in enumerate(gains):
        r[...] = row[k, : r.shape[0]]
    for cp in (*p_out, *leave):
        cp.wait()


def finish(arrays, gi, gg, patches):
    n = len(arrays)
    hbm, vm = pl.BlockSpec(memory_space=HBM), pl.BlockSpec(memory_space=VMEM)
    S = jax.ShapeDtypeStruct
    vec = S((gg.shape[0],), f32)
    return pl.pallas_call(
        functools.partial(finish_kernel, n),
        out_shape=[
            *(S(a.shape, a.dtype) for a in arrays), S((*gi.shape[:2], patches), f32), vec, vec, vec
        ],
        in_specs=[*([hbm] * (n + 1)), vm],
        out_specs=[*([hbm] * (n + 1)), vm, vm, vm],
        scratch_shapes=[
            *(pltpu.VMEM(a.shape, a.dtype) for a in arrays),
            pltpu.VMEM(gi.shape, bf16), pltpu.VMEM((*gi.shape[:2], patches), f32),
            pltpu.SemaphoreType.DMA((n + 2,)), pltpu.SemaphoreType.DMA((n + 2,)),
        ],
        compiler_params=pltpu.CompilerParams(vmem_limit_bytes=62 << 20),
    )(*arrays, gi, gg)


def norm_stats(v):
    mean = jnp.mean(v, axis=-1, keepdims=True)
    centered = v - mean
    r = lax.rsqrt(jnp.mean(centered * centered, axis=-1, keepdims=True) + EPS)
    return centered * r, r


def norm_back(xhat, r, gain, e):
    u = e * gain
    mu = jnp.mean(u, axis=-1, keepdims=True)
    mx = jnp.mean(u * xhat, axis=-1, keepdims=True)
    return r * (u - mu - xhat * mx), jnp.sum(e * xhat, axis=(0, 1))


def mm(a, b):
    return jnp.einsum("btd,de->bte", a, b, preferred_element_type=f32)


def mm_t(a, b):
    return jnp.einsum("bte,de->btd", a, b, preferred_element_type=f32)


def wgrad(a, b):
    return jnp.einsum("btd,bte->de", a, b, preferred_element_type=f32)


def split_heads(a):
    b, t, _ = a.shape
    return a.reshape(b, t, -1, HEAD)


def attend(q, k, v, allowed):
    s = jnp.einsum("bqhe,bkhe->bhqk", q, k, preferred_element_type=f32) * HEAD ** (-0.5)
    s = jnp.where(allowed, s, -1e30)
    ex = jnp.exp(s - jnp.max(s, axis=-1, keepdims=True))
    p = ex / jnp.sum(ex, axis=-1, keepdims=True)
    o = jnp.einsum("bhqk,bkhe->bqhe", p.astype(bf16), v, preferred_element_type=f32)
    return p, o.astype(bf16)


def attend_back(q, k, v, p, g):
    dp = jnp.einsum("bqhe,bkhe->bhqk", g, v, preferred_element_type=f32)
    ds = (p * (dp - jnp.sum(dp * p, axis=-1, keepdims=True)) * HEAD ** (-0.5)).astype(bf16)
    dq = jnp.einsum("bhqk,bkhe->bqhe", ds, k, preferred_element_type=f32).astype(bf16)
    dk = jnp.einsum("bhqk,bqhe->bkhe", ds, q, preferred_element_type=f32).astype(bf16)
    dv = jnp.einsum("bhqk,bqhe->bkhe", p.astype(bf16), g, preferred_element_type=f32).astype(bf16)
    return dq, dk, dv


def layer(x0, img, mask, gains, weights, cot):
    g1, g2, g3 = (g.astype(f32) for g in gains)
    w_qkv, w_so, w_cq, w_ckv, w_co, w_up, w_down = weights
    b, t, d = x0.shape
    x = x0.astype(f32)
    pos = jnp.arange(t)
    causal = (pos[:, None] >= pos[None, :])[None, None]
    allowed = (mask > 0)[:, None, None, :]
    h1, r1 = norm_stats(x)
    n1 = (h1 * g1).astype(bf16)
    qkv = mm(n1, w_qkv).astype(bf16)
    q1, k1, v1 = (split_heads(qkv[..., i * d : (i + 1) * d]) for i in range(3))
    p1, o1 = attend(q1, k1, v1, causal)
    o1 = o1.reshape(b, t, d)
    x1 = x + mm(o1, w_so)
    h2, r2 = norm_stats(x1)
    n2 = (h2 * g2).astype(bf16)
    q2 = split_heads(mm(n2, w_cq).astype(bf16))
    kv = mm(img, w_ckv).astype(bf16)
    k2, v2 = split_heads(kv[..., :d]), split_heads(kv[..., d:])
    p2, o2 = attend(q2, k2, v2, allowed)
    o2 = o2.reshape(b, t, d)
    x2 = x1 + mm(o2, w_co)
    h3, r3 = norm_stats(x2)
    n3 = (h3 * g3).astype(bf16)
    hpre = mm(n3, w_up)
    cdf = 0.5 * (1.0 + lax.erf(hpre * (0.5**0.5)))
    act = (hpre * cdf).astype(bf16)
    out = (x2 + mm(act, w_down)).astype(bf16)

    gw_down = wgrad(act, cot)
    pdf = jnp.exp(-0.5 * hpre * hpre) * (0.5 / jnp.pi) ** 0.5
    gh = (mm_t(cot, w_down) * (cdf + hpre * pdf)).astype(bf16)
    gw_up = wgrad(n3, gh)
    dx2, gg3 = norm_back(h3, r3, g3, mm_t(gh, w_up))
    gx2 = cot.astype(f32) + dx2
    gx2b = gx2.astype(bf16)
    gw_co = wgrad(o2, gx2b)
    go2 = split_heads(mm_t(gx2b, w_co).astype(bf16))
    dq2, dk2, dv2 = attend_back(q2, k2, v2, p2, go2)
    dq2 = dq2.reshape(b, t, d)
    dkv = jnp.concatenate([dk2.reshape(b, -1, d), dv2.reshape(b, -1, d)], axis=-1)
    gw_ckv = wgrad(img, dkv)
    gimg = mm_t(dkv, w_ckv).astype(bf16)
    gw_cq = wgrad(n2, dq2)
    dx1, gg2 = norm_back(h2, r2, g2, mm_t(dq2, w_cq))
    gx1 = gx2 + dx1
    gx1b = gx1.astype(bf16)
    gw_so = wgrad(o1, gx1b)
    go1 = split_heads(mm_t(gx1b, w_so).astype(bf16))
    dq1, dk1, dv1 = attend_back(q1, k1, v1, p1, go1)
    dqkv = jnp.concatenate([a.reshape(b, t, d) for a in (dq1, dk1, dv1)], axis=-1)
    gw_qkv = wgrad(n1, dqkv)
    dx0, gg1 = norm_back(h1, r1, g1, mm_t(dqkv, w_qkv))
    gx0 = gx1 + dx0
    return out, gx0, gimg, (gg1, gg2, gg3), (gw_qkv, gw_so, gw_cq, gw_ckv, gw_co, gw_up, gw_down)


def native(captions, img, mask, gains, weights, cotangent):
    full = [lax.all_gather(w, BOTH, axis=0, tiled=True) for w in weights]
    gains = lax.all_gather(gains, BOTH, axis=0, tiled=True)
    gains = tuple(gains[:, i] for i in range(3))
    out, gx0, gimg, gg, gw = layer(captions, img, mask, gains, full, cotangent)
    gg = lax.psum_scatter(jnp.stack(gg, axis=1), BOTH, scatter_dimension=0, tiled=True)
    shards = [
        lax.psum_scatter(g.astype(bf16), BOTH, scatter_dimension=0, tiled=True).astype(f32)
        for g in gw
    ]
    gimg = lax.all_to_all(gimg, "seq", split_axis=2, concat_axis=0, tiled=True)
    return (out, gx0, gimg.astype(f32), gg[:, 0], gg[:, 1], gg[:, 2], *shards)


def on_device(captions, images, tissue_mask, gain_self, gain_cross, gain_mlp, *rest):
    weights, cotangent = rest[:-1], rest[-1]
    n_dp, n_seq = lax.axis_size("dp"), lax.axis_size("seq")
    b, t, d = captions.shape
    patches = images.shape[1]
    if n_seq != 4 or n_dp % 4 or any(w.shape[0] % 8 for w in weights):
        start = lax.axis_index("seq") * b
        img = lax.dynamic_slice_in_dim(images, start, b, 0)
        mask = lax.dynamic_slice_in_dim(tissue_mask, start, b, 0)
        gains = jnp.stack([gain_self, gain_cross, gain_mlp], axis=1)
        return native(captions, img, mask, gains, weights, cotangent)
    nz = n_dp // 2
    gains = (gain_self, gain_cross, gain_mlp)
    out, res, fulls = forward(nz, captions, images, tissue_mask, gains, weights)
    gx, gimg, *gw, gg = backward(nz, cotangent, patches, captions, weights, res, fulls[1:])
    gimg = gimg.reshape(4 * b, *gimg.shape[2:])
    out, gx, *gw, gimg, gs, gc, gm = finish([out, gx, *gw], gimg, gg, patches)
    out, gx = out.reshape(b, t, d), gx.reshape(b, t, d)
    return (out, gx, gimg.swapaxes(1, 2), gs, gc, gm, *gw)


def solution(mesh):
    tok = P(BOTH, None, None)
    vec = P(BOTH)
    mat = P(BOTH, None)
    return jax.shard_map(
        on_device,
        mesh=mesh,
        in_specs=(tok, P("dp", None, None), P("dp", None), vec, vec, vec, *([mat] * 7), tok),
        out_specs=(tok, tok, P("dp", None, "seq"), vec, vec, vec, *([mat] * 7)),
        check_vma=False,
    )
```
